256 devices in a mesh: tile: 32 (over z_lo, y, core), depth: 8 (over z_hi, x).
Axes of the slice: x: 4, y: 4, z: 8 (z_hi: 2, z_lo: 4; z = z_hi * 4 + z_lo), core: 2. Of those that a mesh axis runs over, the one named last changes fastest.
Arguments:
- objects: float32 [8, 4, 4096, 256], P('depth', None, 'tile'), may hold values from 0.25 to 30, as said below
- observed: float32 [8, 4, 4096, 256], P('depth', None, 'tile'), may hold values from 0.25 to 30, as said below
- pupil_phase: float32 [8, 128, 128], P('depth'), may hold values from -319 to 319
- pupil_amplitude: float32 [8, 128, 128], P('depth'), may hold values from 0.25 to 1.75
Outputs:
- new_objects: float32 [8, 4, 4096, 256], P('depth', None, 'tile')
- new_phase: float32 [8, 128, 128], P('depth')
The draws below stay inside these ranges and needn't reach their ends.
Inputs may be any that keep to these rules, and one draw needn't show every extreme that they name: `objects`: strictly positive intensities. `observed`: strictly positive intensities.
All inputs are finite; a program needn't handle non-finite values.
Results may differ from the reference program's by a relative error of at most 0.0001.
Values sent between devices are 32-bit elements; how exact they have to be, the bound alone decides.
A program may use at most 64 MiB of HBM per device.

```python
import math
import jax
import jax.numpy as jnp
from jax import lax

COLS = 256
PLANES = 4
HALF = 64
PUP = 128
KER = 129
NROWS = 4096
STRATA = 8


def spread_box(field, width):
    reach = width // 2
    rows_summed = field
    for offset in range(1, reach + 1):
        rows_summed = rows_summed + jnp.roll(field, offset, 2) + jnp.roll(field, -offset, 2)
    both_summed = rows_summed
    for offset in range(1, reach + 1):
        both_summed = both_summed + jnp.roll(rows_summed, offset, 3) + jnp.roll(rows_summed, -offset, 3)
    return both_summed


def bright_cells(key):
    full_shape = (STRATA, PLANES, NROWS, COLS)
    place_key, level_key = jax.random.split(jax.random.fold_in(key, 11))
    placed = jax.random.uniform(place_key, full_shape, jnp.float32, 0.0, 1.0) < 0.01
    levels = jnp.exp(jax.random.uniform(level_key, full_shape, jnp.float32, math.log(3.0), math.log(12.0)))
    return jnp.where(placed, levels, 0.0)


def draw_background(key, salt_value):
    base_key = jax.random.fold_in(jax.random.fold_in(key, salt_value), 0)
    full_shape = (STRATA, PLANES, NROWS, COLS)
    position = jnp.arange(NROWS, dtype=jnp.float32) / max(NROWS - 1, 1)
    depth_fraction = jnp.arange(STRATA, dtype=jnp.float32) / max(STRATA - 1, 1)
    depth_ramp = (1.0 + 2.0 * depth_fraction)[:, None, None, None]
    base_level = jnp.exp(jax.random.uniform(base_key, full_shape, jnp.float32, math.log(0.5), math.log(2.0)))
    row_ramp = (1.0 + 2.0 * position)[None, None, :, None]
    return base_level * row_ramp * depth_ramp


def draw_objects(key, part):
    cells = spread_box(bright_cells(key), 3)
    return jnp.minimum(draw_background(key, 3) + cells, 30.0)


def draw_observed(key, part):
    cells = spread_box(bright_cells(key), 5)
    return jnp.minimum(draw_background(key, 7) + 0.5 * cells, 30.0)


def draw_pupil_phase(key, part):
    keys = jax.random.split(jax.random.fold_in(key, 5), 5)
    positions = (jnp.arange(PUP, dtype=jnp.float32) - (PUP - 1) / 2.0) / (PUP / 2.0)
    across = positions[None, :, None]
    along = positions[None, None, :]
    tilt_most = 0.5 * math.pi * HALF * PUP / KER
    focus_most = math.pi * HALF * PUP / (8.0 * KER)
    coeff_shape = (STRATA, 1, 1)
    tilts = tilt_most * jax.random.uniform(keys[0], (2, STRATA, 1, 1), jnp.float32, -1.0, 1.0)
    rough = jnp.clip(0.3 * jax.random.normal(keys[4], (STRATA, PUP, PUP), jnp.float32), -1.2, 1.2)
    focus = focus_most * jax.random.uniform(keys[2], coeff_shape, jnp.float32, -1.0, 1.0) ** 3
    astig = 0.5 * focus_most * jax.random.uniform(keys[3], coeff_shape, jnp.float32, -1.0, 1.0) ** 3
    smooth = tilts[0] * across + tilts[1] * along
    smooth = smooth + focus * (across ** 2 + along ** 2) + astig * (across ** 2 - along ** 2)
    return smooth + rough


def setup_inputs(seed: int = 0) -> dict:
    streams_of = jax.random.split(jax.random.key(seed), 5)
    return {
        "objects": draw_objects(jax.random.fold_in(streams_of[4], 71), 0),
        "observed": draw_observed(jax.random.fold_in(streams_of[4], 71), 0),
        "pupil_phase": draw_pupil_phase(jax.random.fold_in(streams_of[4], 71), 0),
        "pupil_amplitude": jnp.clip(1.0 + 0.15 * jax.random.normal(streams_of[3], (STRATA, PUP, PUP), jnp.float32), 0.25, 1.75),
    }


HIGHEST_PRECISION = lax.Precision.HIGHEST
BACKGROUND = 0.1
STEP_SIZE = 0.3
EPSILON = 1e-06

def twiddle(out_index, in_index, length, flip_sign):
    product = out_index[:, None] * in_index[None, :] % length
    radians = product.astype(jnp.float32) * (2.0 * math.pi / length)
    return (jnp.cos(radians), flip_sign * jnp.sin(radians))

def matmul(left, right):
    return jnp.dot(left, right, precision=HIGHEST_PRECISION)

def point_spread(pupil_angle, amplitude_map):
    pupil_size = pupil_angle.shape[0]
    kernel_size = 2 * HALF + 1
    positions = jnp.arange(pupil_size, dtype=jnp.int32)
    centre = (pupil_size - 1) / 2.0
    offsets = positions.astype(jnp.float32) - centre
    distance = offsets[:, None] ** 2 + offsets[None, :] ** 2
    aperture = (distance <= (pupil_size / 2.0) ** 2).astype(jnp.float32)
    field_real = amplitude_map * aperture * jnp.cos(pupil_angle)
    field_imag = amplitude_map * aperture * jnp.sin(pupil_angle)
    lags = (jnp.arange(kernel_size, dtype=jnp.int32) - HALF) % kernel_size
    fourier_real, fourier_imag = twiddle(lags, positions, kernel_size, -1.0)
    left_real = matmul(fourier_real, field_real) - matmul(fourier_imag, field_imag)
    left_imag = matmul(fourier_real, field_imag) + matmul(fourier_imag, field_real)
    outer_real = matmul(left_real, fourier_real.T) - matmul(left_imag, fourier_imag.T)
    outer_imag = matmul(left_real, fourier_imag.T) + matmul(left_imag, fourier_real.T)
    intensity = outer_real ** 2 + outer_imag ** 2
    return intensity / jnp.sum(intensity)

def full_kernel(kernel):
    padded = jnp.zeros((NROWS, COLS), kernel.dtype).at[:KER, :KER].set(kernel)
    return jnp.fft.fft2(jnp.roll(padded, (-HALF, -HALF), (0, 1)))

def reference(objects, observed, pupil_phase, pupil_amplitude):
    gradients = []
    for stratum in range(STRATA):
        picture = objects[stratum]
        measured = observed[stratum]
        amplitude_map = pupil_amplitude[stratum]
        first_kernel, pullback = jax.vjp(lambda trial: point_spread(trial, amplitude_map), pupil_phase[stratum])
        object_spectrum = jnp.fft.fft2(picture)
        first_blur = jnp.real(jnp.fft.ifft2(object_spectrum * full_kernel(first_kernel))) + BACKGROUND
        misfit = 1.0 - measured / first_blur
        lagged = lax.optimization_barrier(jnp.sum(jnp.real(jnp.fft.ifft2(jnp.fft.fft2(misfit) * jnp.conj(object_spectrum))), axis=0))
        psf_grad = jnp.roll(lagged, (HALF, HALF), (0, 1))[:KER, :KER]
        gradients.append(pullback(psf_grad)[0])
    grand_total = jnp.float32(0.0)
    for stratum in range(STRATA):
        grand_total = grand_total + jnp.sum(gradients[stratum] * gradients[stratum])
    mean_square = grand_total / (STRATA * PUP * PUP)
    new_objects = []
    new_phases = []
    for stratum in range(STRATA):
        picture = objects[stratum]
        measured = observed[stratum]
        updated = pupil_phase[stratum] - STEP_SIZE * gradients[stratum] / jnp.sqrt(mean_square + EPSILON)
        second_kernel = point_spread(updated, pupil_amplitude[stratum])
        kernel_spec = full_kernel(second_kernel)
        second_blur = jnp.real(jnp.fft.ifft2(jnp.fft.fft2(picture) * kernel_spec)) + BACKGROUND
        ratio_field = measured / second_blur
        correction = jnp.real(jnp.fft.ifft2(jnp.fft.fft2(ratio_field) * jnp.conj(kernel_spec)))
        new_objects.append(picture * correction)
        new_phases.append(updated)
    return (jnp.stack(new_objects), jnp.stack(new_phases))
```

```python
import math

import jax
import jax.numpy as jnp
from jax import lax
from jax.experimental import pallas as pl
from jax.experimental.pallas import tpu as pltpu
from jax.sharding import PartitionSpec as P

HALF = 64


HIGHEST_PRECISION = lax.Precision.HIGHEST
BACKGROUND = 0.1
STEP_SIZE = 0.3
EPSILON = 1e-06


def extended(value, sides, width):
    for axis, dim in sides:
        count, length = (lax.axis_size(axis), value.shape[dim])
        up = [(i, (i + 1) % count) for i in range(count)]
        down = [(j, i) for i, j in up]
        last = lax.slice_in_dim(value, length - width, length, axis=dim)
        first = lax.slice_in_dim(value, 0, width, axis=dim)
        before = lax.ppermute(last, axis, up)
        after = lax.ppermute(first, axis, down)
        value = jnp.concatenate([before, value, after], axis=dim)
    return value


def twiddle(out_index, in_index, length, flip_sign):
    product = out_index[:, None] * in_index[None, :] % length
    radians = product.astype(jnp.float32) * (2.0 * math.pi / length)
    return (jnp.cos(radians), flip_sign * jnp.sin(radians))


def matmul(left, right):
    return jnp.dot(left, right, precision=HIGHEST_PRECISION)


def point_spread(pupil_angle, amplitude_map):
    pupil_size = pupil_angle.shape[0]
    kernel_size = 2 * HALF + 1
    positions = jnp.arange(pupil_size, dtype=jnp.int32)
    centre = (pupil_size - 1) / 2.0
    offsets = positions.astype(jnp.float32) - centre
    distance = offsets[:, None] ** 2 + offsets[None, :] ** 2
    aperture = (distance <= (pupil_size / 2.0) ** 2).astype(jnp.float32)
    field_real = amplitude_map * aperture * jnp.cos(pupil_angle)
    field_imag = amplitude_map * aperture * jnp.sin(pupil_angle)
    lags = (jnp.arange(kernel_size, dtype=jnp.int32) - HALF) % kernel_size
    fourier_real, fourier_imag = twiddle(lags, positions, kernel_size, -1.0)
    left_real = matmul(fourier_real, field_real) - matmul(fourier_imag, field_imag)
    left_imag = matmul(fourier_real, field_imag) + matmul(fourier_imag, field_real)
    outer_real = matmul(left_real, fourier_real.T) - matmul(left_imag, fourier_imag.T)
    outer_imag = matmul(left_real, fourier_imag.T) + matmul(left_imag, fourier_real.T)
    intensity = outer_real**2 + outer_imag**2
    return intensity / jnp.sum(intensity)


def along_rows(twiddles, real_part, imag_part):
    cosine_part, sine_part = twiddles

    def multiply(matrix, values):
        return jnp.einsum("kl,plw->pkw", matrix, values, precision=HIGHEST_PRECISION)

    if imag_part is None:
        return (multiply(cosine_part, real_part), multiply(sine_part, real_part))
    return (
        multiply(cosine_part, real_part) - multiply(sine_part, imag_part),
        multiply(cosine_part, imag_part) + multiply(sine_part, real_part),
    )


def along_cols(twiddles, real_part, imag_part):
    cosine_part, sine_part = twiddles

    def multiply(values, matrix):
        return jnp.einsum("plw,kw->plk", values, matrix, precision=HIGHEST_PRECISION)

    return (
        multiply(real_part, cosine_part) - multiply(imag_part, sine_part),
        multiply(imag_part, cosine_part) + multiply(real_part, sine_part),
    )


def forward(values, first_row, length):
    row_count = values.shape[1]
    col_count = values.shape[2]
    row_twiddles = twiddle(
        jnp.arange(length, dtype=jnp.int32),
        jnp.arange(row_count, dtype=jnp.int32) + first_row,
        length,
        -1.0,
    )
    col_positions = jnp.arange(col_count, dtype=jnp.int32)
    col_twiddles = twiddle(col_positions, col_positions, col_count, -1.0)
    halves = along_rows(row_twiddles, values, None)
    return along_cols(col_twiddles, halves[0], halves[1])


def inverse_real(spectrum, first_row, row_count, length):
    col_count = spectrum[0].shape[2]
    cosine_part, sine_part = twiddle(
        jnp.arange(row_count, dtype=jnp.int32) + first_row,
        jnp.arange(length, dtype=jnp.int32),
        length,
        1.0,
    )
    part_real, part_imag = along_rows(
        (cosine_part / length, sine_part / length), spectrum[0], spectrum[1]
    )
    col_positions = jnp.arange(col_count, dtype=jnp.int32)
    col_cos, col_sin = twiddle(col_positions, col_positions, col_count, 1.0)
    first_term = jnp.einsum("plw,kw->plk", part_real, col_cos, precision=HIGHEST_PRECISION)
    second_term = jnp.einsum("plw,kw->plk", part_imag, col_sin, precision=HIGHEST_PRECISION)
    return (first_term - second_term) / col_count


def kernel_spectrum(kernel, length, col_count):
    lags = jnp.arange(kernel.shape[0], dtype=jnp.int32) - HALF
    row_cos, row_sin = twiddle(jnp.arange(length, dtype=jnp.int32), lags % length, length, -1.0)
    col_cos, col_sin = twiddle(
        jnp.arange(col_count, dtype=jnp.int32), lags % col_count, col_count, -1.0
    )
    left_real = matmul(row_cos, kernel)
    left_imag = matmul(row_sin, kernel)
    return (
        matmul(left_real, col_cos.T) - matmul(left_imag, col_sin.T),
        matmul(left_real, col_sin.T) + matmul(left_imag, col_cos.T),
    )


def spectral_product(spectrum, kernel_pair, conjugate):
    spec_real, spec_imag = spectrum
    kern_real, kern_imag = kernel_pair
    if conjugate:
        return (
            spec_real * kern_real + spec_imag * kern_imag,
            spec_imag * kern_real - spec_real * kern_imag,
        )
    return (
        spec_real * kern_real - spec_imag * kern_imag,
        spec_real * kern_imag + spec_imag * kern_real,
    )


def lag_gradient(misfit_spectrum, object_spectrum, length):
    misfit_real, misfit_imag = misfit_spectrum
    object_real, object_imag = object_spectrum
    cross_real = jnp.sum(misfit_real * object_real + misfit_imag * object_imag, axis=0)
    cross_imag = jnp.sum(misfit_imag * object_real - misfit_real * object_imag, axis=0)
    col_count = cross_real.shape[1]
    lags = jnp.arange(2 * HALF + 1, dtype=jnp.int32) - HALF
    row_cos, row_sin = twiddle(lags % length, jnp.arange(length, dtype=jnp.int32), length, 1.0)
    part_real = (matmul(row_cos, cross_real) - matmul(row_sin, cross_imag)) / length
    part_imag = (matmul(row_cos, cross_imag) + matmul(row_sin, cross_real)) / length
    col_cos, col_sin = twiddle(
        lags % col_count, jnp.arange(col_count, dtype=jnp.int32), col_count, 1.0
    )
    return (matmul(part_real, col_cos.T) - matmul(part_imag, col_sin.T)) / col_count


TILES = 32
DEPTHS = 8


def reduce_kernel(share_ref, total_ref, square_ref, part, mine, full, sums, s1, r1, s2, r2, s3, r3):
    me = lax.axis_index("tile")
    layer = lax.axis_index("depth")
    barrier = pltpu.get_barrier_semaphore()
    for off in range(1, TILES):
        pl.semaphore_signal(
            barrier, 1, device_id={"tile": lax.rem(me + off, TILES)}, device_id_type=pl.DeviceIdType.MESH
        )
    for off in range(1, DEPTHS):
        pl.semaphore_signal(
            barrier, 1, device_id={"depth": lax.rem(layer + off, DEPTHS)}, device_id_type=pl.DeviceIdType.MESH
        )
    pl.semaphore_wait(barrier, TILES + DEPTHS - 2)

    def scatter(off):
        peer = lax.rem(me + off, TILES)
        return pltpu.make_async_remote_copy(
            share_ref.at[peer], part.at[off - 1], s1.at[off - 1], r1.at[off - 1],
            device_id={"tile": peer}, device_id_type=pl.DeviceIdType.MESH,
        )

    def gather(off):
        peer = lax.rem(me + off, TILES)
        return pltpu.make_async_remote_copy(
            mine, full.at[off - 1], s2.at[off - 1], r2.at[off - 1],
            device_id={"tile": peer}, device_id_type=pl.DeviceIdType.MESH,
        )

    for off in range(1, TILES):
        scatter(off).start()
    for off in range(1, TILES):
        scatter(off).wait()
    total = share_ref[me]
    for off in range(1, TILES):
        total = total + part[off - 1]
    mine[...] = total
    for off in range(1, TILES):
        gather(off).start()
    for off in range(1, TILES):
        gather(off).wait()
    total_ref[me] = total
    for off in range(1, TILES):
        total_ref[lax.rem(me + TILES - off, TILES)] = full[off - 1]
    whole = total_ref[...]
    square = jnp.sum(whole * whole, axis=0)
    sums[0] = jnp.broadcast_to(jnp.sum(square), (8, 128))

    def spread(off):
        return pltpu.make_async_remote_copy(
            sums.at[0], sums.at[off], s3.at[off - 1], r3.at[off - 1],
            device_id={"depth": lax.rem(layer + off, DEPTHS)}, device_id_type=pl.DeviceIdType.MESH,
        )

    for off in range(1, DEPTHS):
        spread(off).start()
    for off in range(1, DEPTHS):
        spread(off).wait()
    squares = sums[lax.rem(layer, DEPTHS)]
    for other in range(1, DEPTHS):
        squares = squares + sums[lax.rem(layer + DEPTHS - other, DEPTHS)]
    square_ref[...] = squares


def reduce_gradient(share):
    dma = pltpu.SemaphoreType.DMA
    total, square = pl.pallas_call(
        reduce_kernel,
        out_shape=(
            jax.ShapeDtypeStruct((TILES, 4, 128), jnp.float32),
            jax.ShapeDtypeStruct((8, 128), jnp.float32),
        ),
        in_specs=[pl.BlockSpec(memory_space=pltpu.VMEM)],
        out_specs=(pl.BlockSpec(memory_space=pltpu.VMEM), pl.BlockSpec(memory_space=pltpu.VMEM)),
        scratch_shapes=[
            pltpu.VMEM((TILES - 1, 4, 128), jnp.float32),
            pltpu.VMEM((4, 128), jnp.float32),
            pltpu.VMEM((TILES - 1, 4, 128), jnp.float32),
            pltpu.VMEM((DEPTHS, 8, 128), jnp.float32),
            dma((TILES - 1,)), dma((TILES - 1,)), dma((TILES - 1,)), dma((TILES - 1,)),
            dma((DEPTHS - 1,)), dma((DEPTHS - 1,)),
        ],
        compiler_params=pltpu.CompilerParams(collective_id=0, has_side_effects=True),
    )(share.reshape(TILES, 4, 128))
    return total.reshape(128, 128), square[0, 0]


def on_device(objects, observed, pupil_phase, pupil_amplitude):
    picture = objects[0]
    measured = observed[0]
    amplitude_map = pupil_amplitude[0]
    planes, row_count, col_count = picture.shape
    first_kernel, pullback = jax.vjp(
        lambda trial: point_spread(trial, amplitude_map), pupil_phase[0]
    )
    object_strip = extended(picture, (("tile", 1),), HALF)
    length = row_count + 2 * HALF
    centre = HALF
    object_spectrum = forward(object_strip, 0, length)
    first_spectrum = kernel_spectrum(first_kernel, length, col_count)
    first_blur = (
        inverse_real(
            spectral_product(object_spectrum, first_spectrum, False), centre, row_count, length
        )
        + BACKGROUND
    )
    misfit = 1.0 - measured / first_blur
    misfit_spectrum = forward(misfit, centre, length)
    share = pullback(lag_gradient(misfit_spectrum, object_spectrum, length))[0]
    gradient, grand_total = reduce_gradient(share)
    pupil_size = gradient.shape[0]
    mean_square = grand_total / (lax.axis_size("depth") * pupil_size * pupil_size)
    new_phase = pupil_phase[0] - STEP_SIZE * gradient / jnp.sqrt(mean_square + EPSILON)
    second_kernel = point_spread(new_phase, amplitude_map)
    short_length = row_count + 2 * HALF
    second_spectrum = kernel_spectrum(second_kernel, length, col_count)
    second_blur = (
        inverse_real(
            spectral_product(object_spectrum, second_spectrum, False), centre, row_count, length
        )
        + BACKGROUND
    )
    ratio_field = measured / second_blur
    ratio_strip = extended(ratio_field, (("tile", 1),), HALF)
    ratio_spectrum = forward(ratio_strip, 0, short_length)
    correction = inverse_real(
        spectral_product(ratio_spectrum, second_spectrum, True), HALF, row_count, short_length
    )
    return ((picture * correction)[None], new_phase[None])


def solution(mesh):
    return jax.shard_map(
        on_device,
        mesh=mesh,
        in_specs=(
            P("depth", None, "tile", None),
            P("depth", None, "tile", None),
            P("depth", None, None),
            P("depth", None, None),
        ),
        out_specs=(P("depth", None, "tile", None), P("depth", None, None)),
        check_vma=False,
    )
```

```python
import math

import jax
import jax.numpy as jnp
import numpy as np
from jax import lax
from jax.experimental import pallas as pl
from jax.experimental.pallas import tpu as pltpu
from jax.sharding import PartitionSpec as P

HALF = 64
KER = 129
PUP = 128
PAD = 136
BACKGROUND = 0.1
STEP_SIZE = 0.3
EPSILON = 1e-06
MESH = pl.DeviceIdType.MESH


def real_form(matrix):
    return np.block([[matrix.real, matrix.imag], [-matrix.imag, matrix.real]])


def tables(rows, cols):
    span = rows + 2 * HALF
    half = span // 2
    omega = 2.0 * np.pi * (2.0 * np.arange(half) + 0.5) / span
    turn = np.exp(-1j * omega[:, None] * np.arange(span)[None, :])
    row_all = np.concatenate([turn.real, turn.imag])
    row_mid = row_all[:, HALF : HALF + rows]
    lag = np.exp(-1j * omega[:, None] * (np.arange(PAD) - HALF)[None, :]) * (np.arange(PAD) < KER)
    row_lag = np.concatenate([lag.real, lag.imag])
    part = cols // 2
    where = np.arange(part)
    even = np.exp(-2j * np.pi * where[:, None] * (2 * where)[None, :] / cols)
    odd = np.exp(-2j * np.pi * where[:, None] * (2 * where + 1)[None, :] / cols)
    shift_even = np.exp(2j * np.pi * HALF * 2 * where / cols)
    shift_odd = np.exp(2j * np.pi * HALF * (2 * where + 1) / cols)
    col = [real_form(even), real_form(odd)]
    col_lag = [real_form(even * shift_even), real_form(odd * shift_odd)]
    outs = np.arange(PAD)
    ring = np.exp(-2j * np.pi * (((outs - HALF)[:, None] * np.arange(PUP)[None, :]) % KER) / KER)
    ring = ring * (outs < KER)[:, None]
    left = np.block([[ring.real, -ring.imag], [ring.imag, ring.real]])
    wide = np.zeros((PUP, cols), complex)
    wide[:, :PAD] = ring.T
    right = real_form(wide)
    grid = np.arange(PUP) - (PUP - 1) / 2.0
    aperture = (grid[:, None] ** 2 + grid[None, :] ** 2 <= (PUP / 2.0) ** 2).astype(float)
    named = dict(
        row_all=row_all,
        row_mid=row_mid,
        row_back=row_mid.T * (2.0 / span),
        row_lag=row_lag,
        row_lag_back=row_lag.T * (2.0 / span),
        even=col[0],
        odd=col[1],
        even_back=col[0].T / cols,
        odd_back=col[1].T / cols,
        even_lag=col_lag[0],
        odd_lag=col_lag[1],
        even_lag_back=col_lag[0].T / cols,
        odd_lag_back=col_lag[1].T / cols,
        left=left,
        left_back=left.T,
        right=right,
        right_back=right.T,
        aperture=aperture,
    )
    return {name: np.ascontiguousarray(value, dtype=np.float32) for name, value in named.items()}


def fine(left, right):
    return jnp.dot(left, right, precision=lax.Precision.HIGHEST, preferred_element_type=jnp.float32)


def mm(left, right):
    return jnp.dot(left, right, precision=lax.Precision.HIGH, preferred_element_type=jnp.float32)


def sin_cos(angle):
    count = jnp.floor(angle * (2.0 / math.pi) + 0.5)
    rest = angle - count * 1.5703125
    rest = rest - count * 4.8375129699707031e-4
    rest = rest - count * 7.549789954891882e-8
    square = rest * rest
    sine = ((-1.9515295891e-4 * square + 8.3321608736e-3) * square - 1.6666654611e-1) * square * rest + rest
    cosine = (
        (2.443315711809948e-5 * square - 1.388731625493765e-3) * square + 4.166664568298827e-2
    ) * square * square - 0.5 * square + 1.0
    quarter = count - 4.0 * jnp.floor(count * 0.25)
    swap = (quarter == 1.0) | (quarter == 3.0)
    sin_out = jnp.where(swap, cosine, sine)
    cos_out = jnp.where(swap, sine, cosine)
    sin_out = jnp.where(quarter >= 2.0, -sin_out, sin_out)
    cos_out = jnp.where((quarter == 1.0) | (quarter == 2.0), -cos_out, cos_out)
    return sin_out, cos_out


def beside(one, two):
    return jnp.concatenate([one, two], axis=1)


def above(one, two):
    return jnp.concatenate([one, two], axis=0)


def split_cols(rowed):
    half = rowed.shape[0] // 2
    part = rowed.shape[1] // 2
    plus = rowed[:, :part] + rowed[:, part:]
    minus = rowed[:, :part] - rowed[:, part:]
    return beside(plus[:half], plus[half:]), beside(minus[:half], minus[half:])


def join_cols(even, odd):
    part = even.shape[1] // 2
    plus = even + odd
    minus = even - odd
    return above(
        beside(plus[:, :part], minus[:, :part]),
        beside(plus[:, part:], minus[:, part:]),
    )


def times(one, two):
    part = one.shape[1] // 2
    ar, ai, br, bi = one[:, :part], one[:, part:], two[:, :part], two[:, part:]
    return beside(ar * br - ai * bi, ar * bi + ai * br)


def times_conj(one, two):
    part = one.shape[1] // 2
    ar, ai, br, bi = one[:, :part], one[:, part:], two[:, :part], two[:, part:]
    return beside(ar * br + ai * bi, ai * br - ar * bi)


NAMES = (
    "row_all",
    "row_mid",
    "row_back",
    "row_lag",
    "row_lag_back",
    "even",
    "odd",
    "even_back",
    "odd_back",
    "even_lag",
    "odd_lag",
    "even_lag_back",
    "odd_lag_back",
    "left",
    "left_back",
    "right",
    "right_back",
    "aperture",
)


def kernel(tiles, depths, planes, rows, cols, *refs):
    obj, obs, phase_ref, amp_ref = refs[:4]
    t = dict(zip(NAMES, refs[4 : 4 + len(NAMES)]))
    out_obj, out_phase = refs[4 + len(NAMES) : 6 + len(NAMES)]
    (
        strip, rstrip, work_e, work_o, spec_e, spec_o, share, part, mine, full, sums,
        h1s, h1r, h2s, h2r, s1, r1, s2, r2, s3, r3,
    ) = refs[6 + len(NAMES) :]
    me = lax.axis_index("tile")
    layer = lax.axis_index("depth")
    span = rows + 2 * HALF
    half = span // 2
    barrier = pltpu.get_barrier_semaphore()
    for off in range(1, tiles):
        pl.semaphore_signal(barrier, 1, device_id={"tile": lax.rem(me + off, tiles)}, device_id_type=MESH)
    for off in range(1, depths):
        pl.semaphore_signal(barrier, 1, device_id={"depth": lax.rem(layer + off, depths)}, device_id_type=MESH)
    pl.semaphore_wait(barrier, tiles + depths - 2)

    def halo(source, source_row, buffer, sends, recvs, plane, direction):
        peer = lax.rem(me + (1 if direction == 0 else tiles - 1), tiles)
        start = source_row + (rows - HALF if direction == 0 else 0)
        target = 0 if direction == 0 else HALF + rows
        slot = 2 * plane + direction
        return pltpu.make_async_remote_copy(
            source.at[plane, pl.ds(start, HALF)], buffer.at[plane, pl.ds(target, HALF)],
            sends.at[slot], recvs.at[slot], device_id={"tile": peer}, device_id_type=MESH,
        )

    def halo1(plane, direction):
        return halo(obj, 0, strip, h1s, h1r, plane, direction)

    def halo2(plane, direction):
        return halo(rstrip, HALF, rstrip, h2s, h2r, plane, direction)

    for plane in range(planes):
        halo1(plane, 0).start()
        halo1(plane, 1).start()

    def spread_of(angle):
        sine, cosine = sin_cos(angle)
        weight = amp_ref[...] * t["aperture"][...]
        field = above(weight * cosine, weight * sine)
        lefts = fine(t["left"][...], field)
        outer = fine(beside(lefts[:PAD], lefts[PAD:]), t["right"][...])
        real, imag = outer[:, :cols], outer[:, cols:]
        intensity = real * real + imag * imag
        total = jnp.sum(intensity)
        return field, real, imag, total, intensity * (1.0 / total)

    def spectrum_of(psf):
        even, odd = split_cols(mm(t["row_lag"][...], psf))
        return mm(even, t["even_lag"][...]), mm(odd, t["odd_lag"][...])

    def forward(plane, rowed):
        even, odd = split_cols(rowed)
        at = pl.ds(plane * half, half)
        work_e[at] = even
        work_o[at] = odd

    def back(plane, even, odd):
        at = slice(plane * half, plane * half + half)
        return mm(t["row_back"][...], join_cols(even[at], odd[at]))

    def blurred(kernel_e, kernel_o):
        for plane in range(planes):
            at = pl.ds(plane * half, half)
            work_e[at] = times(spec_e[at], kernel_e)
            work_o[at] = times(spec_o[at], kernel_o)
        return mm(work_e[...], t["even_back"][...]), mm(work_o[...], t["odd_back"][...])

    phase = phase_ref[...]
    field, real, imag, total, psf = spread_of(phase)
    kernel_e, kernel_o = spectrum_of(psf)

    for plane in range(planes):
        strip[plane, pl.ds(HALF, rows)] = obj[plane]
    for plane in range(planes):
        halo1(plane, 0).wait()
        halo1(plane, 1).wait()
        forward(plane, mm(t["row_all"][...], strip[plane]))
    spec_e[...] = mm(work_e[...], t["even"][...])
    spec_o[...] = mm(work_o[...], t["odd"][...])

    even, odd = blurred(kernel_e, kernel_o)
    for plane in range(planes):
        misfit = 1.0 - obs[plane] / (back(plane, even, odd) + BACKGROUND)
        forward(plane, mm(t["row_mid"][...], misfit))
    mis_e = mm(work_e[...], t["even"][...])
    mis_o = mm(work_o[...], t["odd"][...])
    cross_e = jnp.zeros((half, cols), jnp.float32)
    cross_o = jnp.zeros((half, cols), jnp.float32)
    for plane in range(planes):
        at = slice(plane * half, plane * half + half)
        cross_e = cross_e + times_conj(mis_e[at], spec_e[at])
        cross_o = cross_o + times_conj(mis_o[at], spec_o[at])
    lagged = join_cols(fine(cross_e, t["even_lag_back"][...]), fine(cross_o, t["odd_lag_back"][...]))
    psf_grad = fine(t["row_lag_back"][...], lagged)

    scale = 2.0 / total
    centred = (psf_grad - jnp.sum(psf_grad * psf)) * scale
    lefts = fine(t["left_back"][...], above(centred * real, centred * imag))
    pupils = fine(beside(lefts[:PUP], lefts[PUP:]), t["right_back"][...])
    mygrad = field[:PUP] * pupils[:, PUP:] - field[PUP:] * pupils[:, :PUP]

    chunk = PUP // tiles
    for piece in range(tiles):
        share[piece] = mygrad[piece * chunk : (piece + 1) * chunk]

    def scatter(off):
        peer = lax.rem(me + off, tiles)
        return pltpu.make_async_remote_copy(
            share.at[peer], part.at[off - 1], s1.at[off - 1], r1.at[off - 1],
            device_id={"tile": peer}, device_id_type=MESH,
        )

    def gather(off):
        peer = lax.rem(me + off, tiles)
        return pltpu.make_async_remote_copy(
            mine, full.at[off - 1], s2.at[off - 1], r2.at[off - 1],
            device_id={"tile": peer}, device_id_type=MESH,
        )

    def spread(off):
        return pltpu.make_async_remote_copy(
            sums.at[0], sums.at[off], s3.at[off - 1], r3.at[off - 1],
            device_id={"depth": lax.rem(layer + off, depths)}, device_id_type=MESH,
        )

    for off in range(1, tiles):
        scatter(off).start()
    for off in range(1, tiles):
        scatter(off).wait()
    summed = share[me]
    for off in range(1, tiles):
        summed = summed + part[off - 1]
    mine[...] = summed
    for off in range(1, tiles):
        gather(off).start()
    for off in range(1, tiles):
        gather(off).wait()
    share[me] = summed
    for off in range(1, tiles):
        share[lax.rem(me + tiles - off, tiles)] = full[off - 1]
    gradient = jnp.concatenate([share[piece] for piece in range(tiles)], axis=0)
    sums[0] = jnp.broadcast_to(jnp.sum(gradient * gradient), (8, 128))
    for off in range(1, depths):
        spread(off).start()
    for off in range(1, depths):
        spread(off).wait()
    squares = sums[0]
    for off in range(1, depths):
        squares = squares + sums[off]
    mean_square = squares[0:1] * (1.0 / (depths * PUP * PUP))
    new_phase = phase - STEP_SIZE * gradient / jnp.sqrt(mean_square + EPSILON)
    out_phase[...] = new_phase

    _, _, _, _, psf = spread_of(new_phase)
    kernel_e, kernel_o = spectrum_of(psf)
    even, odd = blurred(kernel_e, kernel_o)
    for plane in range(planes):
        rstrip[plane, pl.ds(HALF, rows)] = obs[plane] / (back(plane, even, odd) + BACKGROUND)
        halo2(plane, 0).start()
        halo2(plane, 1).start()
    for plane in range(planes):
        halo2(plane, 0).wait()
        halo2(plane, 1).wait()
        forward(plane, mm(t["row_all"][...], rstrip[plane]))
    rat_e = mm(work_e[...], t["even"][...])
    rat_o = mm(work_o[...], t["odd"][...])
    for plane in range(planes):
        at = slice(plane * half, plane * half + half)
        work_e[pl.ds(plane * half, half)] = times_conj(rat_e[at], kernel_e)
        work_o[pl.ds(plane * half, half)] = times_conj(rat_o[at], kernel_o)
    even = mm(work_e[...], t["even_back"][...])
    odd = mm(work_o[...], t["odd_back"][...])
    for plane in range(planes):
        out_obj[plane] = obj[plane] * back(plane, even, odd)


def on_device(objects, observed, pupil_phase, pupil_amplitude):
    tiles, depths = lax.axis_size("tile"), lax.axis_size("depth")
    _, planes, rows, cols = objects.shape
    span = rows + 2 * HALF
    half = span // 2
    table = tables(rows, cols)
    f32 = jnp.float32
    vmem = pltpu.VMEM
    dma = pltpu.SemaphoreType.DMA
    chunk = PUP // tiles
    body = lambda *refs: kernel(tiles, depths, planes, rows, cols, *refs)
    new_objects, new_phase = pl.pallas_call(
        body,
        out_shape=(
            jax.ShapeDtypeStruct((planes, rows, cols), f32),
            jax.ShapeDtypeStruct((PUP, PUP), f32),
        ),
        in_specs=[pl.BlockSpec(memory_space=vmem)] * (4 + len(NAMES)),
        out_specs=(pl.BlockSpec(memory_space=vmem), pl.BlockSpec(memory_space=vmem)),
        scratch_shapes=[
            vmem((planes, span, cols), f32),
            vmem((planes, span, cols), f32),
            vmem((planes * half, cols), f32),
            vmem((planes * half, cols), f32),
            vmem((planes * half, cols), f32),
            vmem((planes * half, cols), f32),
            vmem((tiles, chunk, PUP), f32),
            vmem((tiles - 1, chunk, PUP), f32),
            vmem((chunk, PUP), f32),
            vmem((tiles - 1, chunk, PUP), f32),
            vmem((depths, 8, 128), f32),
            dma((2 * planes,)), dma((2 * planes,)), dma((2 * planes,)), dma((2 * planes,)),
            dma((tiles - 1,)), dma((tiles - 1,)), dma((tiles - 1,)), dma((tiles - 1,)),
            dma((depths - 1,)), dma((depths - 1,)),
        ],
        compiler_params=pltpu.CompilerParams(
            collective_id=0, has_side_effects=True, vmem_limit_bytes=48 * 1024 * 1024
        ),
        name="step",
    )(objects[0], observed[0], pupil_phase[0], pupil_amplitude[0], *[table[name] for name in NAMES])
    return new_objects[None], new_phase[None]


def solution(mesh):
    return jax.shard_map(
        on_device,
        mesh=mesh,
        in_specs=(
            P("depth", None, "tile", None),
            P("depth", None, "tile", None),
            P("depth", None, None),
            P("depth", None, None),
        ),
        out_specs=(P("depth", None, "tile", None), P("depth", None, None)),
        check_vma=False,
    )
```

```python
import math

import jax
import jax.numpy as jnp
import numpy as np
from jax import lax
from jax.experimental import pallas as pl
from jax.experimental.pallas import tpu as pltpu
from jax.sharding import PartitionSpec as P

HALF = 64
KER = 129
PUP = 128
PAD = 136
BACKGROUND = 0.1
STEP_SIZE = 0.3
EPSILON = 1e-06
MESH = pl.DeviceIdType.MESH


def real_form(matrix):
    return np.block([[matrix.real, matrix.imag], [-matrix.imag, matrix.real]])


def tables(rows, cols):
    span = rows + 2 * HALF
    half = span // 2
    omega = 2.0 * np.pi * (2.0 * np.arange(half) + 0.5) / span
    turn = np.exp(-1j * omega[:, None] * np.arange(span)[None, :])
    row_all = np.concatenate([turn.real, turn.imag])
    row_mid = row_all[:, HALF : HALF + rows]
    lag = np.exp(-1j * omega[:, None] * (np.arange(PAD) - HALF)[None, :]) * (np.arange(PAD) < KER)
    row_lag = np.concatenate([lag.real, lag.imag])
    part = cols // 2
    where = np.arange(part)
    even = np.exp(-2j * np.pi * where[:, None] * (2 * where)[None, :] / cols)
    odd = np.exp(-2j * np.pi * where[:, None] * (2 * where + 1)[None, :] / cols)
    shift_even = np.exp(2j * np.pi * HALF * 2 * where / cols)
    shift_odd = np.exp(2j * np.pi * HALF * (2 * where + 1) / cols)
    col = [real_form(even), real_form(odd)]
    col_lag = [real_form(even * shift_even), real_form(odd * shift_odd)]
    outs = np.arange(PAD)
    ring = np.exp(-2j * np.pi * (((outs - HALF)[:, None] * np.arange(PUP)[None, :]) % KER) / KER)
    ring = ring * (outs < KER)[:, None]
    left = np.block([[ring.real, -ring.imag], [ring.imag, ring.real]])
    wide = np.zeros((PUP, cols), complex)
    wide[:, :PAD] = ring.T
    right = real_form(wide)
    grid = np.arange(PUP) - (PUP - 1) / 2.0
    aperture = (grid[:, None] ** 2 + grid[None, :] ** 2 <= (PUP / 2.0) ** 2).astype(float)
    named = dict(
        row_all=row_all,
        row_mid=row_mid,
        row_back=row_mid.T * (2.0 / span),
        row_lag=row_lag,
        row_lag_back=row_lag.T * (2.0 / span),
        even=col[0],
        odd=col[1],
        even_back=col[0].T / cols,
        odd_back=col[1].T / cols,
        even_lag=col_lag[0],
        odd_lag=col_lag[1],
        even_lag_back=col_lag[0].T / cols,
        odd_lag_back=col_lag[1].T / cols,
        left=left,
        left_back=left.T,
        right=right,
        right_back=right.T,
        aperture=aperture,
    )
    return {name: np.ascontiguousarray(value, dtype=np.float32) for name, value in named.items()}


def fine(left, right):
    return jnp.dot(left, right, precision=lax.Precision.HIGHEST, preferred_element_type=jnp.float32)


def mm(left, right):
    return jnp.dot(left, right, precision=lax.Precision.HIGH, preferred_element_type=jnp.float32)


def sin_cos(angle):
    count = jnp.floor(angle * (2.0 / math.pi) + 0.5)
    rest = angle - count * 1.5703125
    rest = rest - count * 4.8375129699707031e-4
    rest = rest - count * 7.549789954891882e-8
    square = rest * rest
    sine = ((-1.9515295891e-4 * square + 8.3321608736e-3) * square - 1.6666654611e-1) * square * rest + rest
    cosine = (
        (2.443315711809948e-5 * square - 1.388731625493765e-3) * square + 4.166664568298827e-2
    ) * square * square - 0.5 * square + 1.0
    quarter = count - 4.0 * jnp.floor(count * 0.25)
    swap = (quarter == 1.0) | (quarter == 3.0)
    sin_out = jnp.where(swap, cosine, sine)
    cos_out = jnp.where(swap, sine, cosine)
    sin_out = jnp.where(quarter >= 2.0, -sin_out, sin_out)
    cos_out = jnp.where((quarter == 1.0) | (quarter == 2.0), -cos_out, cos_out)
    return sin_out, cos_out


def beside(one, two):
    return jnp.concatenate([one, two], axis=1)


def above(one, two):
    return jnp.concatenate([one, two], axis=0)


def split_cols(rowed):
    half = rowed.shape[0] // 2
    part = rowed.shape[1] // 2
    plus = rowed[:, :part] + rowed[:, part:]
    minus = rowed[:, :part] - rowed[:, part:]
    return beside(plus[:half], plus[half:]), beside(minus[:half], minus[half:])


def join_cols(even, odd):
    part = even.shape[1] // 2
    plus = even + odd
    minus = even - odd
    return above(
        beside(plus[:, :part], minus[:, :part]),
        beside(plus[:, part:], minus[:, part:]),
    )


def times(one, two):
    part = one.shape[1] // 2
    ar, ai, br, bi = one[:, :part], one[:, part:], two[:, :part], two[:, part:]
    return beside(ar * br - ai * bi, ar * bi + ai * br)


def times_conj(one, two):
    part = one.shape[1] // 2
    ar, ai, br, bi = one[:, :part], one[:, part:], two[:, :part], two[:, part:]
    return beside(ar * br + ai * bi, ai * br - ar * bi)


NAMES = (
    "row_all",
    "row_mid",
    "row_back",
    "row_lag",
    "row_lag_back",
    "even",
    "odd",
    "even_back",
    "odd_back",
    "even_lag",
    "odd_lag",
    "even_lag_back",
    "odd_lag_back",
    "left",
    "left_back",
    "right",
    "right_back",
    "aperture",
)


def kernel(tiles, depths, planes, rows, cols, *refs):
    count = len(NAMES)
    obj_in, obs_in, phase_in, amp_in = refs[:4]
    table_in = refs[4 : 4 + count]
    out_obj, out_phase = refs[4 + count : 6 + count]
    t = dict(zip(NAMES, refs[6 + count : 6 + 2 * count]))
    (
        obs, phase_ref, amp_ref, load_sem, strip, rstrip, work_e, work_o, spec_e, spec_o, share, part, mine, full, sums,
        h1s, h1r, h2s, h2r, s1, r1, s2, r2, s3, r3,
    ) = refs[6 + 2 * count :]
    me = lax.axis_index("tile")
    layer = lax.axis_index("depth")
    span = rows + 2 * HALF
    half = span // 2
    barrier = pltpu.get_barrier_semaphore()
    for off in range(1, tiles):
        pl.semaphore_signal(barrier, 1, device_id={"tile": lax.rem(me + off, tiles)}, device_id_type=MESH)
    for off in range(1, depths):
        pl.semaphore_signal(barrier, 1, device_id={"depth": lax.rem(layer + off, depths)}, device_id_type=MESH)

    loads = {"phase": pltpu.make_async_copy(phase_in, phase_ref, load_sem.at[0])}
    loads["amp"] = pltpu.make_async_copy(amp_in, amp_ref, load_sem.at[1])
    loads["obj"] = pltpu.make_async_copy(obj_in, strip.at[:, pl.ds(HALF, rows)], load_sem.at[2])
    loads["obs"] = pltpu.make_async_copy(obs_in, obs, load_sem.at[3])
    for index, name in enumerate(NAMES):
        loads[name] = pltpu.make_async_copy(table_in[index], t[name], load_sem.at[4 + index])
    for name in ("phase", "amp", "aperture", "left", "right", "obj"):
        loads[name].start()
    for name in loads:
        if name not in ("phase", "amp", "aperture", "left", "right", "obj"):
            loads[name].start()

    def ready(*names):
        for name in names:
            loads[name].wait()

    def halo(source, source_row, buffer, sends, recvs, plane, direction):
        peer = lax.rem(me + (1 if direction == 0 else tiles - 1), tiles)
        start = source_row + (rows - HALF if direction == 0 else 0)
        target = 0 if direction == 0 else HALF + rows
        slot = 2 * plane + direction
        return pltpu.make_async_remote_copy(
            source.at[plane, pl.ds(start, HALF)], buffer.at[plane, pl.ds(target, HALF)],
            sends.at[slot], recvs.at[slot], device_id={"tile": peer}, device_id_type=MESH,
        )

    def halo1(plane, direction):
        return halo(strip, HALF, strip, h1s, h1r, plane, direction)

    def halo2(plane, direction):
        return halo(rstrip, HALF, rstrip, h2s, h2r, plane, direction)

    def spread_of(angle):
        sine, cosine = sin_cos(angle)
        weight = amp_ref[...] * t["aperture"][...]
        field = above(weight * cosine, weight * sine)
        lefts = fine(t["left"][...], field)
        outer = fine(beside(lefts[:PAD], lefts[PAD:]), t["right"][...])
        real, imag = outer[:, :cols], outer[:, cols:]
        intensity = real * real + imag * imag
        total = jnp.sum(intensity)
        return field, real, imag, total, intensity * (1.0 / total)

    def spectrum_of(psf):
        even, odd = split_cols(mm(t["row_lag"][...], psf))
        return mm(even, t["even_lag"][...]), mm(odd, t["odd_lag"][...])

    def forward(plane, rowed):
        even, odd = split_cols(rowed)
        at = pl.ds(plane * half, half)
        work_e[at] = even
        work_o[at] = odd

    def back(plane, even, odd):
        at = slice(plane * half, plane * half + half)
        return mm(t["row_back"][...], join_cols(even[at], odd[at]))

    def blurred(kernel_e, kernel_o):
        for plane in range(planes):
            at = pl.ds(plane * half, half)
            work_e[at] = times(spec_e[at], kernel_e)
            work_o[at] = times(spec_o[at], kernel_o)
        return mm(work_e[...], t["even_back"][...]), mm(work_o[...], t["odd_back"][...])

    ready("phase", "amp", "aperture", "left", "right")
    phase = phase_ref[...]
    field, real, imag, total, psf = spread_of(phase)
    ready("obj")
    pl.semaphore_wait(barrier, tiles + depths - 2)
    for plane in range(planes):
        halo1(plane, 0).start()
        halo1(plane, 1).start()
    ready(*[name for name in loads if name not in ("phase", "amp", "aperture", "left", "right", "obj")])
    kernel_e, kernel_o = spectrum_of(psf)

    for plane in range(planes):
        halo1(plane, 0).wait()
        halo1(plane, 1).wait()
        forward(plane, mm(t["row_all"][...], strip[plane]))
    spec_e[...] = mm(work_e[...], t["even"][...])
    spec_o[...] = mm(work_o[...], t["odd"][...])

    even, odd = blurred(kernel_e, kernel_o)
    for plane in range(planes):
        misfit = 1.0 - obs[plane] / (back(plane, even, odd) + BACKGROUND)
        forward(plane, mm(t["row_mid"][...], misfit))
    mis_e = mm(work_e[...], t["even"][...])
    mis_o = mm(work_o[...], t["odd"][...])
    cross_e = jnp.zeros((half, cols), jnp.float32)
    cross_o = jnp.zeros((half, cols), jnp.float32)
    for plane in range(planes):
        at = slice(plane * half, plane * half + half)
        cross_e = cross_e + times_conj(mis_e[at], spec_e[at])
        cross_o = cross_o + times_conj(mis_o[at], spec_o[at])
    lagged = join_cols(fine(cross_e, t["even_lag_back"][...]), fine(cross_o, t["odd_lag_back"][...]))
    psf_grad = fine(t["row_lag_back"][...], lagged)

    scale = 2.0 / total
    centred = (psf_grad - jnp.sum(psf_grad * psf)) * scale
    lefts = fine(t["left_back"][...], above(centred * real, centred * imag))
    pupils = fine(beside(lefts[:PUP], lefts[PUP:]), t["right_back"][...])
    mygrad = field[:PUP] * pupils[:, PUP:] - field[PUP:] * pupils[:, :PUP]

    chunk = PUP // tiles
    for piece in range(tiles):
        share[piece] = mygrad[piece * chunk : (piece + 1) * chunk]

    def scatter(off):
        peer = lax.rem(me + off, tiles)
        return pltpu.make_async_remote_copy(
            share.at[peer], part.at[off - 1], s1.at[off - 1], r1.at[off - 1],
            device_id={"tile": peer}, device_id_type=MESH,
        )

    def gather(off):
        peer = lax.rem(me + off, tiles)
        return pltpu.make_async_remote_copy(
            mine, full.at[off - 1], s2.at[off - 1], r2.at[off - 1],
            device_id={"tile": peer}, device_id_type=MESH,
        )

    def spread(off):
        return pltpu.make_async_remote_copy(
            sums.at[0], sums.at[off], s3.at[off - 1], r3.at[off - 1],
            device_id={"depth": lax.rem(layer + off, depths)}, device_id_type=MESH,
        )

    for off in range(1, tiles):
        scatter(off).start()
    for off in range(1, tiles):
        scatter(off).wait()
    summed = share[me]
    for off in range(1, tiles):
        summed = summed + part[off - 1]
    mine[...] = summed
    for off in range(1, tiles):
        gather(off).start()
    for off in range(1, tiles):
        gather(off).wait()
    share[me] = summed
    for off in range(1, tiles):
        share[lax.rem(me + tiles - off, tiles)] = full[off - 1]
    gradient = jnp.concatenate([share[piece] for piece in range(tiles)], axis=0)
    sums[0] = jnp.broadcast_to(jnp.sum(gradient * gradient), (8, 128))
    for off in range(1, depths):
        spread(off).start()
    for off in range(1, depths):
        spread(off).wait()
    squares = sums[0]
    for off in range(1, depths):
        squares = squares + sums[off]
    mean_square = squares[0:1] * (1.0 / (depths * PUP * PUP))
    new_phase = phase - STEP_SIZE * gradient / jnp.sqrt(mean_square + EPSILON)
    out_phase[...] = new_phase

    _, _, _, _, psf = spread_of(new_phase)
    kernel_e, kernel_o = spectrum_of(psf)
    even, odd = blurred(kernel_e, kernel_o)
    for plane in range(planes):
        rstrip[plane, pl.ds(HALF, rows)] = obs[plane] / (back(plane, even, odd) + BACKGROUND)
        halo2(plane, 0).start()
        halo2(plane, 1).start()
    for plane in range(planes):
        halo2(plane, 0).wait()
        halo2(plane, 1).wait()
        forward(plane, mm(t["row_all"][...], rstrip[plane]))
    rat_e = mm(work_e[...], t["even"][...])
    rat_o = mm(work_o[...], t["odd"][...])
    for plane in range(planes):
        at = slice(plane * half, plane * half + half)
        work_e[pl.ds(plane * half, half)] = times_conj(rat_e[at], kernel_e)
        work_o[pl.ds(plane * half, half)] = times_conj(rat_o[at], kernel_o)
    even = mm(work_e[...], t["even_back"][...])
    odd = mm(work_o[...], t["odd_back"][...])
    for plane in range(planes):
        out_obj[plane] = strip[plane, pl.ds(HALF, rows)] * back(plane, even, odd)


def on_device(objects, observed, pupil_phase, pupil_amplitude):
    tiles, depths = lax.axis_size("tile"), lax.axis_size("depth")
    _, planes, rows, cols = objects.shape
    span = rows + 2 * HALF
    half = span // 2
    table = tables(rows, cols)
    f32 = jnp.float32
    vmem = pltpu.VMEM
    dma = pltpu.SemaphoreType.DMA
    chunk = PUP // tiles
    body = lambda *refs: kernel(tiles, depths, planes, rows, cols, *refs)
    new_objects, new_phase = pl.pallas_call(
        body,
        out_shape=(
            jax.ShapeDtypeStruct((planes, rows, cols), f32),
            jax.ShapeDtypeStruct((PUP, PUP), f32),
        ),
        in_specs=[pl.BlockSpec(memory_space=pltpu.HBM)] * (4 + len(NAMES)),
        out_specs=(pl.BlockSpec(memory_space=vmem), pl.BlockSpec(memory_space=vmem)),
        scratch_shapes=[vmem(table[name].shape, f32) for name in NAMES]
        + [
            vmem((planes, rows, cols), f32),
            vmem((PUP, PUP), f32),
            vmem((PUP, PUP), f32),
            dma((4 + len(NAMES),)),
            vmem((planes, span, cols), f32),
            vmem((planes, span, cols), f32),
            vmem((planes * half, cols), f32),
            vmem((planes * half, cols), f32),
            vmem((planes * half, cols), f32),
            vmem((planes * half, cols), f32),
            vmem((tiles, chunk, PUP), f32),
            vmem((tiles - 1, chunk, PUP), f32),
            vmem((chunk, PUP), f32),
            vmem((tiles - 1, chunk, PUP), f32),
            vmem((depths, 8, 128), f32),
            dma((2 * planes,)), dma((2 * planes,)), dma((2 * planes,)), dma((2 * planes,)),
            dma((tiles - 1,)), dma((tiles - 1,)), dma((tiles - 1,)), dma((tiles - 1,)),
            dma((depths - 1,)), dma((depths - 1,)),
        ],
        compiler_params=pltpu.CompilerParams(
            collective_id=0, has_side_effects=True, vmem_limit_bytes=67043328
        ),
        name="step",
    )(objects[0], observed[0], pupil_phase[0], pupil_amplitude[0], *[table[name] for name in NAMES])
    return new_objects[None], new_phase[None]


def solution(mesh):
    return jax.shard_map(
        on_device,
        mesh=mesh,
        in_specs=(
            P("depth", None, "tile", None),
            P("depth", None, "tile", None),
            P("depth", None, None),
            P("depth", None, None),
        ),
        out_specs=(P("depth", None, "tile", None), P("depth", None, None)),
        check_vma=False,
    )
```

```python
import math

import jax
import jax.numpy as jnp
import numpy as np
from jax import lax
from jax.experimental import pallas as pl
from jax.experimental.pallas import tpu as pltpu
from jax.sharding import PartitionSpec as P

HALF = 64
KER = 129
PUP = 128
PAD = 136
BACKGROUND = 0.1
STEP_SIZE = 0.3
EPSILON = 1e-06
RING = 8
SIDES = 2
MESH = pl.DeviceIdType.MESH


def real_form(matrix):
    return np.block([[matrix.real, matrix.imag], [-matrix.imag, matrix.real]])


def tables(rows, cols):
    span = rows + 2 * HALF
    half = span // 2
    omega = 2.0 * np.pi * (2.0 * np.arange(half) + 0.5) / span
    turn = np.exp(-1j * omega[:, None] * np.arange(span)[None, :])
    row_all = np.concatenate([turn.real, turn.imag])
    row_mid = row_all[:, HALF : HALF + rows]
    lag = np.exp(-1j * omega[:, None] * (np.arange(PAD) - HALF)[None, :]) * (np.arange(PAD) < KER)
    row_lag = np.concatenate([lag.real, lag.imag])
    part = cols // 2
    where = np.arange(part)
    even = np.exp(-2j * np.pi * where[:, None] * (2 * where)[None, :] / cols)
    odd = np.exp(-2j * np.pi * where[:, None] * (2 * where + 1)[None, :] / cols)
    outs = np.arange(cols)
    ring = np.exp(-2j * np.pi * (((outs - HALF)[:, None] * np.arange(PUP)[None, :]) % KER) / KER)
    ring = ring * (outs < KER)[:, None]
    left = np.concatenate([ring.real[:PAD], ring.imag[:PAD]])
    right = np.concatenate([ring.real.T, ring.imag.T])
    grid = np.arange(PUP) - (PUP - 1) / 2.0
    aperture = (grid[:, None] ** 2 + grid[None, :] ** 2 <= (PUP / 2.0) ** 2).astype(float)
    named = dict(
        row_all=row_all,
        row_mid=row_mid,
        row_back=row_mid.T * (2.0 / span / cols),
        row_lag=row_lag,
        row_lag_back=row_lag.T * (2.0 / span / cols),
        even=real_form(even),
        odd=real_form(odd),
        left=left,
        right=right,
        aperture=aperture,
    )
    return {name: np.ascontiguousarray(value, dtype=np.float32) for name, value in named.items()}


def fine(left, right):
    return jnp.dot(left, right, precision=lax.Precision.HIGHEST, preferred_element_type=jnp.float32)


def mm(left, right):
    return jnp.dot(left, right, precision=lax.Precision.HIGH, preferred_element_type=jnp.float32)


def sin_cos(angle):
    count = jnp.floor(angle * (2.0 / math.pi) + 0.5)
    rest = angle - count * 1.5703125
    rest = rest - count * 4.8375129699707031e-4
    rest = rest - count * 7.549789954891882e-8
    square = rest * rest
    sine = ((-1.9515295891e-4 * square + 8.3321608736e-3) * square - 1.6666654611e-1) * square * rest + rest
    cosine = (
        (2.443315711809948e-5 * square - 1.388731625493765e-3) * square + 4.166664568298827e-2
    ) * square * square - 0.5 * square + 1.0
    quarter = count - 4.0 * jnp.floor(count * 0.25)
    swap = (quarter == 1.0) | (quarter == 3.0)
    sin_out = jnp.where(swap, cosine, sine)
    cos_out = jnp.where(swap, sine, cosine)
    sin_out = jnp.where(quarter >= 2.0, -sin_out, sin_out)
    cos_out = jnp.where((quarter == 1.0) | (quarter == 2.0), -cos_out, cos_out)
    return sin_out, cos_out


def beside(one, two):
    return jnp.concatenate([one, two], axis=1)


def above(one, two):
    return jnp.concatenate([one, two], axis=0)


def split_cols(rowed):
    half = rowed.shape[0] // 2
    part = rowed.shape[1] // 2
    plus = rowed[:, :part] + rowed[:, part:]
    minus = rowed[:, :part] - rowed[:, part:]
    return beside(plus[:half], plus[half:]), beside(minus[:half], minus[half:])


def join_cols(even, odd):
    part = even.shape[1] // 2
    plus = even + odd
    minus = even - odd
    return above(
        beside(plus[:, :part], minus[:, :part]),
        beside(plus[:, part:], minus[:, part:]),
    )


def times(one, two):
    part = one.shape[1] // 2
    ar, ai, br, bi = one[:, :part], one[:, part:], two[:, :part], two[:, part:]
    return beside(ar * br - ai * bi, ar * bi + ai * br)


def times_conj(one, two):
    part = one.shape[1] // 2
    ar, ai, br, bi = one[:, :part], one[:, part:], two[:, :part], two[:, part:]
    return beside(ar * br + ai * bi, ai * br - ar * bi)


NAMES = ("aperture", "left", "right", "row_lag", "row_all", "even", "odd", "row_back", "row_mid", "row_lag_back")
EARLY = ("phase", "amp", "aperture", "left", "right", "obj")


def kernel(tiles, depths, planes, rows, cols, *refs):
    count = len(NAMES)
    obj_in, obs_in, phase_in, amp_in = refs[:4]
    table_in = refs[4 : 4 + count]
    out_obj, out_phase = refs[4 + count : 6 + count]
    t = dict(zip(NAMES, refs[6 + count : 6 + 2 * count]))
    (
        obs, phase_ref, amp_ref, load_sem, even_back, odd_back, strip, rstrip, spec_e, spec_o,
        share, part, mine, stack, full, square, sums,
        h1s, h1r, h2s, h2r, s1, r1, s2, r2, s3, r3, s4, r4, s5,
    ) = refs[6 + 2 * count :]
    me = lax.axis_index("tile")
    layer = lax.axis_index("depth")
    span = rows + 2 * HALF
    half = span // 2
    slabs = tiles // RING
    slab, spot = me // RING, lax.rem(me, RING)
    lanes = depths // SIDES
    side, lane = layer // lanes, lax.rem(layer, lanes)
    lowest, highest = slab == 0, slab == slabs - 1
    near = slabs // 2
    source_slab = jnp.where(slab < near, slabs - 1, 0)

    def at_tile(tile):
        return {"tile": tile, "depth": layer}

    def at_spot(off):
        return at_tile(slab * RING + lax.rem(spot + off, RING))

    def at_slab(off):
        return at_tile(lax.rem(slab + off, slabs) * RING + spot)

    def at_lane(off):
        return {"tile": me, "depth": side * lanes + lax.rem(lane + off, lanes)}

    def across(to_slab, to_lane):
        return {"tile": to_slab * RING + spot, "depth": (SIDES - 1 - side) * lanes + to_lane}

    barrier = pltpu.get_barrier_semaphore()

    def greet(device):
        pl.semaphore_signal(barrier, 1, device_id=device, device_id_type=MESH)

    greet(at_tile(lax.rem(me + 1, tiles)))
    greet(at_tile(lax.rem(me + tiles - 1, tiles)))
    for off in range(1, RING):
        greet(at_spot(off))
    for off in range(1, slabs):
        greet(at_slab(off))
    for off in range(1, lanes):
        greet(at_lane(off))
    for to_lane in range(lanes):
        greet(across(source_slab, to_lane))
    near_sends = jnp.where(lowest | highest, near * lanes, 0)
    greeted = 2 + RING - 1 + slabs - 1 + lanes - 1 + near_sends

    loads = {"phase": pltpu.make_async_copy(phase_in, phase_ref, load_sem.at[0])}
    loads["amp"] = pltpu.make_async_copy(amp_in, amp_ref, load_sem.at[1])
    loads["obj"] = pltpu.make_async_copy(obj_in, strip.at[:, pl.ds(HALF, rows)], load_sem.at[2])
    loads["obs"] = pltpu.make_async_copy(obs_in, obs, load_sem.at[3])
    for index, name in enumerate(NAMES):
        loads[name] = pltpu.make_async_copy(table_in[index], t[name], load_sem.at[4 + index])
    for name in EARLY:
        loads[name].start()
    for name in loads:
        if name not in EARLY:
            loads[name].start()

    def ready(*names):
        for name in names:
            loads[name].wait()

    def halo(buffer, sends, recvs, plane, direction):
        peer = lax.rem(me + (1 if direction == 0 else tiles - 1), tiles)
        start = rows if direction == 0 else HALF
        target = 0 if direction == 0 else HALF + rows
        slot = 2 * plane + direction
        return pltpu.make_async_remote_copy(
            buffer.at[plane, pl.ds(start, HALF)], buffer.at[plane, pl.ds(target, HALF)],
            sends.at[slot], recvs.at[slot], device_id=at_tile(peer), device_id_type=MESH,
        )

    def halo1(plane, direction):
        return halo(strip, h1s, h1r, plane, direction)

    def halo2(plane, direction):
        return halo(rstrip, h2s, h2r, plane, direction)

    def full_left():
        real, imag = t["left"][:PAD], t["left"][PAD:]
        return above(beside(real, -imag), beside(imag, real))

    def full_right():
        real, imag = t["right"][:PUP], t["right"][PUP:]
        return above(beside(real, imag), beside(-imag, real))

    def spread_of(angle):
        sine, cosine = sin_cos(angle)
        weight = amp_ref[...] * t["aperture"][...]
        field = above(weight * cosine, weight * sine)
        lefts = fine(full_left(), field)
        outer = fine(beside(lefts[:PAD], lefts[PAD:]), full_right())
        real, imag = outer[:, :cols], outer[:, cols:]
        intensity = real * real + imag * imag
        total = jnp.sum(intensity)
        return field, real, imag, total, intensity * (1.0 / total)

    part_cols = cols // 2
    column = lax.broadcasted_iota(jnp.int32, (1, part_cols), 1)
    flip = 1.0 - 2.0 * lax.rem(column, 2).astype(jnp.float32)
    flips = beside(flip, flip)
    turn_on = beside(-flip, flip)
    turn_off = beside(flip, -flip)

    def swapped(value):
        return beside(value[:, part_cols:], value[:, :part_cols])

    def spectrum_of(psf):
        even, odd = split_cols(mm(t["row_lag"][...], psf))
        return mm(even, t["even"][...]) * flips, swapped(mm(odd, t["odd"][...])) * turn_on

    def columns(rowed):
        even, odd = split_cols(rowed)
        return mm(even, t["even"][...]), mm(odd, t["odd"][...])

    def back(even, odd):
        return mm(t["row_back"][...], join_cols(mm(even, even_back[...]), mm(odd, odd_back[...])))

    def blurred(plane, kernel_e, kernel_o):
        at = pl.ds(plane * half, half)
        return back(times(spec_e[at], kernel_e), times(spec_o[at], kernel_o))

    ready("phase", "amp", "aperture", "left", "right")
    phase = phase_ref[...]
    field, real, imag, total, psf = spread_of(phase)
    ready("obj")
    pl.semaphore_wait(barrier, greeted)
    for plane in range(planes):
        halo1(plane, 0).start()
        halo1(plane, 1).start()
    ready(*[name for name in loads if name not in EARLY])
    even_back[...] = t["even"][...].T
    odd_back[...] = t["odd"][...].T
    kernel_e, kernel_o = spectrum_of(psf)

    cross_e = jnp.zeros((half, cols), jnp.float32)
    cross_o = jnp.zeros((half, cols), jnp.float32)
    for plane in range(planes):
        halo1(plane, 0).wait()
        halo1(plane, 1).wait()
        even, odd = columns(mm(t["row_all"][...], strip[plane]))
        at = pl.ds(plane * half, half)
        spec_e[at] = even
        spec_o[at] = odd
        misfit = 1.0 - obs[plane] / (blurred(plane, kernel_e, kernel_o) + BACKGROUND)
        mis_e, mis_o = columns(mm(t["row_mid"][...], misfit))
        cross_e = cross_e + times_conj(mis_e, spec_e[at])
        cross_o = cross_o + times_conj(mis_o, spec_o[at])
    lagged = join_cols(fine(cross_e * flips, even_back[...]), fine(swapped(cross_o) * turn_off, odd_back[...]))
    psf_grad = fine(t["row_lag_back"][...], lagged)

    scale = 2.0 / total
    centred = (psf_grad - jnp.sum(psf_grad * psf)) * scale
    rest = jnp.zeros((cols - PAD, cols), jnp.float32)
    right = full_right()
    lefts = fine(right, jnp.concatenate([centred * real, rest, centred * imag, rest], axis=0))
    pupils = lax.dot_general(
        beside(lefts[:PUP], lefts[PUP:]), right, (((1,), (1,)), ((), ())),
        precision=lax.Precision.HIGHEST, preferred_element_type=jnp.float32,
    )
    mygrad = field[:PUP] * pupils[:, PUP:] - field[PUP:] * pupils[:, :PUP]

    chunk = PUP // RING
    for piece in range(RING):
        share[piece] = mygrad[piece * chunk : (piece + 1) * chunk]

    def scatter(off):
        return pltpu.make_async_remote_copy(
            share.at[lax.rem(spot + off, RING)], part.at[off - 1], s1.at[off - 1], r1.at[off - 1],
            device_id=at_spot(off), device_id_type=MESH,
        )

    def exchange(off):
        return pltpu.make_async_remote_copy(
            mine, stack.at[slab], s2.at[off - 1], r2.at[off - 1],
            device_id=at_slab(off), device_id_type=MESH,
        )

    def gather(off):
        return pltpu.make_async_remote_copy(
            full.at[spot], full.at[spot], s3.at[off - 1], r3.at[off - 1],
            device_id=at_spot(off), device_id_type=MESH,
        )

    def lane_sum(off):
        return pltpu.make_async_remote_copy(
            square, sums.at[layer], s4.at[off - 1], r4.at[layer],
            device_id=at_lane(off), device_id_type=MESH,
        )

    def far_sum(step, to_lane):
        return pltpu.make_async_remote_copy(
            square, sums.at[layer], s5.at[step * lanes + to_lane], r4.at[layer],
            device_id=across(jnp.where(lowest, near, 0) + step, to_lane), device_id_type=MESH,
        )

    for off in range(1, RING):
        scatter(off).start()
    for off in range(1, RING):
        scatter(off).wait()
    summed = share[spot]
    for off in range(1, RING):
        summed = summed + part[off - 1]
    mine[...] = summed
    for off in range(1, slabs):
        exchange(off).start()
    stack[slab] = summed
    for off in range(1, slabs):
        exchange(off).wait()
    summed = stack[0]
    for other in range(1, slabs):
        summed = summed + stack[other]
    full[spot] = summed
    for off in range(1, RING):
        gather(off).start()
    for off in range(1, RING):
        gather(off).wait()
    gradient = jnp.concatenate([full[piece] for piece in range(RING)], axis=0)
    square[...] = jnp.broadcast_to(jnp.sum(gradient * gradient), (8, 128))
    for off in range(1, lanes):
        lane_sum(off).start()

    @pl.when(lowest | highest)
    def _():
        for step in range(near):
            for to_lane in range(lanes):
                far_sum(step, to_lane).start()

    sums[layer] = square[...]
    for off in range(1, depths):
        other = lax.rem(layer + off, depths)
        pltpu.make_async_remote_copy(
            sums.at[other], sums.at[other], s4.at[0], r4.at[other], device_id=at_lane(1), device_id_type=MESH
        ).wait_recv()
    for off in range(1, lanes):
        lane_sum(off).wait_send()

    @pl.when(lowest | highest)
    def _():
        for step in range(near):
            for to_lane in range(lanes):
                far_sum(step, to_lane).wait_send()

    squares = sums[0]
    for other in range(1, depths):
        squares = squares + sums[other]
    mean_square = squares[0:1] * (1.0 / (depths * PUP * PUP))
    new_phase = phase - STEP_SIZE * gradient / jnp.sqrt(mean_square + EPSILON)
    out_phase[...] = new_phase

    _, _, _, _, psf = spread_of(new_phase)
    kernel_e, kernel_o = spectrum_of(psf)
    for plane in range(planes):
        rstrip[plane, pl.ds(HALF, rows)] = obs[plane] / (blurred(plane, kernel_e, kernel_o) + BACKGROUND)
        halo2(plane, 0).start()
        halo2(plane, 1).start()
    for plane in range(planes):
        halo2(plane, 0).wait()
        halo2(plane, 1).wait()
        even, odd = columns(mm(t["row_all"][...], rstrip[plane]))
        correction = back(times_conj(even, kernel_e), times_conj(odd, kernel_o))
        out_obj[plane] = strip[plane, pl.ds(HALF, rows)] * correction


def on_device(objects, observed, pupil_phase, pupil_amplitude):
    tiles, depths = lax.axis_size("tile"), lax.axis_size("depth")
    _, planes, rows, cols = objects.shape
    span = rows + 2 * HALF
    half = span // 2
    table = tables(rows, cols)
    f32 = jnp.float32
    vmem = pltpu.VMEM
    dma = pltpu.SemaphoreType.DMA
    chunk = PUP // RING
    slabs = tiles // RING
    lanes = depths // SIDES
    body = lambda *refs: kernel(tiles, depths, planes, rows, cols, *refs)
    new_objects, new_phase = pl.pallas_call(
        body,
        out_shape=(
            jax.ShapeDtypeStruct((planes, rows, cols), f32),
            jax.ShapeDtypeStruct((PUP, PUP), f32),
        ),
        in_specs=[pl.BlockSpec(memory_space=pltpu.HBM)] * (4 + len(NAMES)),
        out_specs=(pl.BlockSpec(memory_space=vmem), pl.BlockSpec(memory_space=vmem)),
        scratch_shapes=[vmem(table[name].shape, f32) for name in NAMES]
        + [
            vmem((planes, rows, cols), f32),
            vmem((PUP, PUP), f32),
            vmem((PUP, PUP), f32),
            dma((4 + len(NAMES),)),
            vmem((cols, cols), f32),
            vmem((cols, cols), f32),
            vmem((planes, span, cols), f32),
            vmem((planes, span, cols), f32),
            vmem((planes * half, cols), f32),
            vmem((planes * half, cols), f32),
            vmem((RING, chunk, PUP), f32),
            vmem((RING - 1, chunk, PUP), f32),
            vmem((chunk, PUP), f32),
            vmem((slabs, chunk, PUP), f32),
            vmem((RING, chunk, PUP), f32),
            vmem((8, 128), f32),
            vmem((depths, 8, 128), f32),
            dma((2 * planes,)), dma((2 * planes,)), dma((2 * planes,)), dma((2 * planes,)),
            dma((RING - 1,)), dma((RING - 1,)), dma((slabs - 1,)), dma((slabs - 1,)),
            dma((RING - 1,)), dma((RING - 1,)), dma((lanes - 1,)), dma((depths,)),
            dma((slabs // 2 * lanes,)),
        ],
        compiler_params=pltpu.CompilerParams(
            collective_id=0, has_side_effects=True, vmem_limit_bytes=67043328
        ),
        name="step",
    )(objects[0], observed[0], pupil_phase[0], pupil_amplitude[0], *[table[name] for name in NAMES])
    return new_objects[None], new_phase[None]


def solution(mesh):
    return jax.shard_map(
        on_device,
        mesh=mesh,
        in_specs=(
            P("depth", None, "tile", None),
            P("depth", None, "tile", None),
            P("depth", None, None),
            P("depth", None, None),
        ),
        out_specs=(P("depth", None, "tile", None), P("depth", None, None)),
        check_vma=False,
    )
```

```python
import math

import jax
import jax.numpy as jnp
import numpy as np
from jax import lax
from jax.experimental import pallas as pl
from jax.experimental.pallas import tpu as pltpu
from jax.sharding import PartitionSpec as P

HALF = 64
KER = 129
PUP = 128
PAD = 136
BACKGROUND = 0.1
STEP_SIZE = 0.3
EPSILON = 1e-06
RING = 8
SIDES = 2
GROUP = 2
MESH = pl.DeviceIdType.MESH


def real_form(matrix):
    return np.block([[matrix.real, matrix.imag], [-matrix.imag, matrix.real]])


def tables(rows, cols):
    span = rows + 2 * HALF
    half = span // 2
    omega = 2.0 * np.pi * (2.0 * np.arange(half) + 0.5) / span
    turn = np.exp(-1j * omega[:, None] * np.arange(span)[None, :])
    row_all = np.concatenate([turn.real, turn.imag])
    row_mid = row_all[:, HALF : HALF + rows]
    lag = np.exp(-1j * omega[:, None] * (np.arange(PAD) - HALF)[None, :]) * (np.arange(PAD) < KER)
    row_lag = np.concatenate([lag.real, lag.imag])
    part = cols // 2
    where = np.arange(part)
    even = np.exp(-2j * np.pi * where[:, None] * (2 * where)[None, :] / cols)
    odd = np.exp(-2j * np.pi * where[:, None] * (2 * where + 1)[None, :] / cols)
    outs = np.arange(cols)
    ring = np.exp(-2j * np.pi * (((outs - HALF)[:, None] * np.arange(PUP)[None, :]) % KER) / KER)
    ring = ring * (outs < KER)[:, None]
    left = np.concatenate([ring.real[:PAD], ring.imag[:PAD]])
    right = np.concatenate([ring.real.T, ring.imag.T])
    grid = np.arange(PUP) - (PUP - 1) / 2.0
    aperture = (grid[:, None] ** 2 + grid[None, :] ** 2 <= (PUP / 2.0) ** 2).astype(float)
    named = dict(
        row_all=row_all,
        row_mid=row_mid,
        row_back=row_mid.T * (2.0 / span / cols),
        row_lag=row_lag,
        row_lag_back=row_lag.T * (2.0 / span / cols),
        even=real_form(even),
        odd=real_form(odd),
        left=left,
        right=right,
        aperture=aperture,
    )
    return {name: np.ascontiguousarray(value, dtype=np.float32) for name, value in named.items()}


def mm(left, right):
    return jnp.dot(left, right, precision=lax.Precision.HIGH, preferred_element_type=jnp.float32)


def sin_cos(angle):
    count = jnp.floor(angle * (2.0 / math.pi) + 0.5)
    rest = angle - count * 1.5703125
    rest = rest - count * 4.8375129699707031e-4
    rest = rest - count * 7.549789954891882e-8
    square = rest * rest
    sine = ((-1.9515295891e-4 * square + 8.3321608736e-3) * square - 1.6666654611e-1) * square * rest + rest
    cosine = (
        (2.443315711809948e-5 * square - 1.388731625493765e-3) * square + 4.166664568298827e-2
    ) * square * square - 0.5 * square + 1.0
    quarter = count - 4.0 * jnp.floor(count * 0.25)
    swap = (quarter == 1.0) | (quarter == 3.0)
    sin_out = jnp.where(swap, cosine, sine)
    cos_out = jnp.where(swap, sine, cosine)
    sin_out = jnp.where(quarter >= 2.0, -sin_out, sin_out)
    cos_out = jnp.where((quarter == 1.0) | (quarter == 2.0), -cos_out, cos_out)
    return sin_out, cos_out


def beside(one, two):
    return jnp.concatenate([one, two], axis=1)


def above(one, two):
    return jnp.concatenate([one, two], axis=0)


def split_cols(rowed):
    half = rowed.shape[0] // 2
    part = rowed.shape[1] // 2
    plus = rowed[:, :part] + rowed[:, part:]
    minus = rowed[:, :part] - rowed[:, part:]
    return beside(plus[:half], plus[half:]), beside(minus[:half], minus[half:])


def join_cols(even, odd):
    part = even.shape[1] // 2
    plus = even + odd
    minus = even - odd
    return above(
        beside(plus[:, :part], minus[:, :part]),
        beside(plus[:, part:], minus[:, part:]),
    )


def stacked(values):
    return values[0] if len(values) == 1 else jnp.concatenate(values, axis=0)


def summed_over(value, rows):
    total = value[:rows]
    for at in range(rows, value.shape[0], rows):
        total = total + value[at : at + rows]
    return total


def times(one, two):
    part = one.shape[1] // 2
    ar, ai, br, bi = one[:, :part], one[:, part:], two[:, :part], two[:, part:]
    return beside(ar * br - ai * bi, ar * bi + ai * br)


def times_conj(one, two):
    part = one.shape[1] // 2
    ar, ai, br, bi = one[:, :part], one[:, part:], two[:, :part], two[:, part:]
    return beside(ar * br + ai * bi, ai * br - ar * bi)


NAMES = ("aperture", "left", "right", "row_lag", "row_all", "even", "odd", "row_back", "row_mid", "row_lag_back")
EARLY = ("phase", "amp", "aperture", "left", "right", "obj")


def kernel(tiles, depths, planes, rows, cols, *refs):
    count = len(NAMES)
    obj_in, obs_in, phase_in, amp_in = refs[:4]
    table_in = refs[4 : 4 + count]
    out_obj, out_phase = refs[4 + count : 6 + count]
    t = dict(zip(NAMES, refs[6 + count : 6 + 2 * count]))
    (
        obs, phase_ref, amp_ref, load_sem, even_back, odd_back, strip, rstrip, spec_e, spec_o,
        share, part, mine, stack, full, square, sums,
        h1s, h1r, h2s, h2r, s1, r1, s2, r2, s3, r3, s4, r4, s5,
    ) = refs[6 + 2 * count :]
    me = lax.axis_index("tile")
    layer = lax.axis_index("depth")
    span = rows + 2 * HALF
    half = span // 2
    slabs = tiles // RING
    slab, spot = me // RING, lax.rem(me, RING)
    lanes = depths // SIDES
    side, lane = layer // lanes, lax.rem(layer, lanes)
    lowest, highest = slab == 0, slab == slabs - 1
    near = slabs // 2
    source_slab = jnp.where(slab < near, slabs - 1, 0)

    def at_tile(tile):
        return {"tile": tile, "depth": layer}

    def at_spot(off):
        return at_tile(slab * RING + lax.rem(spot + off, RING))

    def at_slab(off):
        return at_tile(lax.rem(slab + off, slabs) * RING + spot)

    def at_lane(off):
        return {"tile": me, "depth": side * lanes + lax.rem(lane + off, lanes)}

    def across(to_slab, to_lane):
        return {"tile": to_slab * RING + spot, "depth": (SIDES - 1 - side) * lanes + to_lane}

    barrier = pltpu.get_barrier_semaphore()

    def greet(device):
        pl.semaphore_signal(barrier, 1, device_id=device, device_id_type=MESH)

    greet(at_tile(lax.rem(me + 1, tiles)))
    greet(at_tile(lax.rem(me + tiles - 1, tiles)))
    for off in range(1, RING):
        greet(at_spot(off))
    for off in range(1, slabs):
        greet(at_slab(off))
    for off in range(1, lanes):
        greet(at_lane(off))
    for to_lane in range(lanes):
        greet(across(source_slab, to_lane))
    near_sends = jnp.where(lowest | highest, near * lanes, 0)
    greeted = 2 + RING - 1 + slabs - 1 + lanes - 1 + near_sends

    loads = {"phase": pltpu.make_async_copy(phase_in, phase_ref, load_sem.at[0])}
    loads["amp"] = pltpu.make_async_copy(amp_in, amp_ref, load_sem.at[1])
    loads["obj"] = pltpu.make_async_copy(obj_in, strip.at[:, pl.ds(HALF, rows)], load_sem.at[2])
    loads["obs"] = pltpu.make_async_copy(obs_in, obs, load_sem.at[3])
    for index, name in enumerate(NAMES):
        loads[name] = pltpu.make_async_copy(table_in[index], t[name], load_sem.at[4 + index])
    for name in EARLY:
        loads[name].start()
    for name in loads:
        if name not in EARLY:
            loads[name].start()

    def ready(*names):
        for name in names:
            loads[name].wait()

    def halo(buffer, sends, recvs, plane, direction):
        peer = lax.rem(me + (1 if direction == 0 else tiles - 1), tiles)
        start = rows if direction == 0 else HALF
        target = 0 if direction == 0 else HALF + rows
        slot = 2 * plane + direction
        return pltpu.make_async_remote_copy(
            buffer.at[plane, pl.ds(start, HALF)], buffer.at[plane, pl.ds(target, HALF)],
            sends.at[slot], recvs.at[slot], device_id=at_tile(peer), device_id_type=MESH,
        )

    def halo1(plane, direction):
        return halo(strip, h1s, h1r, plane, direction)

    def halo2(plane, direction):
        return halo(rstrip, h2s, h2r, plane, direction)

    def full_left():
        real, imag = t["left"][:PAD], t["left"][PAD:]
        return above(beside(real, -imag), beside(imag, real))

    def full_right():
        real, imag = t["right"][:PUP], t["right"][PUP:]
        return above(beside(real, imag), beside(-imag, real))

    def spread_of(angle):
        sine, cosine = sin_cos(angle)
        weight = amp_ref[...] * t["aperture"][...]
        field = above(weight * cosine, weight * sine)
        lefts = mm(full_left(), field)
        outer = mm(beside(lefts[:PAD], lefts[PAD:]), full_right())
        real, imag = outer[:, :cols], outer[:, cols:]
        intensity = real * real + imag * imag
        total = jnp.sum(intensity)
        return field, real, imag, total, intensity

    part_cols = cols // 2
    column = lax.broadcasted_iota(jnp.int32, (1, part_cols), 1)
    flip = 1.0 - 2.0 * lax.rem(column, 2).astype(jnp.float32)
    flips = beside(flip, flip)
    turn_on = beside(-flip, flip)
    turn_off = beside(flip, -flip)

    def swapped(value):
        return beside(value[:, part_cols:], value[:, :part_cols])

    def spectrum_of(intensity, total):
        even, odd = split_cols(mm(t["row_lag"][...], intensity))
        share_of = 1.0 / total
        return (
            mm(even, t["even"][...]) * (flips * share_of),
            swapped(mm(odd, t["odd"][...])) * (turn_on * share_of),
        )

    def columns(rowed):
        pairs = [split_cols(value) for value in rowed]
        return (
            mm(stacked([even for even, _ in pairs]), t["even"][...]),
            mm(stacked([odd for _, odd in pairs]), t["odd"][...]),
        )

    def back(even, odd):
        even, odd = mm(even, even_back[...]), mm(odd, odd_back[...])
        return [
            mm(t["row_back"][...], join_cols(even[at : at + half], odd[at : at + half]))
            for at in range(0, even.shape[0], half)
        ]

    def twice(value):
        return stacked([value] * GROUP)

    def blurred(first, kernel_e, kernel_o):
        at = pl.ds(first * half, GROUP * half)
        return back(times(spec_e[at], twice(kernel_e)), times(spec_o[at], twice(kernel_o)))

    groups = range(0, planes, GROUP)

    def wait_group(halo_of, first):
        for plane in range(first, first + GROUP):
            halo_of(plane, 0).wait()
            halo_of(plane, 1).wait()

    ready("phase", "amp", "aperture", "left", "right")
    phase = phase_ref[...]
    field, real, imag, total, intensity = spread_of(phase)
    ready("obj")
    pl.semaphore_wait(barrier, greeted)
    for plane in range(planes):
        halo1(plane, 0).start()
        halo1(plane, 1).start()
    ready(*[name for name in loads if name not in EARLY])
    even_back[...] = t["even"][...].T
    odd_back[...] = t["odd"][...].T
    kernel_e, kernel_o = spectrum_of(intensity, total)

    cross_e = jnp.zeros((half, cols), jnp.float32)
    cross_o = jnp.zeros((half, cols), jnp.float32)
    for first in groups:
        wait_group(halo1, first)
        mates = range(first, first + GROUP)
        even, odd = columns([mm(t["row_all"][...], strip[plane]) for plane in mates])
        at = pl.ds(first * half, GROUP * half)
        spec_e[at] = even
        spec_o[at] = odd
        blurs = back(times(even, twice(kernel_e)), times(odd, twice(kernel_o)))
        misfits = [1.0 - obs[plane] / (blur + BACKGROUND) for plane, blur in zip(mates, blurs)]
        mis_e, mis_o = columns([mm(t["row_mid"][...], misfit) for misfit in misfits])
        cross_e = cross_e + summed_over(times_conj(mis_e, spec_e[at]), half)
        cross_o = cross_o + summed_over(times_conj(mis_o, spec_o[at]), half)
    lagged = join_cols(mm(cross_e * flips, even_back[...]), mm(swapped(cross_o) * turn_off, odd_back[...]))
    psf_grad = mm(t["row_lag_back"][...], lagged)

    scale = 2.0 / total
    centred = (psf_grad - jnp.sum(psf_grad * intensity) / total) * scale
    rest = jnp.zeros((cols - PAD, cols), jnp.float32)
    right = full_right()
    lefts = mm(right, jnp.concatenate([centred * real, rest, centred * imag, rest], axis=0))
    pupils = lax.dot_general(
        beside(lefts[:PUP], lefts[PUP:]), right, (((1,), (1,)), ((), ())),
        precision=lax.Precision.HIGH, preferred_element_type=jnp.float32,
    )
    mygrad = field[:PUP] * pupils[:, PUP:] - field[PUP:] * pupils[:, :PUP]

    chunk = PUP // RING
    for piece in range(RING):
        share[piece] = mygrad[piece * chunk : (piece + 1) * chunk]

    def scatter(off):
        return pltpu.make_async_remote_copy(
            share.at[lax.rem(spot + off, RING)], part.at[off - 1], s1.at[off - 1], r1.at[off - 1],
            device_id=at_spot(off), device_id_type=MESH,
        )

    def exchange(off):
        return pltpu.make_async_remote_copy(
            mine, stack.at[slab], s2.at[off - 1], r2.at[off - 1],
            device_id=at_slab(off), device_id_type=MESH,
        )

    def gather(off):
        return pltpu.make_async_remote_copy(
            full.at[spot], full.at[spot], s3.at[off - 1], r3.at[off - 1],
            device_id=at_spot(off), device_id_type=MESH,
        )

    def lane_sum(off):
        return pltpu.make_async_remote_copy(
            square, sums.at[layer], s4.at[off - 1], r4.at[layer],
            device_id=at_lane(off), device_id_type=MESH,
        )

    def far_sum(step, to_lane):
        return pltpu.make_async_remote_copy(
            square, sums.at[layer], s5.at[step * lanes + to_lane], r4.at[layer],
            device_id=across(jnp.where(lowest, near, 0) + step, to_lane), device_id_type=MESH,
        )

    for off in range(1, RING):
        scatter(off).start()
    for off in range(1, RING):
        scatter(off).wait()
    summed = share[spot]
    for off in range(1, RING):
        summed = summed + part[off - 1]
    mine[...] = summed
    for off in range(1, slabs):
        exchange(off).start()
    stack[slab] = summed
    for off in range(1, slabs):
        exchange(off).wait()
    summed = stack[0]
    for other in range(1, slabs):
        summed = summed + stack[other]
    full[spot] = summed
    for off in range(1, RING):
        gather(off).start()
    for off in range(1, RING):
        gather(off).wait()
    gradient = jnp.concatenate([full[piece] for piece in range(RING)], axis=0)
    square[...] = jnp.broadcast_to(jnp.sum(gradient * gradient), (8, 128))
    for off in range(1, lanes):
        lane_sum(off).start()

    @pl.when(lowest | highest)
    def _():
        for step in range(near):
            for to_lane in range(lanes):
                far_sum(step, to_lane).start()

    sums[layer] = square[...]
    for off in range(1, depths):
        other = lax.rem(layer + off, depths)
        pltpu.make_async_remote_copy(
            sums.at[other], sums.at[other], s4.at[0], r4.at[other], device_id=at_lane(1), device_id_type=MESH
        ).wait_recv()
    for off in range(1, lanes):
        lane_sum(off).wait_send()

    @pl.when(lowest | highest)
    def _():
        for step in range(near):
            for to_lane in range(lanes):
                far_sum(step, to_lane).wait_send()

    squares = sums[0]
    for other in range(1, depths):
        squares = squares + sums[other]
    mean_square = squares[0:1] * (1.0 / (depths * PUP * PUP))
    new_phase = phase - STEP_SIZE * gradient / jnp.sqrt(mean_square + EPSILON)
    out_phase[...] = new_phase

    _, _, _, total, intensity = spread_of(new_phase)
    kernel_e, kernel_o = spectrum_of(intensity, total)
    for first in groups:
        for plane, blur in zip(range(first, first + GROUP), blurred(first, kernel_e, kernel_o)):
            rstrip[plane, pl.ds(HALF, rows)] = obs[plane] / (blur + BACKGROUND)
            halo2(plane, 0).start()
            halo2(plane, 1).start()
    for first in groups:
        wait_group(halo2, first)
        mates = range(first, first + GROUP)
        even, odd = columns([mm(t["row_all"][...], rstrip[plane]) for plane in mates])
        corrections = back(times_conj(even, twice(kernel_e)), times_conj(odd, twice(kernel_o)))
        for plane, correction in zip(mates, corrections):
            out_obj[plane] = strip[plane, pl.ds(HALF, rows)] * correction


def write_kernel(objects, phase, objects_out, phase_out, sem):
    one = pltpu.make_async_copy(objects, objects_out, sem.at[0])
    two = pltpu.make_async_copy(phase, phase_out, sem.at[1])
    one.start()
    two.start()
    one.wait()
    two.wait()


def on_device(objects, observed, pupil_phase, pupil_amplitude):
    tiles, depths = lax.axis_size("tile"), lax.axis_size("depth")
    _, planes, rows, cols = objects.shape
    span = rows + 2 * HALF
    half = span // 2
    table = tables(rows, cols)
    f32 = jnp.float32
    vmem = pltpu.VMEM
    dma = pltpu.SemaphoreType.DMA
    chunk = PUP // RING
    slabs = tiles // RING
    lanes = depths // SIDES
    body = lambda *refs: kernel(tiles, depths, planes, rows, cols, *refs)
    new_objects, new_phase = pl.pallas_call(
        body,
        out_shape=(
            jax.ShapeDtypeStruct((planes, rows, cols), f32),
            jax.ShapeDtypeStruct((PUP, PUP), f32),
        ),
        in_specs=[pl.BlockSpec(memory_space=pltpu.HBM)] * (4 + len(NAMES)),
        out_specs=(pl.BlockSpec(memory_space=vmem), pl.BlockSpec(memory_space=vmem)),
        scratch_shapes=[vmem(table[name].shape, f32) for name in NAMES]
        + [
            vmem((planes, rows, cols), f32),
            vmem((PUP, PUP), f32),
            vmem((PUP, PUP), f32),
            dma((4 + len(NAMES),)),
            vmem((cols, cols), f32),
            vmem((cols, cols), f32),
            vmem((planes, span, cols), f32),
            vmem((planes, span, cols), f32),
            vmem((planes * half, cols), f32),
            vmem((planes * half, cols), f32),
            vmem((RING, chunk, PUP), f32),
            vmem((RING - 1, chunk, PUP), f32),
            vmem((chunk, PUP), f32),
            vmem((slabs, chunk, PUP), f32),
            vmem((RING, chunk, PUP), f32),
            vmem((8, 128), f32),
            vmem((depths, 8, 128), f32),
            dma((2 * planes,)), dma((2 * planes,)), dma((2 * planes,)), dma((2 * planes,)),
            dma((RING - 1,)), dma((RING - 1,)), dma((slabs - 1,)), dma((slabs - 1,)),
            dma((RING - 1,)), dma((RING - 1,)), dma((lanes - 1,)), dma((depths,)),
            dma((slabs // 2 * lanes,)),
        ],
        compiler_params=pltpu.CompilerParams(
            collective_id=0, has_side_effects=True, vmem_limit_bytes=48 * 1024 * 1024
        ),
        name="step",
    )(*[
        pltpu.with_memory_space_constraint(value, pltpu.HBM)
        for value in (objects[0], observed[0], pupil_phase[0], pupil_amplitude[0], *[table[name] for name in NAMES])
    ])
    new_objects, new_phase = pl.pallas_call(
        write_kernel,
        out_shape=(
            jax.ShapeDtypeStruct((planes, rows, cols), f32),
            jax.ShapeDtypeStruct((PUP, PUP), f32),
        ),
        in_specs=[pl.BlockSpec(memory_space=pl.ANY)] * 2,
        out_specs=(pl.BlockSpec(memory_space=pltpu.HBM), pl.BlockSpec(memory_space=pltpu.HBM)),
        scratch_shapes=[dma((2,))],
        name="write",
    )(*[pltpu.with_memory_space_constraint(value, vmem) for value in (new_objects, new_phase)])
    return new_objects[None], new_phase[None]


def solution(mesh):
    return jax.shard_map(
        on_device,
        mesh=mesh,
        in_specs=(
            P("depth", None, "tile", None),
            P("depth", None, "tile", None),
            P("depth", None, None),
            P("depth", None, None),
        ),
        out_specs=(P("depth", None, "tile", None), P("depth", None, None)),
        check_vma=False,
    )
```

```python
import math

import jax
import jax.numpy as jnp
import numpy as np
from jax import lax
from jax.experimental import pallas as pl
from jax.experimental.pallas import tpu as pltpu
from jax.sharding import PartitionSpec as P

HALF = 64
KER = 129
PUP = 128
PAD = 136
BACKGROUND = 0.1
STEP_SIZE = 0.3
EPSILON = 1e-06
RING = 8
SIDES = 2
GROUP = 2
MESH = pl.DeviceIdType.MESH


def real_form(matrix):
    return np.block([[matrix.real, matrix.imag], [-matrix.imag, matrix.real]])


def tables(rows, cols):
    span = rows + 2 * HALF
    half = span // 2
    omega = 2.0 * np.pi * (2.0 * np.arange(half) + 0.5) / span
    turn = np.exp(-1j * omega[:, None] * np.arange(span)[None, :])
    row_all = np.concatenate([turn.real, turn.imag])
    row_mid = row_all[:, HALF : HALF + rows]
    lag = np.exp(-1j * omega[:, None] * (np.arange(PAD) - HALF)[None, :]) * (np.arange(PAD) < KER)
    row_lag = np.concatenate([lag.real, lag.imag])
    part = cols // 2
    where = np.arange(part)
    even = np.exp(-2j * np.pi * where[:, None] * (2 * where)[None, :] / cols)
    odd = np.exp(-2j * np.pi * where[:, None] * (2 * where + 1)[None, :] / cols)
    outs = np.arange(cols)
    ring = np.exp(-2j * np.pi * (((outs - HALF)[:, None] * np.arange(PUP)[None, :]) % KER) / KER)
    ring = ring * (outs < KER)[:, None]
    left = np.concatenate([ring.real[:PAD], ring.imag[:PAD]])
    right = np.concatenate([ring.real.T, ring.imag.T])
    grid = np.arange(PUP) - (PUP - 1) / 2.0
    aperture = (grid[:, None] ** 2 + grid[None, :] ** 2 <= (PUP / 2.0) ** 2).astype(float)
    named = dict(
        row_all=row_all,
        row_mid=row_mid,
        row_back=row_mid.T * (2.0 / span / cols),
        row_lag=row_lag,
        row_lag_back=row_lag.T * (2.0 / span / cols),
        even=real_form(even),
        odd=real_form(odd),
        left=left,
        right=right,
        aperture=aperture,
    )
    return {name: np.ascontiguousarray(value, dtype=np.float32) for name, value in named.items()}


def mm(left, right):
    return jnp.dot(left, right, precision=lax.Precision.HIGH, preferred_element_type=jnp.float32)


def sin_cos(angle):
    count = jnp.floor(angle * (2.0 / math.pi) + 0.5)
    rest = angle - count * 1.5703125
    rest = rest - count * 4.8375129699707031e-4
    rest = rest - count * 7.549789954891882e-8
    square = rest * rest
    sine = ((-1.9515295891e-4 * square + 8.3321608736e-3) * square - 1.6666654611e-1) * square * rest + rest
    cosine = (
        (2.443315711809948e-5 * square - 1.388731625493765e-3) * square + 4.166664568298827e-2
    ) * square * square - 0.5 * square + 1.0
    quarter = count - 4.0 * jnp.floor(count * 0.25)
    swap = (quarter == 1.0) | (quarter == 3.0)
    sin_out = jnp.where(swap, cosine, sine)
    cos_out = jnp.where(swap, sine, cosine)
    sin_out = jnp.where(quarter >= 2.0, -sin_out, sin_out)
    cos_out = jnp.where((quarter == 1.0) | (quarter == 2.0), -cos_out, cos_out)
    return sin_out, cos_out


def beside(one, two):
    return jnp.concatenate([one, two], axis=1)


def above(one, two):
    return jnp.concatenate([one, two], axis=0)


def split_cols(rowed):
    half = rowed.shape[0] // 2
    part = rowed.shape[1] // 2
    plus = rowed[:, :part] + rowed[:, part:]
    minus = rowed[:, :part] - rowed[:, part:]
    return beside(plus[:half], plus[half:]), beside(minus[:half], minus[half:])


def join_cols(even, odd):
    part = even.shape[1] // 2
    plus = even + odd
    minus = even - odd
    return above(
        beside(plus[:, :part], minus[:, :part]),
        beside(plus[:, part:], minus[:, part:]),
    )


def stacked(values):
    return values[0] if len(values) == 1 else jnp.concatenate(values, axis=0)


def summed_over(value, rows):
    total = value[:rows]
    for at in range(rows, value.shape[0], rows):
        total = total + value[at : at + rows]
    return total


def times(one, two):
    part = one.shape[1] // 2
    ar, ai, br, bi = one[:, :part], one[:, part:], two[:, :part], two[:, part:]
    return beside(ar * br - ai * bi, ar * bi + ai * br)


def times_conj(one, two):
    part = one.shape[1] // 2
    ar, ai, br, bi = one[:, :part], one[:, part:], two[:, :part], two[:, part:]
    return beside(ar * br + ai * bi, ai * br - ar * bi)


NAMES = ("aperture", "left", "right", "row_lag", "row_all", "even", "odd", "row_back", "row_mid", "row_lag_back")
EARLY = ("phase", "amp", "aperture", "left", "right", "obj")


def kernel(tiles, depths, planes, rows, cols, *refs):
    count = len(NAMES)
    obj_in, obs_in, phase_in, amp_in = refs[:4]
    table_in = refs[4 : 4 + count]
    out_obj, out_phase = refs[4 + count : 6 + count]
    t = dict(zip(NAMES, refs[6 + count : 6 + 2 * count]))
    (
        phase_ref, amp_ref, load_sem, even_back, odd_back, big, obs, spec_e, spec_o,
        share, part, mine, stack, full, square, sums, spots, spot_sum,
        h1s, h1r, h2s, h2r, h3s, h3r, s1, r1, s2, r2, s3, r3, s4, r4, s5, s6, r6,
    ) = refs[6 + 2 * count :]
    me = lax.axis_index("tile")
    layer = lax.axis_index("depth")
    span = rows + 2 * HALF
    half = span // 2
    slabs = tiles // RING
    slab, spot = me // RING, lax.rem(me, RING)
    lanes = depths // SIDES
    side, lane = layer // lanes, lax.rem(layer, lanes)
    lowest, highest = slab == 0, slab == slabs - 1
    near = slabs // 2
    source_slab = jnp.where(slab < near, slabs - 1, 0)

    def at_tile(tile):
        return {"tile": tile, "depth": layer}

    def at_spot(off):
        return at_tile(slab * RING + lax.rem(spot + off, RING))

    def at_slab(off):
        return at_tile(lax.rem(slab + off, slabs) * RING + spot)

    def at_lane(off):
        return {"tile": me, "depth": side * lanes + lax.rem(lane + off, lanes)}

    def across(to_slab, to_lane):
        return {"tile": to_slab * RING + spot, "depth": (SIDES - 1 - side) * lanes + to_lane}

    barrier = pltpu.get_barrier_semaphore()

    def greet(device):
        pl.semaphore_signal(barrier, 1, device_id=device, device_id_type=MESH)

    greet(at_tile(lax.rem(me + 1, tiles)))
    greet(at_tile(lax.rem(me + tiles - 1, tiles)))
    for off in range(1, RING):
        greet(at_spot(off))
    for off in range(1, slabs):
        greet(at_slab(off))
    for off in range(1, lanes):
        greet(at_lane(off))
    for to_lane in range(lanes):
        greet(across(source_slab, to_lane))
    near_sends = jnp.where(lowest | highest, near * lanes, 0)
    greeted = 2 + RING - 1 + slabs - 1 + lanes - 1 + near_sends

    loads = {"phase": pltpu.make_async_copy(phase_in, phase_ref, load_sem.at[0])}
    loads["amp"] = pltpu.make_async_copy(amp_in, amp_ref, load_sem.at[1])
    loads["obj"] = pltpu.make_async_copy(obj_in, big.at[:, pl.ds(rows, rows)], load_sem.at[2])
    loads["obs"] = pltpu.make_async_copy(obs_in, obs.at[:, pl.ds(HALF, rows)], load_sem.at[3])
    for index, name in enumerate(NAMES):
        loads[name] = pltpu.make_async_copy(table_in[index], t[name], load_sem.at[4 + index])
    for name in EARLY:
        loads[name].start()
    for name in loads:
        if name not in EARLY:
            loads[name].start()

    def ready(*names):
        for name in names:
            loads[name].wait()

    def halo(buffer, first, mine_from, theirs_to, sends, recvs, plane, direction):
        peer = lax.rem(me + (1 if direction == 0 else tiles - 1), tiles)
        slot = 2 * plane + direction
        return pltpu.make_async_remote_copy(
            buffer.at[plane, pl.ds(first + mine_from, HALF)], buffer.at[plane, pl.ds(first + theirs_to, HALF)],
            sends.at[slot], recvs.at[slot], device_id=at_tile(peer), device_id_type=MESH,
        )

    def halo1(plane, direction):
        return halo(big, rows, *((rows - HALF, -HALF) if direction == 0 else (0, rows)), h1s, h1r, plane, direction)

    def halo2(plane, direction):
        return halo(big, rows, *((0, -rows) if direction == 0 else (HALF, rows + HALF)), h2s, h2r, plane, direction)

    def halo3(plane, direction):
        return halo(obs, HALF, *((rows - HALF, -HALF) if direction == 0 else (0, rows)), h3s, h3r, plane, direction)

    def full_left():
        real, imag = t["left"][:PAD], t["left"][PAD:]
        return above(beside(real, -imag), beside(imag, real))

    def full_right():
        real, imag = t["right"][:PUP], t["right"][PUP:]
        return above(beside(real, imag), beside(-imag, real))

    def spread_of(angle):
        sine, cosine = sin_cos(angle)
        weight = amp_ref[...] * t["aperture"][...]
        field = above(weight * cosine, weight * sine)
        lefts = mm(full_left(), field)
        outer = mm(beside(lefts[:PAD], lefts[PAD:]), full_right())
        real, imag = outer[:, :cols], outer[:, cols:]
        intensity = real * real + imag * imag
        total = jnp.sum(intensity)
        return field, real, imag, total, intensity

    part_cols = cols // 2
    column = lax.broadcasted_iota(jnp.int32, (1, part_cols), 1)
    flip = 1.0 - 2.0 * lax.rem(column, 2).astype(jnp.float32)
    flips = beside(flip, flip)
    turn_on = beside(-flip, flip)
    turn_off = beside(flip, -flip)

    def swapped(value):
        return beside(value[:, part_cols:], value[:, :part_cols])

    def spectrum_of(intensity, total):
        even, odd = split_cols(mm(t["row_lag"][...], intensity))
        share_of = 1.0 / total
        return (
            mm(even, t["even"][...]) * (flips * share_of),
            swapped(mm(odd, t["odd"][...])) * (turn_on * share_of),
        )

    def columns(rowed):
        pairs = [split_cols(value) for value in rowed]
        return (
            mm(stacked([even for even, _ in pairs]), t["even"][...]),
            mm(stacked([odd for _, odd in pairs]), t["odd"][...]),
        )

    def back(even, odd):
        even, odd = mm(even, even_back[...]), mm(odd, odd_back[...])
        return [
            mm(t["row_back"][...], join_cols(even[at : at + half], odd[at : at + half]))
            for at in range(0, even.shape[0], half)
        ]

    def twice(value):
        return stacked([value] * GROUP)

    groups = range(0, planes, GROUP)

    def wait_group(halo_of, first):
        for plane in range(first, first + GROUP):
            halo_of(plane, 0).wait()
            halo_of(plane, 1).wait()

    ready("phase", "amp", "aperture", "left", "right")
    phase = phase_ref[...]
    field, real, imag, total, intensity = spread_of(phase)
    ready("obj")
    pl.semaphore_wait(barrier, greeted)
    for plane in range(planes):
        halo1(plane, 0).start()
        halo1(plane, 1).start()
    for plane in range(planes):
        halo2(plane, 0).start()
        halo2(plane, 1).start()
    ready(*[name for name in loads if name not in EARLY])
    for plane in range(planes):
        halo3(plane, 0).start()
        halo3(plane, 1).start()
    even_back[...] = t["even"][...].T
    odd_back[...] = t["odd"][...].T
    kernel_e, kernel_o = spectrum_of(intensity, total)

    cross_e = jnp.zeros((half, cols), jnp.float32)
    cross_o = jnp.zeros((half, cols), jnp.float32)
    for first in groups:
        wait_group(halo1, first)
        mates = range(first, first + GROUP)
        even, odd = columns([mm(t["row_all"][...], big[plane, pl.ds(HALF, span)]) for plane in mates])
        blurs = back(times(even, twice(kernel_e)), times(odd, twice(kernel_o)))
        misfits = [1.0 - obs[plane, pl.ds(HALF, rows)] / (blur + BACKGROUND) for plane, blur in zip(mates, blurs)]
        mis_e, mis_o = columns([mm(t["row_mid"][...], misfit) for misfit in misfits])
        cross_e = cross_e + summed_over(times_conj(mis_e, even), half)
        cross_o = cross_o + summed_over(times_conj(mis_o, odd), half)
    lagged = join_cols(mm(cross_e * flips, even_back[...]), mm(swapped(cross_o) * turn_off, odd_back[...]))
    psf_grad = mm(t["row_lag_back"][...], lagged)

    scale = 2.0 / total
    centred = (psf_grad - jnp.sum(psf_grad * intensity) / total) * scale
    rest = jnp.zeros((cols - PAD, cols), jnp.float32)
    right = full_right()
    lefts = mm(right, jnp.concatenate([centred * real, rest, centred * imag, rest], axis=0))
    pupils = lax.dot_general(
        beside(lefts[:PUP], lefts[PUP:]), right, (((1,), (1,)), ((), ())),
        precision=lax.Precision.HIGH, preferred_element_type=jnp.float32,
    )
    mygrad = field[:PUP] * pupils[:, PUP:] - field[PUP:] * pupils[:, :PUP]

    chunk = PUP // RING
    for piece in range(RING):
        share[piece] = mygrad[piece * chunk : (piece + 1) * chunk]

    def scatter(off):
        return pltpu.make_async_remote_copy(
            share.at[lax.rem(spot + off, RING)], part.at[off - 1], s1.at[off - 1], r1.at[off - 1],
            device_id=at_spot(off), device_id_type=MESH,
        )

    def exchange(off):
        return pltpu.make_async_remote_copy(
            mine, stack.at[slab], s2.at[off - 1], r2.at[off - 1],
            device_id=at_slab(off), device_id_type=MESH,
        )

    def gather(off):
        return pltpu.make_async_remote_copy(
            full.at[spot], full.at[spot], s3.at[off - 1], r3.at[off - 1],
            device_id=at_spot(off), device_id_type=MESH,
        )

    def lane_sum(off):
        return pltpu.make_async_remote_copy(
            square, sums.at[layer], s4.at[off - 1], r4.at[layer],
            device_id=at_lane(off), device_id_type=MESH,
        )

    def far_sum(step, to_lane):
        return pltpu.make_async_remote_copy(
            square, sums.at[layer], s5.at[step * lanes + to_lane], r4.at[layer],
            device_id=across(jnp.where(lowest, near, 0) + step, to_lane), device_id_type=MESH,
        )

    def spot_send(off):
        return pltpu.make_async_remote_copy(
            spot_sum, spots.at[spot], s6.at[off - 1], r6.at[off - 1],
            device_id=at_spot(off), device_id_type=MESH,
        )

    def window(which):
        for first in groups:
            even, odd = columns(
                [mm(t["row_all"][...], big[plane, pl.ds(which * rows, span)]) for plane in range(first, first + GROUP)]
            )
            spec_e[which, pl.ds(first * half, GROUP * half)] = even
            spec_o[which, pl.ds(first * half, GROUP * half)] = odd

    for off in range(1, RING):
        scatter(off).start()
    for first in groups:
        wait_group(halo2, first)
    for first in groups:
        wait_group(halo3, first)
    for off in range(1, RING):
        scatter(off).wait()
    summed = share[spot]
    for off in range(1, RING):
        summed = summed + part[off - 1]
    mine[...] = summed
    for off in range(1, slabs):
        exchange(off).start()
    stack[slab] = summed
    window(0)
    for off in range(1, slabs):
        exchange(off).wait()
    summed = stack[0]
    for other in range(1, slabs):
        summed = summed + stack[other]
    full[spot] = summed
    for off in range(1, RING):
        gather(off).start()
    square[...] = jnp.broadcast_to(jnp.sum(summed * summed), (8, 128))
    for off in range(1, lanes):
        lane_sum(off).start()

    @pl.when(lowest | highest)
    def _():
        for step in range(near):
            for to_lane in range(lanes):
                far_sum(step, to_lane).start()

    sums[layer] = square[...]
    window(1)
    for off in range(1, depths):
        other = lax.rem(layer + off, depths)
        pltpu.make_async_remote_copy(
            sums.at[other], sums.at[other], s4.at[0], r4.at[other], device_id=at_lane(1), device_id_type=MESH
        ).wait_recv()
    squares = sums[0]
    for other in range(1, depths):
        squares = squares + sums[other]
    spot_sum[...] = squares
    for off in range(1, RING):
        spot_send(off).start()
    spots[spot] = squares
    for off in range(1, lanes):
        lane_sum(off).wait_send()

    @pl.when(lowest | highest)
    def _():
        for step in range(near):
            for to_lane in range(lanes):
                far_sum(step, to_lane).wait_send()

    for off in range(1, RING):
        gather(off).wait()
    gradient = jnp.concatenate([full[piece] for piece in range(RING)], axis=0)
    for off in range(1, RING):
        spot_send(off).wait()
    squares = spots[0]
    for other in range(1, RING):
        squares = squares + spots[other]
    mean_square = squares[0:1] * (1.0 / (depths * PUP * PUP))
    new_phase = phase - STEP_SIZE * gradient / jnp.sqrt(mean_square + EPSILON)
    out_phase[...] = new_phase

    _, _, _, total, intensity = spread_of(new_phase)
    kernel_e, kernel_o = spectrum_of(intensity, total)
    twice_e, twice_o = twice(kernel_e), twice(kernel_o)
    for first in groups:
        mates = range(first, first + GROUP)
        at = pl.ds(first * half, GROUP * half)
        ratios = []
        for which in range(2):
            blurs = back(times(spec_e[which, at], twice_e), times(spec_o[which, at], twice_o))
            ratios.append(
                [obs[plane, pl.ds(which * rows, rows)] / (blur + BACKGROUND) for plane, blur in zip(mates, blurs)]
            )
        even, odd = columns([mm(t["row_all"][...], above(one, two)) for one, two in zip(*ratios)])
        corrections = back(times_conj(even, twice_e), times_conj(odd, twice_o))
        for plane, correction in zip(mates, corrections):
            out_obj[plane] = big[plane, pl.ds(rows, rows)] * correction


def write_kernel(objects, phase, objects_out, phase_out, sem):
    one = pltpu.make_async_copy(objects, objects_out, sem.at[0])
    two = pltpu.make_async_copy(phase, phase_out, sem.at[1])
    one.start()
    two.start()
    one.wait()
    two.wait()


def on_device(objects, observed, pupil_phase, pupil_amplitude):
    tiles, depths = lax.axis_size("tile"), lax.axis_size("depth")
    _, planes, rows, cols = objects.shape
    span = rows + 2 * HALF
    half = span // 2
    table = tables(rows, cols)
    f32 = jnp.float32
    vmem = pltpu.VMEM
    dma = pltpu.SemaphoreType.DMA
    chunk = PUP // RING
    slabs = tiles // RING
    lanes = depths // SIDES
    body = lambda *refs: kernel(tiles, depths, planes, rows, cols, *refs)
    new_objects, new_phase = pl.pallas_call(
        body,
        out_shape=(
            jax.ShapeDtypeStruct((planes, rows, cols), f32),
            jax.ShapeDtypeStruct((PUP, PUP), f32),
        ),
        in_specs=[pl.BlockSpec(memory_space=pltpu.HBM)] * (4 + len(NAMES)),
        out_specs=(pl.BlockSpec(memory_space=vmem), pl.BlockSpec(memory_space=vmem)),
        scratch_shapes=[vmem(table[name].shape, f32) for name in NAMES]
        + [
            vmem((PUP, PUP), f32),
            vmem((PUP, PUP), f32),
            dma((4 + len(NAMES),)),
            vmem((cols, cols), f32),
            vmem((cols, cols), f32),
            vmem((planes, 3 * rows, cols), f32),
            vmem((planes, span, cols), f32),
            vmem((2, planes * half, cols), f32),
            vmem((2, planes * half, cols), f32),
            vmem((RING, chunk, PUP), f32),
            vmem((RING - 1, chunk, PUP), f32),
            vmem((chunk, PUP), f32),
            vmem((slabs, chunk, PUP), f32),
            vmem((RING, chunk, PUP), f32),
            vmem((8, 128), f32),
            vmem((depths, 8, 128), f32),
            vmem((RING, 8, 128), f32),
            vmem((8, 128), f32),
            dma((2 * planes,)), dma((2 * planes,)), dma((2 * planes,)), dma((2 * planes,)), dma((2 * planes,)), dma((2 * planes,)),
            dma((RING - 1,)), dma((RING - 1,)), dma((slabs - 1,)), dma((slabs - 1,)),
            dma((RING - 1,)), dma((RING - 1,)), dma((lanes - 1,)), dma((depths,)),
            dma((slabs // 2 * lanes,)), dma((RING - 1,)), dma((RING - 1,)),
        ],
        compiler_params=pltpu.CompilerParams(
            collective_id=0, has_side_effects=True, vmem_limit_bytes=48 * 1024 * 1024
        ),
        name="step",
    )(*[
        pltpu.with_memory_space_constraint(value, pltpu.HBM)
        for value in (objects[0], observed[0], pupil_phase[0], pupil_amplitude[0], *[table[name] for name in NAMES])
    ])
    new_objects, new_phase = pl.pallas_call(
        write_kernel,
        out_shape=(
            jax.ShapeDtypeStruct((planes, rows, cols), f32),
            jax.ShapeDtypeStruct((PUP, PUP), f32),
        ),
        in_specs=[pl.BlockSpec(memory_space=pl.ANY)] * 2,
        out_specs=(pl.BlockSpec(memory_space=pltpu.HBM), pl.BlockSpec(memory_space=pltpu.HBM)),
        scratch_shapes=[dma((2,))],
        name="write",
    )(*[pltpu.with_memory_space_constraint(value, vmem) for value in (new_objects, new_phase)])
    return new_objects[None], new_phase[None]


def solution(mesh):
    return jax.shard_map(
        on_device,
        mesh=mesh,
        in_specs=(
            P("depth", None, "tile", None),
            P("depth", None, "tile", None),
            P("depth", None, None),
            P("depth", None, None),
        ),
        out_specs=(P("depth", None, "tile", None), P("depth", None, None)),
        check_vma=False,
    )
```

```python
import math

import jax
import jax.numpy as jnp
import numpy as np
from jax import lax
from jax.experimental import pallas as pl
from jax.experimental.pallas import tpu as pltpu
from jax.sharding import PartitionSpec as P

HALF = 64
KER = 129
PUP = 128
PAD = 136
BACKGROUND = 0.1
STEP_SIZE = 0.3
EPSILON = 1e-06
RING = 8
SIDES = 2
GROUP = 2
MESH = pl.DeviceIdType.MESH


def real_form(matrix):
    return np.block([[matrix.real, matrix.imag], [-matrix.imag, matrix.real]])


def tables(rows, cols):
    span = rows + 2 * HALF
    half = span // 2
    omega = 2.0 * np.pi * (2.0 * np.arange(half) + 0.5) / span
    turn = np.exp(-1j * omega[:, None] * np.arange(span)[None, :])
    row_all = np.concatenate([turn.real, turn.imag])
    row_mid = row_all[:, HALF : HALF + rows]
    lag = np.exp(-1j * omega[:, None] * (np.arange(PAD) - HALF)[None, :]) * (np.arange(PAD) < KER)
    row_lag = np.concatenate([lag.real, lag.imag])
    part = cols // 2
    where = np.arange(part)
    even = np.exp(-2j * np.pi * where[:, None] * (2 * where)[None, :] / cols)
    odd = np.exp(-2j * np.pi * where[:, None] * (2 * where + 1)[None, :] / cols)
    outs = np.arange(cols)
    ring = np.exp(-2j * np.pi * (((outs - HALF)[:, None] * np.arange(PUP)[None, :]) % KER) / KER)
    ring = ring * (outs < KER)[:, None]
    left = np.concatenate([ring.real[:PAD], ring.imag[:PAD]])
    right = np.concatenate([ring.real.T, ring.imag.T])
    grid = np.arange(PUP) - (PUP - 1) / 2.0
    aperture = (grid[:, None] ** 2 + grid[None, :] ** 2 <= (PUP / 2.0) ** 2).astype(float)
    named = dict(
        row_all=row_all,
        row_mid=row_mid,
        row_back=row_mid.T * (2.0 / span / cols),
        row_lag=row_lag,
        row_lag_back=row_lag.T * (2.0 / span / cols),
        even=real_form(even),
        odd=real_form(odd),
        left=left,
        right=right,
        aperture=aperture,
    )
    return {name: np.ascontiguousarray(value, dtype=np.float32) for name, value in named.items()}


def mm(left, right):
    return jnp.dot(left, right, precision=lax.Precision.HIGH, preferred_element_type=jnp.float32)


def sin_cos(angle):
    count = jnp.floor(angle * (2.0 / math.pi) + 0.5)
    rest = angle - count * 1.5703125
    rest = rest - count * 4.8375129699707031e-4
    rest = rest - count * 7.549789954891882e-8
    square = rest * rest
    sine = ((-1.9515295891e-4 * square + 8.3321608736e-3) * square - 1.6666654611e-1) * square * rest + rest
    cosine = (
        (2.443315711809948e-5 * square - 1.388731625493765e-3) * square + 4.166664568298827e-2
    ) * square * square - 0.5 * square + 1.0
    quarter = count - 4.0 * jnp.floor(count * 0.25)
    swap = (quarter == 1.0) | (quarter == 3.0)
    sin_out = jnp.where(swap, cosine, sine)
    cos_out = jnp.where(swap, sine, cosine)
    sin_out = jnp.where(quarter >= 2.0, -sin_out, sin_out)
    cos_out = jnp.where((quarter == 1.0) | (quarter == 2.0), -cos_out, cos_out)
    return sin_out, cos_out


def beside(one, two):
    return jnp.concatenate([one, two], axis=1)


def above(one, two):
    return jnp.concatenate([one, two], axis=0)


def split_cols(rowed):
    half = rowed.shape[0] // 2
    part = rowed.shape[1] // 2
    plus = rowed[:, :part] + rowed[:, part:]
    minus = rowed[:, :part] - rowed[:, part:]
    return beside(plus[:half], plus[half:]), beside(minus[:half], minus[half:])


def join_cols(even, odd):
    part = even.shape[1] // 2
    plus = even + odd
    minus = even - odd
    return above(
        beside(plus[:, :part], minus[:, :part]),
        beside(plus[:, part:], minus[:, part:]),
    )


def stacked(values):
    return values[0] if len(values) == 1 else jnp.concatenate(values, axis=0)


def summed_over(value, rows):
    total = value[:rows]
    for at in range(rows, value.shape[0], rows):
        total = total + value[at : at + rows]
    return total


def times(one, two):
    part = one.shape[1] // 2
    ar, ai, br, bi = one[:, :part], one[:, part:], two[:, :part], two[:, part:]
    return beside(ar * br - ai * bi, ar * bi + ai * br)


def times_conj(one, two):
    part = one.shape[1] // 2
    ar, ai, br, bi = one[:, :part], one[:, part:], two[:, :part], two[:, part:]
    return beside(ar * br + ai * bi, ai * br - ar * bi)


NAMES = ("aperture", "left", "right", "row_lag", "row_all", "even", "odd", "row_back", "row_mid", "row_lag_back")
EARLY = ("phase", "amp", "aperture", "left", "right", "obj")


def kernel(tiles, depths, planes, rows, cols, *refs):
    count = len(NAMES)
    obj_in, obs_in, phase_in, amp_in = refs[:4]
    table_in = refs[4 : 4 + count]
    out_obj, out_phase = refs[4 + count : 6 + count]
    t = dict(zip(NAMES, refs[6 + count : 6 + 2 * count]))
    (
        phase_ref, amp_ref, load_sem, even_back, odd_back, big, obs, spec_e, spec_o,
        share, part, mine, stack, full, square, sums, spots, spot_sum,
        h1s, h1r, h2s, h2r, h3s, h3r, s1, r1, s2, r2, s3, r3, s4, r4, s5, s6, r6,
    ) = refs[6 + 2 * count :]
    me = lax.axis_index("tile")
    layer = lax.axis_index("depth")
    span = rows + 2 * HALF
    half = span // 2
    slabs = tiles // RING
    slab, spot = me // RING, lax.rem(me, RING)
    lanes = depths // SIDES
    side, lane = layer // lanes, lax.rem(layer, lanes)
    lowest, highest = slab == 0, slab == slabs - 1
    near = slabs // 2
    source_slab = jnp.where(slab < near, slabs - 1, 0)

    def at_tile(tile):
        return {"tile": tile, "depth": layer}

    def at_spot(off):
        return at_tile(slab * RING + lax.rem(spot + off, RING))

    def at_slab(off):
        return at_tile(lax.rem(slab + off, slabs) * RING + spot)

    def at_lane(off):
        return {"tile": me, "depth": side * lanes + lax.rem(lane + off, lanes)}

    def across(to_slab, to_lane):
        return {"tile": to_slab * RING + spot, "depth": (SIDES - 1 - side) * lanes + to_lane}

    barrier = pltpu.get_barrier_semaphore()

    def greet(device):
        pl.semaphore_signal(barrier, 1, device_id=device, device_id_type=MESH)

    greet(at_tile(lax.rem(me + 1, tiles)))
    greet(at_tile(lax.rem(me + tiles - 1, tiles)))
    for off in range(1, RING):
        greet(at_spot(off))
    for off in range(1, slabs):
        greet(at_slab(off))
    for off in range(1, lanes):
        greet(at_lane(off))
    for to_lane in range(lanes):
        greet(across(source_slab, to_lane))
    near_sends = jnp.where(lowest | highest, near * lanes, 0)
    greeted = 2 + RING - 1 + slabs - 1 + lanes - 1 + near_sends

    loads = {"phase": pltpu.make_async_copy(phase_in, phase_ref, load_sem.at[0])}
    loads["amp"] = pltpu.make_async_copy(amp_in, amp_ref, load_sem.at[1])
    loads["obj"] = pltpu.make_async_copy(obj_in, big.at[:, pl.ds(rows, rows)], load_sem.at[2])
    loads["obs"] = pltpu.make_async_copy(obs_in, obs.at[:, pl.ds(HALF, rows)], load_sem.at[3])
    for index, name in enumerate(NAMES):
        loads[name] = pltpu.make_async_copy(table_in[index], t[name], load_sem.at[4 + index])
    for name in EARLY:
        loads[name].start()
    for name in loads:
        if name not in EARLY:
            loads[name].start()

    def ready(*names):
        for name in names:
            loads[name].wait()

    def halo(buffer, first, mine_from, theirs_to, sends, recvs, plane, direction):
        peer = lax.rem(me + (1 if direction == 0 else tiles - 1), tiles)
        slot = 2 * plane + direction
        return pltpu.make_async_remote_copy(
            buffer.at[plane, pl.ds(first + mine_from, HALF)], buffer.at[plane, pl.ds(first + theirs_to, HALF)],
            sends.at[slot], recvs.at[slot], device_id=at_tile(peer), device_id_type=MESH,
        )

    def halo1(plane, direction):
        return halo(big, rows, *((rows - HALF, -HALF) if direction == 0 else (0, rows)), h1s, h1r, plane, direction)

    def halo2(plane, direction):
        return halo(big, rows, *((0, -rows) if direction == 0 else (HALF, rows + HALF)), h2s, h2r, plane, direction)

    def halo3(plane, direction):
        return halo(obs, HALF, *((rows - HALF, -HALF) if direction == 0 else (0, rows)), h3s, h3r, plane, direction)

    def full_left():
        real, imag = t["left"][:PAD], t["left"][PAD:]
        return above(beside(real, -imag), beside(imag, real))

    def full_right():
        real, imag = t["right"][:PUP], t["right"][PUP:]
        return above(beside(real, imag), beside(-imag, real))

    def spread_of(angle):
        sine, cosine = sin_cos(angle)
        weight = amp_ref[...] * t["aperture"][...]
        field = above(weight * cosine, weight * sine)
        lefts = mm(full_left(), field)
        outer = mm(beside(lefts[:PAD], lefts[PAD:]), full_right())
        real, imag = outer[:, :cols], outer[:, cols:]
        intensity = real * real + imag * imag
        total = jnp.sum(intensity)
        return field, real, imag, total, intensity

    part_cols = cols // 2
    column = lax.broadcasted_iota(jnp.int32, (1, part_cols), 1)
    flip = 1.0 - 2.0 * lax.rem(column, 2).astype(jnp.float32)
    flips = beside(flip, flip)
    turn_on = beside(-flip, flip)
    turn_off = beside(flip, -flip)

    def swapped(value):
        return beside(value[:, part_cols:], value[:, :part_cols])

    def spectrum_of(intensity, total):
        even, odd = split_cols(mm(t["row_lag"][...], intensity))
        share_of = 1.0 / total
        return (
            mm(even, t["even"][...]) * (flips * share_of),
            swapped(mm(odd, t["odd"][...])) * (turn_on * share_of),
        )

    def columns(rowed):
        pairs = [split_cols(value) for value in rowed]
        return (
            mm(stacked([even for even, _ in pairs]), t["even"][...]),
            mm(stacked([odd for _, odd in pairs]), t["odd"][...]),
        )

    def back(even, odd):
        even, odd = mm(even, even_back[...]), mm(odd, odd_back[...])
        return [
            mm(t["row_back"][...], join_cols(even[at : at + half], odd[at : at + half]))
            for at in range(0, even.shape[0], half)
        ]

    def twice(value):
        return stacked([value] * GROUP)

    groups = range(0, planes, GROUP)

    def wait_group(halo_of, first):
        for plane in range(first, first + GROUP):
            halo_of(plane, 0).wait()
            halo_of(plane, 1).wait()

    ready("phase", "amp", "aperture", "left", "right")
    phase = phase_ref[...]
    field, real, imag, total, intensity = spread_of(phase)
    ready("obj")
    pl.semaphore_wait(barrier, greeted)
    for plane in range(planes):
        halo1(plane, 0).start()
        halo1(plane, 1).start()
    ready(*[name for name in loads if name not in EARLY])
    even_back[...] = t["even"][...].T
    odd_back[...] = t["odd"][...].T
    kernel_e, kernel_o = spectrum_of(intensity, total)

    cross_e = jnp.zeros((half, cols), jnp.float32)
    cross_o = jnp.zeros((half, cols), jnp.float32)
    for first in groups:
        wait_group(halo1, first)
        mates = range(first, first + GROUP)
        even, odd = columns([mm(t["row_all"][...], big[plane, pl.ds(HALF, span)]) for plane in mates])
        blurs = back(times(even, twice(kernel_e)), times(odd, twice(kernel_o)))
        misfits = [1.0 - obs[plane, pl.ds(HALF, rows)] / (blur + BACKGROUND) for plane, blur in zip(mates, blurs)]
        mis_e, mis_o = columns([mm(t["row_mid"][...], misfit) for misfit in misfits])
        cross_e = cross_e + summed_over(times_conj(mis_e, even), half)
        cross_o = cross_o + summed_over(times_conj(mis_o, odd), half)
    lagged = join_cols(mm(cross_e * flips, even_back[...]), mm(swapped(cross_o) * turn_off, odd_back[...]))
    psf_grad = mm(t["row_lag_back"][...], lagged)

    scale = 2.0 / total
    centred = (psf_grad - jnp.sum(psf_grad * intensity) / total) * scale
    rest = jnp.zeros((cols - PAD, cols), jnp.float32)
    right = full_right()
    lefts = mm(right, jnp.concatenate([centred * real, rest, centred * imag, rest], axis=0))
    pupils = lax.dot_general(
        beside(lefts[:PUP], lefts[PUP:]), right, (((1,), (1,)), ((), ())),
        precision=lax.Precision.HIGH, preferred_element_type=jnp.float32,
    )
    mygrad = field[:PUP] * pupils[:, PUP:] - field[PUP:] * pupils[:, :PUP]

    chunk = PUP // RING
    for piece in range(RING):
        share[piece] = mygrad[piece * chunk : (piece + 1) * chunk]

    def scatter(off):
        return pltpu.make_async_remote_copy(
            share.at[lax.rem(spot + off, RING)], part.at[off - 1], s1.at[off - 1], r1.at[off - 1],
            device_id=at_spot(off), device_id_type=MESH,
        )

    def exchange(off):
        return pltpu.make_async_remote_copy(
            mine, stack.at[slab], s2.at[off - 1], r2.at[off - 1],
            device_id=at_slab(off), device_id_type=MESH,
        )

    def gather(off):
        return pltpu.make_async_remote_copy(
            full.at[spot], full.at[spot], s3.at[off - 1], r3.at[off - 1],
            device_id=at_spot(off), device_id_type=MESH,
        )

    def lane_sum(off):
        return pltpu.make_async_remote_copy(
            square, sums.at[layer], s4.at[off - 1], r4.at[layer],
            device_id=at_lane(off), device_id_type=MESH,
        )

    def far_sum(step, to_lane):
        return pltpu.make_async_remote_copy(
            square, sums.at[layer], s5.at[step * lanes + to_lane], r4.at[layer],
            device_id=across(jnp.where(lowest, near, 0) + step, to_lane), device_id_type=MESH,
        )

    def spot_send(off):
        return pltpu.make_async_remote_copy(
            spot_sum, spots.at[spot], s6.at[off - 1], r6.at[off - 1],
            device_id=at_spot(off), device_id_type=MESH,
        )

    def window(which):
        for first in groups:
            even, odd = columns(
                [mm(t["row_all"][...], big[plane, pl.ds(which * rows, span)]) for plane in range(first, first + GROUP)]
            )
            spec_e[which, pl.ds(first * half, GROUP * half)] = even
            spec_o[which, pl.ds(first * half, GROUP * half)] = odd

    for off in range(1, RING):
        scatter(off).start()
    for plane in range(planes):
        halo2(plane, 0).start()
        halo2(plane, 1).start()
    for off in range(1, RING):
        scatter(off).wait()
    summed = share[spot]
    for off in range(1, RING):
        summed = summed + part[off - 1]
    mine[...] = summed
    for off in range(1, slabs):
        exchange(off).start()
    stack[slab] = summed
    for plane in range(planes):
        halo3(plane, 0).start()
        halo3(plane, 1).start()
    for off in range(1, slabs):
        exchange(off).wait()
    summed = stack[0]
    for other in range(1, slabs):
        summed = summed + stack[other]
    full[spot] = summed
    for off in range(1, RING):
        gather(off).start()
    square[...] = jnp.broadcast_to(jnp.sum(summed * summed), (8, 128))
    for off in range(1, lanes):
        lane_sum(off).start()

    @pl.when(lowest | highest)
    def _():
        for step in range(near):
            for to_lane in range(lanes):
                far_sum(step, to_lane).start()

    sums[layer] = square[...]
    for first in groups:
        wait_group(halo2, first)
    window(0)
    window(1)
    for off in range(1, depths):
        other = lax.rem(layer + off, depths)
        pltpu.make_async_remote_copy(
            sums.at[other], sums.at[other], s4.at[0], r4.at[other], device_id=at_lane(1), device_id_type=MESH
        ).wait_recv()
    squares = sums[0]
    for other in range(1, depths):
        squares = squares + sums[other]
    spot_sum[...] = squares
    for off in range(1, RING):
        spot_send(off).start()
    spots[spot] = squares
    for off in range(1, lanes):
        lane_sum(off).wait_send()

    @pl.when(lowest | highest)
    def _():
        for step in range(near):
            for to_lane in range(lanes):
                far_sum(step, to_lane).wait_send()

    for off in range(1, RING):
        gather(off).wait()
    gradient = jnp.concatenate([full[piece] for piece in range(RING)], axis=0)
    for first in groups:
        wait_group(halo3, first)
    for off in range(1, RING):
        spot_send(off).wait()
    squares = spots[0]
    for other in range(1, RING):
        squares = squares + spots[other]
    mean_square = squares[0:1] * (1.0 / (depths * PUP * PUP))
    new_phase = phase - STEP_SIZE * gradient / jnp.sqrt(mean_square + EPSILON)
    out_phase[...] = new_phase

    _, _, _, total, intensity = spread_of(new_phase)
    kernel_e, kernel_o = spectrum_of(intensity, total)
    twice_e, twice_o = stacked([kernel_e] * planes), stacked([kernel_o] * planes)
    for first in range(0, planes, planes):
        mates = range(first, first + planes)
        at = pl.ds(first * half, planes * half)
        ratios = []
        for which in range(2):
            blurs = back(times(spec_e[which, at], twice_e), times(spec_o[which, at], twice_o))
            ratios.append(
                [obs[plane, pl.ds(which * rows, rows)] / (blur + BACKGROUND) for plane, blur in zip(mates, blurs)]
            )
        even, odd = columns([mm(t["row_all"][...], above(one, two)) for one, two in zip(*ratios)])
        corrections = back(times_conj(even, twice_e), times_conj(odd, twice_o))
        for plane, correction in zip(mates, corrections):
            out_obj[plane] = big[plane, pl.ds(rows, rows)] * correction


def write_kernel(objects, phase, objects_out, phase_out, sem):
    one = pltpu.make_async_copy(objects, objects_out, sem.at[0])
    two = pltpu.make_async_copy(phase, phase_out, sem.at[1])
    one.start()
    two.start()
    one.wait()
    two.wait()


def on_device(objects, observed, pupil_phase, pupil_amplitude):
    tiles, depths = lax.axis_size("tile"), lax.axis_size("depth")
    _, planes, rows, cols = objects.shape
    span = rows + 2 * HALF
    half = span // 2
    table = tables(rows, cols)
    f32 = jnp.float32
    vmem = pltpu.VMEM
    dma = pltpu.SemaphoreType.DMA
    chunk = PUP // RING
    slabs = tiles // RING
    lanes = depths // SIDES
    body = lambda *refs: kernel(tiles, depths, planes, rows, cols, *refs)
    new_objects, new_phase = pl.pallas_call(
        body,
        out_shape=(
            jax.ShapeDtypeStruct((planes, rows, cols), f32),
            jax.ShapeDtypeStruct((PUP, PUP), f32),
        ),
        in_specs=[pl.BlockSpec(memory_space=pltpu.HBM)] * (4 + len(NAMES)),
        out_specs=(pl.BlockSpec(memory_space=vmem), pl.BlockSpec(memory_space=vmem)),
        scratch_shapes=[vmem(table[name].shape, f32) for name in NAMES]
        + [
            vmem((PUP, PUP), f32),
            vmem((PUP, PUP), f32),
            dma((4 + len(NAMES),)),
            vmem((cols, cols), f32),
            vmem((cols, cols), f32),
            vmem((planes, 3 * rows, cols), f32),
            vmem((planes, span, cols), f32),
            vmem((2, planes * half, cols), f32),
            vmem((2, planes * half, cols), f32),
            vmem((RING, chunk, PUP), f32),
            vmem((RING - 1, chunk, PUP), f32),
            vmem((chunk, PUP), f32),
            vmem((slabs, chunk, PUP), f32),
            vmem((RING, chunk, PUP), f32),
            vmem((8, 128), f32),
            vmem((depths, 8, 128), f32),
            vmem((RING, 8, 128), f32),
            vmem((8, 128), f32),
            dma((2 * planes,)), dma((2 * planes,)), dma((2 * planes,)), dma((2 * planes,)), dma((2 * planes,)), dma((2 * planes,)),
            dma((RING - 1,)), dma((RING - 1,)), dma((slabs - 1,)), dma((slabs - 1,)),
            dma((RING - 1,)), dma((RING - 1,)), dma((lanes - 1,)), dma((depths,)),
            dma((slabs // 2 * lanes,)), dma((RING - 1,)), dma((RING - 1,)),
        ],
        compiler_params=pltpu.CompilerParams(
            collective_id=0, has_side_effects=True, vmem_limit_bytes=48 * 1024 * 1024
        ),
        name="step",
    )(*[
        pltpu.with_memory_space_constraint(value, pltpu.HBM)
        for value in (objects[0], observed[0], pupil_phase[0], pupil_amplitude[0], *[table[name] for name in NAMES])
    ])
    new_objects, new_phase = pl.pallas_call(
        write_kernel,
        out_shape=(
            jax.ShapeDtypeStruct((planes, rows, cols), f32),
            jax.ShapeDtypeStruct((PUP, PUP), f32),
        ),
        in_specs=[pl.BlockSpec(memory_space=pl.ANY)] * 2,
        out_specs=(pl.BlockSpec(memory_space=pltpu.HBM), pl.BlockSpec(memory_space=pltpu.HBM)),
        scratch_shapes=[dma((2,))],
        name="write",
    )(*[pltpu.with_memory_space_constraint(value, vmem) for value in (new_objects, new_phase)])
    return new_objects[None], new_phase[None]


def solution(mesh):
    return jax.shard_map(
        on_device,
        mesh=mesh,
        in_specs=(
            P("depth", None, "tile", None),
            P("depth", None, "tile", None),
            P("depth", None, None),
            P("depth", None, None),
        ),
        out_specs=(P("depth", None, "tile", None), P("depth", None, None)),
        check_vma=False,
    )
```

```python
import math

import jax
import jax.numpy as jnp
import numpy as np
from jax import lax
from jax.experimental import pallas as pl
from jax.experimental.pallas import tpu as pltpu
from jax.sharding import PartitionSpec as P

HALF = 64
KER = 129
PUP = 128
PAD = 136
BACKGROUND = 0.1
STEP_SIZE = 0.3
EPSILON = 1e-06
RING = 8
SIDES = 2
GROUP = 2
MESH = pl.DeviceIdType.MESH


def real_form(matrix):
    return np.block([[matrix.real, matrix.imag], [-matrix.imag, matrix.real]])


def tables(rows, cols):
    span = rows + 2 * HALF
    half = span // 2
    omega = 2.0 * np.pi * (2.0 * np.arange(half) + 0.5) / span
    turn = np.exp(-1j * omega[:, None] * np.arange(span)[None, :])
    row_all = np.concatenate([turn.real, turn.imag])
    row_mid = row_all[:, HALF : HALF + rows]
    lag = np.exp(-1j * omega[:, None] * (np.arange(PAD) - HALF)[None, :]) * (np.arange(PAD) < KER)
    row_lag = np.concatenate([lag.real, lag.imag])
    part = cols // 2
    where = np.arange(part)
    even = np.exp(-2j * np.pi * where[:, None] * (2 * where)[None, :] / cols)
    odd = np.exp(-2j * np.pi * where[:, None] * (2 * where + 1)[None, :] / cols)
    outs = np.arange(cols)
    ring = np.exp(-2j * np.pi * (((outs - HALF)[:, None] * np.arange(PUP)[None, :]) % KER) / KER)
    ring = ring * (outs < KER)[:, None]
    left = np.concatenate([ring.real[:PAD], ring.imag[:PAD]])
    right = np.concatenate([ring.real.T, ring.imag.T])
    grid = np.arange(PUP) - (PUP - 1) / 2.0
    aperture = (grid[:, None] ** 2 + grid[None, :] ** 2 <= (PUP / 2.0) ** 2).astype(float)
    named = dict(
        row_all=row_all,
        row_mid=row_mid,
        row_back=row_mid.T * (2.0 / span / cols),
        row_lag=row_lag,
        row_lag_back=row_lag.T * (2.0 / span / cols),
        even=real_form(even),
        odd=real_form(odd),
        left=left,
        right=right,
        aperture=aperture,
    )
    return {name: np.ascontiguousarray(value, dtype=np.float32) for name, value in named.items()}


def mm(left, right):
    return jnp.dot(left, right, precision=lax.Precision.HIGH, preferred_element_type=jnp.float32)


def sin_cos(angle):
    count = jnp.floor(angle * (2.0 / math.pi) + 0.5)
    rest = angle - count * 1.5703125
    rest = rest - count * 4.8375129699707031e-4
    rest = rest - count * 7.549789954891882e-8
    square = rest * rest
    sine = ((-1.9515295891e-4 * square + 8.3321608736e-3) * square - 1.6666654611e-1) * square * rest + rest
    cosine = (
        (2.443315711809948e-5 * square - 1.388731625493765e-3) * square + 4.166664568298827e-2
    ) * square * square - 0.5 * square + 1.0
    quarter = count - 4.0 * jnp.floor(count * 0.25)
    swap = (quarter == 1.0) | (quarter == 3.0)
    sin_out = jnp.where(swap, cosine, sine)
    cos_out = jnp.where(swap, sine, cosine)
    sin_out = jnp.where(quarter >= 2.0, -sin_out, sin_out)
    cos_out = jnp.where((quarter == 1.0) | (quarter == 2.0), -cos_out, cos_out)
    return sin_out, cos_out


def beside(one, two):
    return jnp.concatenate([one, two], axis=1)


def above(one, two):
    return jnp.concatenate([one, two], axis=0)


def split_cols(rowed):
    half = rowed.shape[0] // 2
    part = rowed.shape[1] // 2
    plus = rowed[:, :part] + rowed[:, part:]
    minus = rowed[:, :part] - rowed[:, part:]
    return beside(plus[:half], plus[half:]), beside(minus[:half], minus[half:])


def join_cols(even, odd):
    part = even.shape[1] // 2
    plus = even + odd
    minus = even - odd
    return above(
        beside(plus[:, :part], minus[:, :part]),
        beside(plus[:, part:], minus[:, part:]),
    )


def stacked(values):
    return values[0] if len(values) == 1 else jnp.concatenate(values, axis=0)


def summed_over(value, rows):
    total = value[:rows]
    for at in range(rows, value.shape[0], rows):
        total = total + value[at : at + rows]
    return total


def times(one, two):
    part = one.shape[1] // 2
    ar, ai, br, bi = one[:, :part], one[:, part:], two[:, :part], two[:, part:]
    return beside(ar * br - ai * bi, ar * bi + ai * br)


def times_conj(one, two):
    part = one.shape[1] // 2
    ar, ai, br, bi = one[:, :part], one[:, part:], two[:, :part], two[:, part:]
    return beside(ar * br + ai * bi, ai * br - ar * bi)


NAMES = ("aperture", "left", "right", "row_lag", "row_all", "even", "odd", "row_back", "row_mid", "row_lag_back")
EARLY = ("left", "right", "phase", "amp", "aperture", "obj")


def kernel(tiles, depths, planes, rows, cols, *refs):
    count = len(NAMES)
    obj_in, obs_in, phase_in, amp_in = refs[:4]
    table_in = refs[4 : 4 + count]
    out_obj, out_phase = refs[4 + count : 6 + count]
    t = dict(zip(NAMES, refs[6 + count : 6 + 2 * count]))
    (
        phase_ref, amp_ref, load_sem, left_full, right_full, even_back, odd_back, big, obs, spec_e, spec_o,
        share, part, mine, stack, full, square, sums, spots, spot_sum,
        h1s, h1r, h2s, h2r, h3s, h3r, s1, r1, s2, r2, s3, r3, s4, r4, s5, s6, r6,
    ) = refs[6 + 2 * count :]
    me = lax.axis_index("tile")
    layer = lax.axis_index("depth")
    span = rows + 2 * HALF
    half = span // 2
    slabs = tiles // RING
    slab, spot = me // RING, lax.rem(me, RING)
    lanes = depths // SIDES
    side, lane = layer // lanes, lax.rem(layer, lanes)
    lowest, highest = slab == 0, slab == slabs - 1
    near = slabs // 2
    source_slab = jnp.where(slab < near, slabs - 1, 0)

    def at_tile(tile):
        return {"tile": tile, "depth": layer}

    def at_spot(off):
        return at_tile(slab * RING + lax.rem(spot + off, RING))

    def at_slab(off):
        return at_tile(lax.rem(slab + off, slabs) * RING + spot)

    def at_lane(off):
        return {"tile": me, "depth": side * lanes + lax.rem(lane + off, lanes)}

    def across(to_slab, to_lane):
        return {"tile": to_slab * RING + spot, "depth": (SIDES - 1 - side) * lanes + to_lane}

    barrier = pltpu.get_barrier_semaphore()

    def greet(device):
        pl.semaphore_signal(barrier, 1, device_id=device, device_id_type=MESH)

    for to_lane in range(lanes):
        greet(across(source_slab, to_lane))
    greet(at_tile(lax.rem(me + 1, tiles)))
    greet(at_tile(lax.rem(me + tiles - 1, tiles)))
    for off in range(1, slabs):
        greet(at_slab(off))
    for off in range(1, lanes):
        greet(at_lane(off))
    for off in range(1, RING):
        greet(at_spot(off))
    near_sends = jnp.where(lowest | highest, near * lanes, 0)
    greeted = 2 + RING - 1 + slabs - 1 + lanes - 1 + near_sends

    loads = {"phase": pltpu.make_async_copy(phase_in, phase_ref, load_sem.at[0])}
    loads["amp"] = pltpu.make_async_copy(amp_in, amp_ref, load_sem.at[1])
    loads["obj"] = pltpu.make_async_copy(obj_in, big.at[:, pl.ds(rows, rows)], load_sem.at[2])
    loads["obs"] = pltpu.make_async_copy(obs_in, obs.at[:, pl.ds(HALF, rows)], load_sem.at[3])
    for index, name in enumerate(NAMES):
        loads[name] = pltpu.make_async_copy(table_in[index], t[name], load_sem.at[4 + index])
    for name in EARLY:
        loads[name].start()
    for name in loads:
        if name not in EARLY:
            loads[name].start()

    def ready(*names):
        for name in names:
            loads[name].wait()

    def halo(buffer, first, mine_from, theirs_to, sends, recvs, plane, direction):
        peer = lax.rem(me + (1 if direction == 0 else tiles - 1), tiles)
        slot = 2 * plane + direction
        return pltpu.make_async_remote_copy(
            buffer.at[plane, pl.ds(first + mine_from, HALF)], buffer.at[plane, pl.ds(first + theirs_to, HALF)],
            sends.at[slot], recvs.at[slot], device_id=at_tile(peer), device_id_type=MESH,
        )

    def halo1(plane, direction):
        return halo(big, rows, *((rows - HALF, -HALF) if direction == 0 else (0, rows)), h1s, h1r, plane, direction)

    def halo2(plane, direction):
        return halo(big, rows, *((0, -rows) if direction == 0 else (HALF, rows + HALF)), h2s, h2r, plane, direction)

    def halo3(plane, direction):
        return halo(obs, HALF, *((rows - HALF, -HALF) if direction == 0 else (0, rows)), h3s, h3r, plane, direction)

    def build_pupil():
        real, imag = t["left"][:PAD], t["left"][PAD:]
        left_full[...] = above(beside(real, -imag), beside(imag, real))
        real, imag = t["right"][:PUP], t["right"][PUP:]
        right_full[...] = above(beside(real, imag), beside(-imag, real))

    def spread_of(angle):
        sine, cosine = sin_cos(angle)
        weight = amp_ref[...] * t["aperture"][...]
        field = above(weight * cosine, weight * sine)
        lefts = mm(left_full[...], field)
        outer = mm(beside(lefts[:PAD], lefts[PAD:]), right_full[...])
        real, imag = outer[:, :cols], outer[:, cols:]
        intensity = real * real + imag * imag
        total = jnp.sum(intensity)
        return field, real, imag, total, intensity

    part_cols = cols // 2
    column = lax.broadcasted_iota(jnp.int32, (1, part_cols), 1)
    flip = 1.0 - 2.0 * lax.rem(column, 2).astype(jnp.float32)
    flips = beside(flip, flip)
    turn_on = beside(-flip, flip)
    turn_off = beside(flip, -flip)

    def swapped(value):
        return beside(value[:, part_cols:], value[:, :part_cols])

    def spectrum_of(intensity, total):
        even, odd = split_cols(mm(t["row_lag"][...], intensity))
        share_of = 1.0 / total
        return (
            mm(even, t["even"][...]) * (flips * share_of),
            swapped(mm(odd, t["odd"][...])) * (turn_on * share_of),
        )

    def columns(rowed):
        pairs = [split_cols(value) for value in rowed]
        return (
            mm(stacked([even for even, _ in pairs]), t["even"][...]),
            mm(stacked([odd for _, odd in pairs]), t["odd"][...]),
        )

    def back(even, odd):
        even, odd = mm(even, even_back[...]), mm(odd, odd_back[...])
        return [
            mm(t["row_back"][...], join_cols(even[at : at + half], odd[at : at + half]))
            for at in range(0, even.shape[0], half)
        ]

    def twice(value):
        return stacked([value] * GROUP)

    groups = range(0, planes, GROUP)

    def wait_group(halo_of, first):
        for plane in range(first, first + GROUP):
            halo_of(plane, 0).wait()
            halo_of(plane, 1).wait()

    ready("left", "right")
    build_pupil()
    ready("phase", "amp", "aperture")
    phase = phase_ref[...]
    field, real, imag, total, intensity = spread_of(phase)
    ready("obj")
    pl.semaphore_wait(barrier, greeted)
    for plane in range(planes):
        halo1(plane, 0).start()
        halo1(plane, 1).start()
    ready(*[name for name in loads if name not in EARLY])
    even_back[...] = t["even"][...].T
    odd_back[...] = t["odd"][...].T
    kernel_e, kernel_o = spectrum_of(intensity, total)

    cross_e = jnp.zeros((half, cols), jnp.float32)
    cross_o = jnp.zeros((half, cols), jnp.float32)
    for first in groups:
        wait_group(halo1, first)
        mates = range(first, first + GROUP)
        even, odd = columns([mm(t["row_all"][...], big[plane, pl.ds(HALF, span)]) for plane in mates])
        blurs = back(times(even, twice(kernel_e)), times(odd, twice(kernel_o)))
        misfits = [1.0 - obs[plane, pl.ds(HALF, rows)] / (blur + BACKGROUND) for plane, blur in zip(mates, blurs)]
        mis_e, mis_o = columns([mm(t["row_mid"][...], misfit) for misfit in misfits])
        cross_e = cross_e + summed_over(times_conj(mis_e, even), half)
        cross_o = cross_o + summed_over(times_conj(mis_o, odd), half)
    lagged = join_cols(mm(cross_e * flips, even_back[...]), mm(swapped(cross_o) * turn_off, odd_back[...]))
    psf_grad = mm(t["row_lag_back"][...], lagged)

    scale = 2.0 / total
    centred = (psf_grad - jnp.sum(psf_grad * intensity) / total) * scale
    rest = jnp.zeros((cols - PAD, cols), jnp.float32)
    right = right_full[...]
    lefts = mm(right, jnp.concatenate([centred * real, rest, centred * imag, rest], axis=0))
    pupils = lax.dot_general(
        beside(lefts[:PUP], lefts[PUP:]), right, (((1,), (1,)), ((), ())),
        precision=lax.Precision.HIGH, preferred_element_type=jnp.float32,
    )
    mygrad = field[:PUP] * pupils[:, PUP:] - field[PUP:] * pupils[:, :PUP]

    chunk = PUP // RING
    for piece in range(RING):
        share[piece] = mygrad[piece * chunk : (piece + 1) * chunk]

    def scatter(off):
        return pltpu.make_async_remote_copy(
            share.at[lax.rem(spot + off, RING)], part.at[off - 1], s1.at[off - 1], r1.at[off - 1],
            device_id=at_spot(off), device_id_type=MESH,
        )

    def exchange(off):
        return pltpu.make_async_remote_copy(
            mine, stack.at[slab], s2.at[off - 1], r2.at[off - 1],
            device_id=at_slab(off), device_id_type=MESH,
        )

    def gather(off):
        return pltpu.make_async_remote_copy(
            full.at[spot], full.at[spot], s3.at[off - 1], r3.at[off - 1],
            device_id=at_spot(off), device_id_type=MESH,
        )

    def lane_sum(off):
        return pltpu.make_async_remote_copy(
            square, sums.at[layer], s4.at[off - 1], r4.at[layer],
            device_id=at_lane(off), device_id_type=MESH,
        )

    def far_sum(step, to_lane):
        return pltpu.make_async_remote_copy(
            square, sums.at[layer], s5.at[step * lanes + to_lane], r4.at[layer],
            device_id=across(jnp.where(lowest, near, 0) + step, to_lane), device_id_type=MESH,
        )

    def spot_send(off):
        return pltpu.make_async_remote_copy(
            spot_sum, spots.at[spot], s6.at[off - 1], r6.at[off - 1],
            device_id=at_spot(off), device_id_type=MESH,
        )

    def window(which):
        for first in groups:
            even, odd = columns(
                [mm(t["row_all"][...], big[plane, pl.ds(which * rows, span)]) for plane in range(first, first + GROUP)]
            )
            spec_e[which, pl.ds(first * half, GROUP * half)] = even
            spec_o[which, pl.ds(first * half, GROUP * half)] = odd

    for off in range(1, RING):
        scatter(off).start()
    for plane in range(planes):
        halo2(plane, 0).start()
        halo2(plane, 1).start()
    for off in range(1, RING):
        scatter(off).wait()
    summed = share[spot]
    for off in range(1, RING):
        summed = summed + part[off - 1]
    mine[...] = summed
    for off in range(1, slabs):
        exchange(off).start()
    stack[slab] = summed
    for plane in range(planes):
        halo3(plane, 0).start()
        halo3(plane, 1).start()
    for off in range(1, slabs):
        exchange(off).wait()
    summed = stack[0]
    for other in range(1, slabs):
        summed = summed + stack[other]
    full[spot] = summed
    for off in range(1, RING):
        gather(off).start()
    square[...] = jnp.broadcast_to(jnp.sum(summed * summed), (1, 128))
    for off in range(1, lanes):
        lane_sum(off).start()

    @pl.when(lowest | highest)
    def _():
        for step in range(near):
            for to_lane in range(lanes):
                far_sum(step, to_lane).start()

    sums[layer] = square[...]
    for first in groups:
        wait_group(halo2, first)
    window(0)
    window(1)
    for off in range(1, depths):
        other = lax.rem(layer + off, depths)
        pltpu.make_async_remote_copy(
            sums.at[other], sums.at[other], s4.at[0], r4.at[other], device_id=at_lane(1), device_id_type=MESH
        ).wait_recv()
    squares = sums[0]
    for other in range(1, depths):
        squares = squares + sums[other]
    spot_sum[...] = squares
    for off in range(1, RING):
        spot_send(off).start()
    spots[spot] = squares
    for off in range(1, lanes):
        lane_sum(off).wait_send()

    @pl.when(lowest | highest)
    def _():
        for step in range(near):
            for to_lane in range(lanes):
                far_sum(step, to_lane).wait_send()

    for off in range(1, RING):
        gather(off).wait()
    gradient = jnp.concatenate([full[piece] for piece in range(RING)], axis=0)
    for first in groups:
        wait_group(halo3, first)
    for off in range(1, RING):
        spot_send(off).wait()
    squares = spots[0]
    for other in range(1, RING):
        squares = squares + spots[other]
    mean_square = squares * (1.0 / (depths * PUP * PUP))
    new_phase = phase - STEP_SIZE * gradient / jnp.sqrt(mean_square + EPSILON)
    out_phase[...] = new_phase

    _, _, _, total, intensity = spread_of(new_phase)
    kernel_e, kernel_o = spectrum_of(intensity, total)
    twice_e, twice_o = stacked([kernel_e] * planes), stacked([kernel_o] * planes)
    for first in range(0, planes, planes):
        mates = range(first, first + planes)
        at = pl.ds(first * half, planes * half)
        ratios = []
        for which in range(2):
            blurs = back(times(spec_e[which, at], twice_e), times(spec_o[which, at], twice_o))
            ratios.append(
                [obs[plane, pl.ds(which * rows, rows)] / (blur + BACKGROUND) for plane, blur in zip(mates, blurs)]
            )
        even, odd = columns([mm(t["row_all"][...], above(one, two)) for one, two in zip(*ratios)])
        corrections = back(times_conj(even, twice_e), times_conj(odd, twice_o))
        for plane, correction in zip(mates, corrections):
            out_obj[plane] = big[plane, pl.ds(rows, rows)] * correction


def write_kernel(objects, phase, objects_out, phase_out, sem):
    one = pltpu.make_async_copy(objects, objects_out, sem.at[0])
    two = pltpu.make_async_copy(phase, phase_out, sem.at[1])
    one.start()
    two.start()
    one.wait()
    two.wait()


def on_device(objects, observed, pupil_phase, pupil_amplitude):
    tiles, depths = lax.axis_size("tile"), lax.axis_size("depth")
    _, planes, rows, cols = objects.shape
    span = rows + 2 * HALF
    half = span // 2
    table = tables(rows, cols)
    f32 = jnp.float32
    vmem = pltpu.VMEM
    dma = pltpu.SemaphoreType.DMA
    chunk = PUP // RING
    slabs = tiles // RING
    lanes = depths // SIDES
    body = lambda *refs: kernel(tiles, depths, planes, rows, cols, *refs)
    new_objects, new_phase = pl.pallas_call(
        body,
        out_shape=(
            jax.ShapeDtypeStruct((planes, rows, cols), f32),
            jax.ShapeDtypeStruct((PUP, PUP), f32),
        ),
        in_specs=[pl.BlockSpec(memory_space=pltpu.HBM)] * (4 + len(NAMES)),
        out_specs=(pl.BlockSpec(memory_space=vmem), pl.BlockSpec(memory_space=vmem)),
        scratch_shapes=[vmem(table[name].shape, f32) for name in NAMES]
        + [
            vmem((PUP, PUP), f32),
            vmem((PUP, PUP), f32),
            dma((4 + len(NAMES),)),
            vmem((2 * PAD, 2 * PUP), f32),
            vmem((2 * PUP, 2 * cols), f32),
            vmem((cols, cols), f32),
            vmem((cols, cols), f32),
            vmem((planes, 3 * rows, cols), f32),
            vmem((planes, span, cols), f32),
            vmem((2, planes * half, cols), f32),
            vmem((2, planes * half, cols), f32),
            vmem((RING, chunk, PUP), f32),
            vmem((RING - 1, chunk, PUP), f32),
            vmem((chunk, PUP), f32),
            vmem((slabs, chunk, PUP), f32),
            vmem((RING, chunk, PUP), f32),
            vmem((1, 128), f32),
            vmem((depths, 1, 128), f32),
            vmem((RING, 1, 128), f32),
            vmem((1, 128), f32),
            dma((2 * planes,)), dma((2 * planes,)), dma((2 * planes,)), dma((2 * planes,)), dma((2 * planes,)), dma((2 * planes,)),
            dma((RING - 1,)), dma((RING - 1,)), dma((slabs - 1,)), dma((slabs - 1,)),
            dma((RING - 1,)), dma((RING - 1,)), dma((lanes - 1,)), dma((depths,)),
            dma((slabs // 2 * lanes,)), dma((RING - 1,)), dma((RING - 1,)),
        ],
        compiler_params=pltpu.CompilerParams(
            collective_id=0, has_side_effects=True, vmem_limit_bytes=48 * 1024 * 1024
        ),
        name="step",
    )(*[
        pltpu.with_memory_space_constraint(value, pltpu.HBM)
        for value in (objects[0], observed[0], pupil_phase[0], pupil_amplitude[0], *[table[name] for name in NAMES])
    ])
    new_objects, new_phase = pl.pallas_call(
        write_kernel,
        out_shape=(
            jax.ShapeDtypeStruct((planes, rows, cols), f32),
            jax.ShapeDtypeStruct((PUP, PUP), f32),
        ),
        in_specs=[pl.BlockSpec(memory_space=pl.ANY)] * 2,
        out_specs=(pl.BlockSpec(memory_space=pltpu.HBM), pl.BlockSpec(memory_space=pltpu.HBM)),
        scratch_shapes=[dma((2,))],
        name="write",
    )(*[pltpu.with_memory_space_constraint(value, vmem) for value in (new_objects, new_phase)])
    return new_objects[None], new_phase[None]


def solution(mesh):
    return jax.shard_map(
        on_device,
        mesh=mesh,
        in_specs=(
            P("depth", None, "tile", None),
            P("depth", None, "tile", None),
            P("depth", None, None),
            P("depth", None, None),
        ),
        out_specs=(P("depth", None, "tile", None), P("depth", None, None)),
        check_vma=False,
    )
```

```python
import math

import jax
import jax.numpy as jnp
import numpy as np
from jax import lax
from jax.experimental import pallas as pl
from jax.experimental.pallas import tpu as pltpu
from jax.sharding import PartitionSpec as P

HALF = 64
KER = 129
PUP = 128
PAD = 136
BACKGROUND = 0.1
STEP_SIZE = 0.3
EPSILON = 1e-06
RING = 8
SIDES = 2
GROUP = 2
MESH = pl.DeviceIdType.MESH


def real_form(matrix):
    return np.block([[matrix.real, matrix.imag], [-matrix.imag, matrix.real]])


def tables(rows, cols):
    span = rows + 2 * HALF
    half = span // 2
    omega = 2.0 * np.pi * (2.0 * np.arange(half) + 0.5) / span
    turn = np.exp(-1j * omega[:, None] * np.arange(span)[None, :])
    row_all = np.concatenate([turn.real, turn.imag])
    row_mid = row_all[:, HALF : HALF + rows]
    lag = np.exp(-1j * omega[:, None] * (np.arange(PAD) - HALF)[None, :]) * (np.arange(PAD) < KER)
    row_lag = np.concatenate([lag.real, lag.imag])
    part = cols // 2
    where = np.arange(part)
    even = np.exp(-2j * np.pi * where[:, None] * (2 * where)[None, :] / cols)
    odd = np.exp(-2j * np.pi * where[:, None] * (2 * where + 1)[None, :] / cols)
    outs = np.arange(cols)
    ring = np.exp(-2j * np.pi * (((outs - HALF)[:, None] * np.arange(PUP)[None, :]) % KER) / KER)
    ring = ring * (outs < KER)[:, None]
    left = np.concatenate([ring.real[:PAD], ring.imag[:PAD]])
    right = np.concatenate([ring.real.T, ring.imag.T])
    grid = np.arange(PUP) - (PUP - 1) / 2.0
    aperture = (grid[:, None] ** 2 + grid[None, :] ** 2 <= (PUP / 2.0) ** 2).astype(float)
    named = dict(
        row_all=row_all,
        row_mid=row_mid,
        row_back=row_mid.T * (2.0 / span / cols),
        row_lag=row_lag,
        row_lag_back=row_lag.T * (2.0 / span / cols),
        even=real_form(even),
        odd=real_form(odd),
        left=left,
        right=right,
        aperture=aperture,
    )
    return {name: np.ascontiguousarray(value, dtype=np.float32) for name, value in named.items()}


def mm(left, right):
    return jnp.dot(left, right, precision=lax.Precision.HIGH, preferred_element_type=jnp.float32)


def sin_cos(angle):
    count = jnp.floor(angle * (2.0 / math.pi) + 0.5)
    rest = angle - count * 1.5703125
    rest = rest - count * 4.8375129699707031e-4
    rest = rest - count * 7.549789954891882e-8
    square = rest * rest
    sine = ((-1.9515295891e-4 * square + 8.3321608736e-3) * square - 1.6666654611e-1) * square * rest + rest
    cosine = (
        (2.443315711809948e-5 * square - 1.388731625493765e-3) * square + 4.166664568298827e-2
    ) * square * square - 0.5 * square + 1.0
    quarter = count - 4.0 * jnp.floor(count * 0.25)
    swap = (quarter == 1.0) | (quarter == 3.0)
    sin_out = jnp.where(swap, cosine, sine)
    cos_out = jnp.where(swap, sine, cosine)
    sin_out = jnp.where(quarter >= 2.0, -sin_out, sin_out)
    cos_out = jnp.where((quarter == 1.0) | (quarter == 2.0), -cos_out, cos_out)
    return sin_out, cos_out


def beside(one, two):
    return jnp.concatenate([one, two], axis=1)


def above(one, two):
    return jnp.concatenate([one, two], axis=0)


def split_cols(rowed):
    half = rowed.shape[0] // 2
    part = rowed.shape[1] // 2
    plus = rowed[:, :part] + rowed[:, part:]
    minus = rowed[:, :part] - rowed[:, part:]
    return beside(plus[:half], plus[half:]), beside(minus[:half], minus[half:])


def join_cols(even, odd):
    part = even.shape[1] // 2
    plus = even + odd
    minus = even - odd
    return above(
        beside(plus[:, :part], minus[:, :part]),
        beside(plus[:, part:], minus[:, part:]),
    )


def stacked(values):
    return values[0] if len(values) == 1 else jnp.concatenate(values, axis=0)


def summed_over(value, rows):
    total = value[:rows]
    for at in range(rows, value.shape[0], rows):
        total = total + value[at : at + rows]
    return total


def times(one, two):
    part = one.shape[1] // 2
    ar, ai, br, bi = one[:, :part], one[:, part:], two[:, :part], two[:, part:]
    return beside(ar * br - ai * bi, ar * bi + ai * br)


def times_conj(one, two):
    part = one.shape[1] // 2
    ar, ai, br, bi = one[:, :part], one[:, part:], two[:, :part], two[:, part:]
    return beside(ar * br + ai * bi, ai * br - ar * bi)


NAMES = ("aperture", "left", "right", "row_lag", "row_all", "even", "odd", "row_back", "row_mid", "row_lag_back")
EARLY = ("left", "right", "phase", "amp", "aperture", "obj")


def kernel(tiles, depths, planes, rows, cols, *refs):
    count = len(NAMES)
    obj_in, obs_in, phase_in, amp_in = refs[:4]
    table_in = refs[4 : 4 + count]
    out_obj, out_phase = refs[4 + count : 6 + count]
    t = dict(zip(NAMES, refs[6 + count : 6 + 2 * count]))
    (
        phase_ref, amp_ref, load_sem, left_full, right_full, even_back, odd_back, big, obs, spec_e, spec_o,
        share, part, mine, stack, full, square, sums, spots, spot_sum,
        h1s, h1r, h2s, h2r, h3s, h3r, s1, r1, s2, r2, s3, r3, s4, r4, s5, s6, r6,
    ) = refs[6 + 2 * count :]
    me = lax.axis_index("tile")
    layer = lax.axis_index("depth")
    span = rows + 2 * HALF
    half = span // 2
    slabs = tiles // RING
    slab, spot = me // RING, lax.rem(me, RING)
    lanes = depths // SIDES
    side, lane = layer // lanes, lax.rem(layer, lanes)
    lowest, highest = slab == 0, slab == slabs - 1
    near = slabs // 2
    source_slab = jnp.where(slab < near, slabs - 1, 0)

    def at_tile(tile):
        return {"tile": tile, "depth": layer}

    def at_spot(off):
        return at_tile(slab * RING + lax.rem(spot + off, RING))

    def at_slab(off):
        return at_tile(lax.rem(slab + off, slabs) * RING + spot)

    def at_lane(off):
        return {"tile": me, "depth": side * lanes + lax.rem(lane + off, lanes)}

    def across(to_slab, to_lane):
        return {"tile": to_slab * RING + spot, "depth": (SIDES - 1 - side) * lanes + to_lane}

    barrier = pltpu.get_barrier_semaphore()

    def greet(device):
        pl.semaphore_signal(barrier, 1, device_id=device, device_id_type=MESH)

    for to_lane in range(lanes):
        greet(across(source_slab, to_lane))
    greet(at_tile(lax.rem(me + 1, tiles)))
    greet(at_tile(lax.rem(me + tiles - 1, tiles)))
    for off in range(1, slabs):
        greet(at_slab(off))
    for off in range(1, lanes):
        greet(at_lane(off))
    for off in range(1, RING):
        greet(at_spot(off))
    near_sends = jnp.where(lowest | highest, near * lanes, 0)
    greeted = 2 + RING - 1 + slabs - 1 + lanes - 1 + near_sends

    loads = {"phase": pltpu.make_async_copy(phase_in, phase_ref, load_sem.at[0])}
    loads["amp"] = pltpu.make_async_copy(amp_in, amp_ref, load_sem.at[1])
    loads["obj"] = pltpu.make_async_copy(obj_in, big.at[:, pl.ds(rows, rows)], load_sem.at[2])
    loads["obs"] = pltpu.make_async_copy(obs_in, obs.at[:, pl.ds(HALF, rows)], load_sem.at[3])
    for index, name in enumerate(NAMES):
        loads[name] = pltpu.make_async_copy(table_in[index], t[name], load_sem.at[4 + index])
    for name in EARLY:
        loads[name].start()
    for name in loads:
        if name not in EARLY:
            loads[name].start()

    def ready(*names):
        for name in names:
            loads[name].wait()

    def halo(buffer, first, mine_from, theirs_to, sends, recvs, plane, direction):
        peer = lax.rem(me + (1 if direction == 0 else tiles - 1), tiles)
        slot = 2 * plane + direction
        return pltpu.make_async_remote_copy(
            buffer.at[plane, pl.ds(first + mine_from, HALF)], buffer.at[plane, pl.ds(first + theirs_to, HALF)],
            sends.at[slot], recvs.at[slot], device_id=at_tile(peer), device_id_type=MESH,
        )

    def halo1(plane, direction):
        return halo(big, rows, *((rows - HALF, -HALF) if direction == 0 else (0, rows)), h1s, h1r, plane, direction)

    def halo2(plane, direction):
        return halo(big, rows, *((0, -rows) if direction == 0 else (HALF, rows + HALF)), h2s, h2r, plane, direction)

    def halo3(plane, direction):
        return halo(obs, HALF, *((rows - HALF, -HALF) if direction == 0 else (0, rows)), h3s, h3r, plane, direction)

    def build_pupil():
        real, imag = t["left"][:PAD], t["left"][PAD:]
        left_full[...] = above(beside(real, -imag), beside(imag, real))
        real, imag = t["right"][:PUP], t["right"][PUP:]
        right_full[...] = above(beside(real, imag), beside(-imag, real))

    def spread_of(angle):
        sine, cosine = sin_cos(angle)
        weight = amp_ref[...] * t["aperture"][...]
        field = above(weight * cosine, weight * sine)
        lefts = mm(left_full[...], field)
        outer = mm(beside(lefts[:PAD], lefts[PAD:]), right_full[...])
        real, imag = outer[:, :cols], outer[:, cols:]
        intensity = real * real + imag * imag
        total = jnp.sum(intensity)
        return field, real, imag, total, intensity

    part_cols = cols // 2
    column = lax.broadcasted_iota(jnp.int32, (1, part_cols), 1)
    flip = 1.0 - 2.0 * lax.rem(column, 2).astype(jnp.float32)
    flips = beside(flip, flip)
    turn_on = beside(-flip, flip)
    turn_off = beside(flip, -flip)

    def swapped(value):
        return beside(value[:, part_cols:], value[:, :part_cols])

    def spectrum_of(intensity, total):
        even, odd = split_cols(mm(t["row_lag"][...], intensity))
        share_of = 1.0 / total
        return (
            mm(even, t["even"][...]) * (flips * share_of),
            swapped(mm(odd, t["odd"][...])) * (turn_on * share_of),
        )

    def columns(rowed):
        pairs = [split_cols(value) for value in rowed]
        return (
            mm(stacked([even for even, _ in pairs]), t["even"][...]),
            mm(stacked([odd for _, odd in pairs]), t["odd"][...]),
        )

    def back(even, odd):
        even, odd = mm(even, even_back[...]), mm(odd, odd_back[...])
        return [
            mm(t["row_back"][...], join_cols(even[at : at + half], odd[at : at + half]))
            for at in range(0, even.shape[0], half)
        ]

    def twice(value):
        return stacked([value] * GROUP)

    groups = range(0, planes, GROUP)

    def wait_group(halo_of, first):
        for plane in range(first, first + GROUP):
            halo_of(plane, 0).wait()
            halo_of(plane, 1).wait()

    ready("left", "right")
    build_pupil()
    ready("phase", "amp", "aperture")
    phase = phase_ref[...]
    field, real, imag, total, intensity = spread_of(phase)
    ready("obj")
    pl.semaphore_wait(barrier, greeted)
    for plane in range(planes):
        halo1(plane, 0).start()
        halo1(plane, 1).start()
    ready(*[name for name in loads if name not in EARLY])
    even_back[...] = t["even"][...].T
    odd_back[...] = t["odd"][...].T
    kernel_e, kernel_o = spectrum_of(intensity, total)

    cross_e = jnp.zeros((half, cols), jnp.float32)
    cross_o = jnp.zeros((half, cols), jnp.float32)
    for first in groups:
        wait_group(halo1, first)
        mates = range(first, first + GROUP)
        even, odd = columns([mm(t["row_all"][...], big[plane, pl.ds(HALF, span)]) for plane in mates])
        blurs = back(times(even, twice(kernel_e)), times(odd, twice(kernel_o)))
        misfits = [1.0 - obs[plane, pl.ds(HALF, rows)] / (blur + BACKGROUND) for plane, blur in zip(mates, blurs)]
        mis_e, mis_o = columns([mm(t["row_mid"][...], misfit) for misfit in misfits])
        cross_e = cross_e + summed_over(times_conj(mis_e, even), half)
        cross_o = cross_o + summed_over(times_conj(mis_o, odd), half)
    lagged = join_cols(mm(cross_e * flips, even_back[...]), mm(swapped(cross_o) * turn_off, odd_back[...]))
    psf_grad = mm(t["row_lag_back"][...], lagged)

    scale = 2.0 / total
    centred = (psf_grad - jnp.sum(psf_grad * intensity) / total) * scale
    rest = jnp.zeros((cols - PAD, cols), jnp.float32)
    right = right_full[...]
    lefts = mm(right, jnp.concatenate([centred * real, rest, centred * imag, rest], axis=0))
    pupils = lax.dot_general(
        beside(lefts[:PUP], lefts[PUP:]), right, (((1,), (1,)), ((), ())),
        precision=lax.Precision.HIGH, preferred_element_type=jnp.float32,
    )
    mygrad = field[:PUP] * pupils[:, PUP:] - field[PUP:] * pupils[:, :PUP]

    chunk = PUP // RING
    for piece in range(RING):
        share[piece] = mygrad[piece * chunk : (piece + 1) * chunk]

    def scatter(off):
        return pltpu.make_async_remote_copy(
            share.at[lax.rem(spot + off, RING)], part.at[off - 1], s1.at[off - 1], r1.at[off - 1],
            device_id=at_spot(off), device_id_type=MESH,
        )

    def exchange(off):
        return pltpu.make_async_remote_copy(
            mine, stack.at[slab], s2.at[off - 1], r2.at[off - 1],
            device_id=at_slab(off), device_id_type=MESH,
        )

    def gather(off):
        return pltpu.make_async_remote_copy(
            full.at[spot], full.at[spot], s3.at[off - 1], r3.at[off - 1],
            device_id=at_spot(off), device_id_type=MESH,
        )

    def lane_sum(off):
        return pltpu.make_async_remote_copy(
            square, sums.at[layer], s4.at[off - 1], r4.at[layer],
            device_id=at_lane(off), device_id_type=MESH,
        )

    def far_sum(step, to_lane):
        return pltpu.make_async_remote_copy(
            square, sums.at[layer], s5.at[step * lanes + to_lane], r4.at[layer],
            device_id=across(jnp.where(lowest, near, 0) + step, to_lane), device_id_type=MESH,
        )

    def spot_send(off):
        return pltpu.make_async_remote_copy(
            spot_sum, spots.at[spot], s6.at[off - 1], r6.at[off - 1],
            device_id=at_spot(off), device_id_type=MESH,
        )

    def windows(first):
        wait_group(halo2, first)
        for which in range(2):
            even, odd = columns(
                [mm(t["row_all"][...], big[plane, pl.ds(which * rows, span)]) for plane in range(first, first + GROUP)]
            )
            spec_e[which, pl.ds(first * half, GROUP * half)] = even
            spec_o[which, pl.ds(first * half, GROUP * half)] = odd

    for off in range(1, RING):
        scatter(off).start()
    for off in range(1, RING):
        scatter(off).wait()
    summed = share[spot]
    for off in range(1, RING):
        summed = summed + part[off - 1]
    mine[...] = summed
    for off in range(1, slabs):
        exchange(off).start()
    stack[slab] = summed
    for plane in range(planes):
        halo2(plane, 0).start()
        halo2(plane, 1).start()
    for plane in range(planes):
        halo3(plane, 0).start()
        halo3(plane, 1).start()
    for off in range(1, slabs):
        exchange(off).wait()
    summed = stack[0]
    for other in range(1, slabs):
        summed = summed + stack[other]
    full[spot] = summed
    for off in range(1, RING):
        gather(off).start()
    square[...] = jnp.broadcast_to(jnp.sum(summed * summed), (1, 128))
    for off in range(1, lanes):
        lane_sum(off).start()

    @pl.when(lowest | highest)
    def _():
        for step in range(near):
            for to_lane in range(lanes):
                far_sum(step, to_lane).start()

    sums[layer] = square[...]
    windows(0)
    for off in range(1, depths):
        other = lax.rem(layer + off, depths)
        pltpu.make_async_remote_copy(
            sums.at[other], sums.at[other], s4.at[0], r4.at[other], device_id=at_lane(1), device_id_type=MESH
        ).wait_recv()
    squares = sums[0]
    for other in range(1, depths):
        squares = squares + sums[other]
    spot_sum[...] = squares
    for off in range(1, RING):
        spot_send(off).start()
    spots[spot] = squares
    for first in groups[1:]:
        windows(first)
    for off in range(1, lanes):
        lane_sum(off).wait_send()

    @pl.when(lowest | highest)
    def _():
        for step in range(near):
            for to_lane in range(lanes):
                far_sum(step, to_lane).wait_send()

    for off in range(1, RING):
        gather(off).wait()
    gradient = jnp.concatenate([full[piece] for piece in range(RING)], axis=0)
    for first in groups:
        wait_group(halo3, first)
    for off in range(1, RING):
        spot_send(off).wait()
    squares = spots[0]
    for other in range(1, RING):
        squares = squares + spots[other]
    mean_square = squares * (1.0 / (depths * PUP * PUP))
    new_phase = phase - STEP_SIZE * gradient / jnp.sqrt(mean_square + EPSILON)
    out_phase[...] = new_phase

    _, _, _, total, intensity = spread_of(new_phase)
    kernel_e, kernel_o = spectrum_of(intensity, total)
    twice_e, twice_o = stacked([kernel_e] * planes), stacked([kernel_o] * planes)
    for first in range(0, planes, planes):
        mates = range(first, first + planes)
        at = pl.ds(first * half, planes * half)
        ratios = []
        for which in range(2):
            blurs = back(times(spec_e[which, at], twice_e), times(spec_o[which, at], twice_o))
            ratios.append(
                [obs[plane, pl.ds(which * rows, rows)] / (blur + BACKGROUND) for plane, blur in zip(mates, blurs)]
            )
        even, odd = columns([mm(t["row_all"][...], above(one, two)) for one, two in zip(*ratios)])
        corrections = back(times_conj(even, twice_e), times_conj(odd, twice_o))
        for plane, correction in zip(mates, corrections):
            out_obj[plane] = big[plane, pl.ds(rows, rows)] * correction


def write_kernel(objects, phase, objects_out, phase_out, sem):
    one = pltpu.make_async_copy(objects, objects_out, sem.at[0])
    two = pltpu.make_async_copy(phase, phase_out, sem.at[1])
    one.start()
    two.start()
    one.wait()
    two.wait()


def on_device(objects, observed, pupil_phase, pupil_amplitude):
    tiles, depths = lax.axis_size("tile"), lax.axis_size("depth")
    _, planes, rows, cols = objects.shape
    span = rows + 2 * HALF
    half = span // 2
    table = tables(rows, cols)
    f32 = jnp.float32
    vmem = pltpu.VMEM
    dma = pltpu.SemaphoreType.DMA
    chunk = PUP // RING
    slabs = tiles // RING
    lanes = depths // SIDES
    body = lambda *refs: kernel(tiles, depths, planes, rows, cols, *refs)
    new_objects, new_phase = pl.pallas_call(
        body,
        out_shape=(
            jax.ShapeDtypeStruct((planes, rows, cols), f32),
            jax.ShapeDtypeStruct((PUP, PUP), f32),
        ),
        in_specs=[pl.BlockSpec(memory_space=pltpu.HBM)] * (4 + len(NAMES)),
        out_specs=(pl.BlockSpec(memory_space=vmem), pl.BlockSpec(memory_space=vmem)),
        scratch_shapes=[vmem(table[name].shape, f32) for name in NAMES]
        + [
            vmem((PUP, PUP), f32),
            vmem((PUP, PUP), f32),
            dma((4 + len(NAMES),)),
            vmem((2 * PAD, 2 * PUP), f32),
            vmem((2 * PUP, 2 * cols), f32),
            vmem((cols, cols), f32),
            vmem((cols, cols), f32),
            vmem((planes, 3 * rows, cols), f32),
            vmem((planes, span, cols), f32),
            vmem((2, planes * half, cols), f32),
            vmem((2, planes * half, cols), f32),
            vmem((RING, chunk, PUP), f32),
            vmem((RING - 1, chunk, PUP), f32),
            vmem((chunk, PUP), f32),
            vmem((slabs, chunk, PUP), f32),
            vmem((RING, chunk, PUP), f32),
            vmem((1, 128), f32),
            vmem((depths, 1, 128), f32),
            vmem((RING, 1, 128), f32),
            vmem((1, 128), f32),
            dma((2 * planes,)), dma((2 * planes,)), dma((2 * planes,)), dma((2 * planes,)), dma((2 * planes,)), dma((2 * planes,)),
            dma((RING - 1,)), dma((RING - 1,)), dma((slabs - 1,)), dma((slabs - 1,)),
            dma((RING - 1,)), dma((RING - 1,)), dma((lanes - 1,)), dma((depths,)),
            dma((slabs // 2 * lanes,)), dma((RING - 1,)), dma((RING - 1,)),
        ],
        compiler_params=pltpu.CompilerParams(
            collective_id=0, has_side_effects=True, vmem_limit_bytes=48 * 1024 * 1024
        ),
        name="step",
    )(*[
        pltpu.with_memory_space_constraint(value, pltpu.HBM)
        for value in (objects[0], observed[0], pupil_phase[0], pupil_amplitude[0], *[table[name] for name in NAMES])
    ])
    new_objects, new_phase = pl.pallas_call(
        write_kernel,
        out_shape=(
            jax.ShapeDtypeStruct((planes, rows, cols), f32),
            jax.ShapeDtypeStruct((PUP, PUP), f32),
        ),
        in_specs=[pl.BlockSpec(memory_space=pl.ANY)] * 2,
        out_specs=(pl.BlockSpec(memory_space=pltpu.HBM), pl.BlockSpec(memory_space=pltpu.HBM)),
        scratch_shapes=[dma((2,))],
        name="write",
    )(*[pltpu.with_memory_space_constraint(value, vmem) for value in (new_objects, new_phase)])
    return new_objects[None], new_phase[None]


def solution(mesh):
    return jax.shard_map(
        on_device,
        mesh=mesh,
        in_specs=(
            P("depth", None, "tile", None),
            P("depth", None, "tile", None),
            P("depth", None, None),
            P("depth", None, None),
        ),
        out_specs=(P("depth", None, "tile", None), P("depth", None, None)),
        check_vma=False,
    )
```

```python
import math

import jax
import jax.numpy as jnp
import numpy as np
from jax import lax
from jax.experimental import pallas as pl
from jax.experimental.pallas import tpu as pltpu
from jax.sharding import PartitionSpec as P

HALF = 64
KER = 129
PUP = 128
PAD = 136
BACKGROUND = 0.1
STEP_SIZE = 0.3
EPSILON = 1e-06
RING = 8
SIDES = 2
GROUP = 2
MESH = pl.DeviceIdType.MESH


def real_form(matrix):
    return np.block([[matrix.real, matrix.imag], [-matrix.imag, matrix.real]])


def tables(rows, cols):
    span = rows + 2 * HALF
    half = span // 2
    omega = 2.0 * np.pi * (2.0 * np.arange(half) + 0.5) / span
    turn = np.exp(-1j * omega[:, None] * np.arange(span)[None, :])
    row_all = np.concatenate([turn.real, turn.imag])
    row_mid = row_all[:, HALF : HALF + rows]
    lag = np.exp(-1j * omega[:, None] * (np.arange(PAD) - HALF)[None, :]) * (np.arange(PAD) < KER)
    row_lag = np.concatenate([lag.real, lag.imag])
    part = cols // 2
    where = np.arange(part)
    even = np.exp(-2j * np.pi * where[:, None] * (2 * where)[None, :] / cols)
    odd = np.exp(-2j * np.pi * where[:, None] * (2 * where + 1)[None, :] / cols)
    outs = np.arange(cols)
    ring = np.exp(-2j * np.pi * (((outs - HALF)[:, None] * np.arange(PUP)[None, :]) % KER) / KER)
    ring = ring * (outs < KER)[:, None]
    left = np.concatenate([ring.real[:PAD], ring.imag[:PAD]])
    right = np.concatenate([ring.real.T, ring.imag.T])
    grid = np.arange(PUP) - (PUP - 1) / 2.0
    aperture = (grid[:, None] ** 2 + grid[None, :] ** 2 <= (PUP / 2.0) ** 2).astype(float)
    named = dict(
        row_all=row_all,
        row_mid=row_mid,
        row_back=row_mid.T * (2.0 / span / cols),
        row_lag=row_lag,
        row_lag_back=row_lag.T * (2.0 / span / cols),
        even=real_form(even),
        odd=real_form(odd),
        left=left,
        right=right,
        aperture=aperture,
    )
    return {name: np.ascontiguousarray(value, dtype=np.float32) for name, value in named.items()}


def mm(left, right):
    return jnp.dot(left, right, precision=lax.Precision.HIGH, preferred_element_type=jnp.float32)


def sin_cos(angle):
    count = jnp.floor(angle * (2.0 / math.pi) + 0.5)
    rest = angle - count * 1.5703125
    rest = rest - count * 4.8375129699707031e-4
    rest = rest - count * 7.549789954891882e-8
    square = rest * rest
    sine = ((-1.9515295891e-4 * square + 8.3321608736e-3) * square - 1.6666654611e-1) * square * rest + rest
    cosine = (
        (2.443315711809948e-5 * square - 1.388731625493765e-3) * square + 4.166664568298827e-2
    ) * square * square - 0.5 * square + 1.0
    quarter = count - 4.0 * jnp.floor(count * 0.25)
    swap = (quarter == 1.0) | (quarter == 3.0)
    sin_out = jnp.where(swap, cosine, sine)
    cos_out = jnp.where(swap, sine, cosine)
    sin_out = jnp.where(quarter >= 2.0, -sin_out, sin_out)
    cos_out = jnp.where((quarter == 1.0) | (quarter == 2.0), -cos_out, cos_out)
    return sin_out, cos_out


def beside(one, two):
    return jnp.concatenate([one, two], axis=1)


def above(one, two):
    return jnp.concatenate([one, two], axis=0)


def split_cols(rowed):
    half = rowed.shape[0] // 2
    part = rowed.shape[1] // 2
    plus = rowed[:, :part] + rowed[:, part:]
    minus = rowed[:, :part] - rowed[:, part:]
    return beside(plus[:half], plus[half:]), beside(minus[:half], minus[half:])


def join_cols(even, odd):
    part = even.shape[1] // 2
    plus = even + odd
    minus = even - odd
    return above(
        beside(plus[:, :part], minus[:, :part]),
        beside(plus[:, part:], minus[:, part:]),
    )


def stacked(values):
    return values[0] if len(values) == 1 else jnp.concatenate(values, axis=0)


def summed_over(value, rows):
    total = value[:rows]
    for at in range(rows, value.shape[0], rows):
        total = total + value[at : at + rows]
    return total


def times(one, two):
    part = one.shape[1] // 2
    ar, ai, br, bi = one[:, :part], one[:, part:], two[:, :part], two[:, part:]
    return beside(ar * br - ai * bi, ar * bi + ai * br)


def times_conj(one, two):
    part = one.shape[1] // 2
    ar, ai, br, bi = one[:, :part], one[:, part:], two[:, :part], two[:, part:]
    return beside(ar * br + ai * bi, ai * br - ar * bi)


NAMES = ("aperture", "left", "right", "row_lag", "row_all", "even", "odd", "row_back", "row_mid", "row_lag_back")
EARLY = ("left", "right", "phase", "amp", "aperture", "obj")


def kernel(tiles, depths, planes, rows, cols, *refs):
    count = len(NAMES)
    obj_in, obs_in, phase_in, amp_in = refs[:4]
    table_in = refs[4 : 4 + count]
    out_obj, out_phase = refs[4 + count : 6 + count]
    t = dict(zip(NAMES, refs[6 + count : 6 + 2 * count]))
    (
        phase_ref, amp_ref, load_sem, left_full, right_full, even_back, odd_back, big, obs, spec_e, spec_o,
        share, part, mine, stack, full, square, sums, spots, spot_sum,
        h1s, h1r, h2s, h2r, h3s, h3r, s1, r1, s2, r2, s3, r3, s4, r4, s5, s6, r6,
    ) = refs[6 + 2 * count :]
    me = lax.axis_index("tile")
    layer = lax.axis_index("depth")
    span = rows + 2 * HALF
    half = span // 2
    slabs = tiles // RING
    slab, spot = me // RING, lax.rem(me, RING)
    lanes = depths // SIDES
    side, lane = layer // lanes, lax.rem(layer, lanes)
    lowest, highest = slab == 0, slab == slabs - 1
    near = slabs // 2
    source_slab = jnp.where(slab < near, slabs - 1, 0)

    def at_tile(tile):
        return {"tile": tile, "depth": layer}

    def at_spot(off):
        return at_tile(slab * RING + lax.rem(spot + off, RING))

    def at_slab(off):
        return at_tile(lax.rem(slab + off, slabs) * RING + spot)

    def at_lane(off):
        return {"tile": me, "depth": side * lanes + lax.rem(lane + off, lanes)}

    def across(to_slab, to_lane):
        return {"tile": to_slab * RING + spot, "depth": (SIDES - 1 - side) * lanes + to_lane}

    barrier = pltpu.get_barrier_semaphore()

    def greet(device):
        pl.semaphore_signal(barrier, 1, device_id=device, device_id_type=MESH)

    for to_lane in range(lanes):
        greet(across(source_slab, to_lane))
    greet(at_tile(lax.rem(me + 1, tiles)))
    greet(at_tile(lax.rem(me + tiles - 1, tiles)))
    for off in range(1, slabs):
        greet(at_slab(off))
    for off in range(1, lanes):
        greet(at_lane(off))
    for off in range(1, RING):
        greet(at_spot(off))
    near_sends = jnp.where(lowest | highest, near * lanes, 0)
    greeted = 2 + RING - 1 + slabs - 1 + lanes - 1 + near_sends

    loads = {"phase": pltpu.make_async_copy(phase_in, phase_ref, load_sem.at[0])}
    loads["amp"] = pltpu.make_async_copy(amp_in, amp_ref, load_sem.at[1])
    loads["obj"] = pltpu.make_async_copy(obj_in, big.at[:, pl.ds(rows, rows)], load_sem.at[2])
    loads["obs"] = pltpu.make_async_copy(obs_in, obs.at[:, pl.ds(HALF, rows)], load_sem.at[3])
    for index, name in enumerate(NAMES):
        loads[name] = pltpu.make_async_copy(table_in[index], t[name], load_sem.at[4 + index])
    for name in EARLY:
        loads[name].start()
    for name in loads:
        if name not in EARLY:
            loads[name].start()

    def ready(*names):
        for name in names:
            loads[name].wait()

    def halo(buffer, first, mine_from, theirs_to, sends, recvs, plane, direction):
        peer = lax.rem(me + (1 if direction == 0 else tiles - 1), tiles)
        slot = 2 * plane + direction
        return pltpu.make_async_remote_copy(
            buffer.at[plane, pl.ds(first + mine_from, HALF)], buffer.at[plane, pl.ds(first + theirs_to, HALF)],
            sends.at[slot], recvs.at[slot], device_id=at_tile(peer), device_id_type=MESH,
        )

    def halo1(plane, direction):
        return halo(big, rows, *((rows - HALF, -HALF) if direction == 0 else (0, rows)), h1s, h1r, plane, direction)

    def halo2(plane, direction):
        return halo(big, rows, *((0, -rows) if direction == 0 else (HALF, rows + HALF)), h2s, h2r, plane, direction)

    def halo3(plane, direction):
        return halo(obs, HALF, *((rows - HALF, -HALF) if direction == 0 else (0, rows)), h3s, h3r, plane, direction)

    def build_pupil():
        real, imag = t["left"][:PAD], t["left"][PAD:]
        left_full[...] = above(beside(real, -imag), beside(imag, real))
        real, imag = t["right"][:PUP], t["right"][PUP:]
        right_full[...] = above(beside(real, imag), beside(-imag, real))

    def spread_of(angle):
        sine, cosine = sin_cos(angle)
        weight = amp_ref[...] * t["aperture"][...]
        field = above(weight * cosine, weight * sine)
        lefts = mm(left_full[...], field)
        outer = mm(beside(lefts[:PAD], lefts[PAD:]), right_full[...])
        real, imag = outer[:, :cols], outer[:, cols:]
        intensity = real * real + imag * imag
        total = jnp.sum(intensity)
        return field, real, imag, total, intensity

    part_cols = cols // 2
    column = lax.broadcasted_iota(jnp.int32, (1, part_cols), 1)
    flip = 1.0 - 2.0 * lax.rem(column, 2).astype(jnp.float32)
    flips = beside(flip, flip)
    turn_on = beside(-flip, flip)
    turn_off = beside(flip, -flip)

    def swapped(value):
        return beside(value[:, part_cols:], value[:, :part_cols])

    def spectrum_of(intensity, total):
        even, odd = split_cols(mm(t["row_lag"][...], intensity))
        share_of = 1.0 / total
        return (
            mm(even, t["even"][...]) * (flips * share_of),
            swapped(mm(odd, t["odd"][...])) * (turn_on * share_of),
        )

    def columns(rowed):
        pairs = [split_cols(value) for value in rowed]
        return (
            mm(stacked([even for even, _ in pairs]), t["even"][...]),
            mm(stacked([odd for _, odd in pairs]), t["odd"][...]),
        )

    def back(even, odd):
        even, odd = mm(even, even_back[...]), mm(odd, odd_back[...])
        return [
            mm(t["row_back"][...], join_cols(even[at : at + half], odd[at : at + half]))
            for at in range(0, even.shape[0], half)
        ]

    def twice(value):
        return stacked([value] * GROUP)

    groups = range(0, planes, GROUP)

    def wait_group(halo_of, first):
        for plane in range(first, first + GROUP):
            halo_of(plane, 0).wait()
            halo_of(plane, 1).wait()

    ready("left", "right")
    build_pupil()
    ready("phase", "amp", "aperture")
    phase = phase_ref[...]
    field, real, imag, total, intensity = spread_of(phase)
    ready("obj")
    pl.semaphore_wait(barrier, greeted)
    for plane in range(planes):
        halo1(plane, 0).start()
        halo1(plane, 1).start()
    ready(*[name for name in loads if name not in EARLY])
    even_back[...] = t["even"][...].T
    odd_back[...] = t["odd"][...].T
    kernel_e, kernel_o = spectrum_of(intensity, total)

    cross_e = jnp.zeros((half, cols), jnp.float32)
    cross_o = jnp.zeros((half, cols), jnp.float32)
    for first in groups:
        wait_group(halo1, first)
        mates = range(first, first + GROUP)
        even, odd = columns([mm(t["row_all"][...], big[plane, pl.ds(HALF, span)]) for plane in mates])
        blurs = back(times(even, twice(kernel_e)), times(odd, twice(kernel_o)))
        misfits = [1.0 - obs[plane, pl.ds(HALF, rows)] / (blur + BACKGROUND) for plane, blur in zip(mates, blurs)]
        mis_e, mis_o = columns([mm(t["row_mid"][...], misfit) for misfit in misfits])
        cross_e = cross_e + summed_over(times_conj(mis_e, even), half)
        cross_o = cross_o + summed_over(times_conj(mis_o, odd), half)
    lagged = join_cols(mm(cross_e * flips, even_back[...]), mm(swapped(cross_o) * turn_off, odd_back[...]))
    psf_grad = mm(t["row_lag_back"][...], lagged)

    scale = 2.0 / total
    centred = (psf_grad - jnp.sum(psf_grad * intensity) / total) * scale
    rest = jnp.zeros((cols - PAD, cols), jnp.float32)
    right = right_full[...]
    lefts = mm(right, jnp.concatenate([centred * real, rest, centred * imag, rest], axis=0))
    pupils = lax.dot_general(
        beside(lefts[:PUP], lefts[PUP:]), right, (((1,), (1,)), ((), ())),
        precision=lax.Precision.HIGH, preferred_element_type=jnp.float32,
    )
    mygrad = field[:PUP] * pupils[:, PUP:] - field[PUP:] * pupils[:, :PUP]

    chunk = PUP // RING
    for piece in range(RING):
        share[piece] = mygrad[piece * chunk : (piece + 1) * chunk]

    def scatter(off):
        return pltpu.make_async_remote_copy(
            share.at[lax.rem(spot + off, RING)], part.at[off - 1], s1.at[off - 1], r1.at[off - 1],
            device_id=at_spot(off), device_id_type=MESH,
        )

    def exchange(off):
        return pltpu.make_async_remote_copy(
            mine, stack.at[slab], s2.at[off - 1], r2.at[off - 1],
            device_id=at_slab(off), device_id_type=MESH,
        )

    def gather(off):
        return pltpu.make_async_remote_copy(
            full.at[spot], full.at[spot], s3.at[off - 1], r3.at[off - 1],
            device_id=at_spot(off), device_id_type=MESH,
        )

    def lane_sum(off):
        return pltpu.make_async_remote_copy(
            square, sums.at[layer], s4.at[off - 1], r4.at[layer],
            device_id=at_lane(off), device_id_type=MESH,
        )

    def far_sum(step, to_lane):
        return pltpu.make_async_remote_copy(
            square, sums.at[layer], s5.at[step * lanes + to_lane], r4.at[layer],
            device_id=across(jnp.where(lowest, near, 0) + step, to_lane), device_id_type=MESH,
        )

    def spot_send(off):
        return pltpu.make_async_remote_copy(
            spot_sum, spots.at[spot], s6.at[off - 1], r6.at[off - 1],
            device_id=at_spot(off), device_id_type=MESH,
        )

    def windows(first):
        wait_group(halo2, first)
        for which in range(2):
            even, odd = columns(
                [mm(t["row_all"][...], big[plane, pl.ds(which * rows, span)]) for plane in range(first, first + GROUP)]
            )
            spec_e[which, pl.ds(first * half, GROUP * half)] = even
            spec_o[which, pl.ds(first * half, GROUP * half)] = odd

    for off in range(1, RING):
        scatter(off).start()
    for off in range(1, RING):
        scatter(off).wait()
    summed = share[spot]
    for off in range(1, RING):
        summed = summed + part[off - 1]
    mine[...] = summed
    for off in range(1, slabs):
        exchange(off).start()
    stack[slab] = summed
    for plane in range(planes):
        halo2(plane, 0).start()
        halo2(plane, 1).start()
    for off in range(1, slabs):
        exchange(off).wait()
    summed = stack[0]
    for other in range(1, slabs):
        summed = summed + stack[other]
    full[spot] = summed
    for off in range(1, RING):
        gather(off).start()
    square[...] = jnp.broadcast_to(jnp.sum(summed * summed), (1, 128))
    for off in range(1, lanes):
        lane_sum(off).start()

    @pl.when(lowest | highest)
    def _():
        for step in range(near):
            for to_lane in range(lanes):
                far_sum(step, to_lane).start()

    for plane in range(planes):
        halo3(plane, 0).start()
        halo3(plane, 1).start()
    sums[layer] = square[...]
    windows(0)
    for off in range(1, depths):
        other = lax.rem(layer + off, depths)
        pltpu.make_async_remote_copy(
            sums.at[other], sums.at[other], s4.at[0], r4.at[other], device_id=at_lane(1), device_id_type=MESH
        ).wait_recv()
    squares = sums[0]
    for other in range(1, depths):
        squares = squares + sums[other]
    spot_sum[...] = squares
    for off in range(1, RING):
        spot_send(off).start()
    spots[spot] = squares
    for first in groups[1:]:
        windows(first)
    for off in range(1, lanes):
        lane_sum(off).wait_send()

    @pl.when(lowest | highest)
    def _():
        for step in range(near):
            for to_lane in range(lanes):
                far_sum(step, to_lane).wait_send()

    for off in range(1, RING):
        gather(off).wait()
    gradient = jnp.concatenate([full[piece] for piece in range(RING)], axis=0)
    for first in groups:
        wait_group(halo3, first)
    for off in range(1, RING):
        spot_send(off).wait()
    squares = spots[0]
    for other in range(1, RING):
        squares = squares + spots[other]
    mean_square = squares * (1.0 / (depths * PUP * PUP))
    new_phase = phase - STEP_SIZE * gradient / jnp.sqrt(mean_square + EPSILON)
    out_phase[...] = new_phase

    _, _, _, total, intensity = spread_of(new_phase)
    kernel_e, kernel_o = spectrum_of(intensity, total)
    twice_e, twice_o = stacked([kernel_e] * planes), stacked([kernel_o] * planes)
    for first in range(0, planes, planes):
        mates = range(first, first + planes)
        at = pl.ds(first * half, planes * half)
        ratios = []
        for which in range(2):
            blurs = back(times(spec_e[which, at], twice_e), times(spec_o[which, at], twice_o))
            ratios.append(
                [obs[plane, pl.ds(which * rows, rows)] / (blur + BACKGROUND) for plane, blur in zip(mates, blurs)]
            )
        even, odd = columns([mm(t["row_all"][...], above(one, two)) for one, two in zip(*ratios)])
        corrections = back(times_conj(even, twice_e), times_conj(odd, twice_o))
        for plane, correction in zip(mates, corrections):
            out_obj[plane] = big[plane, pl.ds(rows, rows)] * correction


def write_kernel(objects, phase, objects_out, phase_out, sem):
    one = pltpu.make_async_copy(objects, objects_out, sem.at[0])
    two = pltpu.make_async_copy(phase, phase_out, sem.at[1])
    one.start()
    two.start()
    one.wait()
    two.wait()


def on_device(objects, observed, pupil_phase, pupil_amplitude):
    tiles, depths = lax.axis_size("tile"), lax.axis_size("depth")
    _, planes, rows, cols = objects.shape
    span = rows + 2 * HALF
    half = span // 2
    table = tables(rows, cols)
    f32 = jnp.float32
    vmem = pltpu.VMEM
    dma = pltpu.SemaphoreType.DMA
    chunk = PUP // RING
    slabs = tiles // RING
    lanes = depths // SIDES
    body = lambda *refs: kernel(tiles, depths, planes, rows, cols, *refs)
    new_objects, new_phase = pl.pallas_call(
        body,
        out_shape=(
            jax.ShapeDtypeStruct((planes, rows, cols), f32),
            jax.ShapeDtypeStruct((PUP, PUP), f32),
        ),
        in_specs=[pl.BlockSpec(memory_space=pltpu.HBM)] * (4 + len(NAMES)),
        out_specs=(pl.BlockSpec(memory_space=vmem), pl.BlockSpec(memory_space=vmem)),
        scratch_shapes=[vmem(table[name].shape, f32) for name in NAMES]
        + [
            vmem((PUP, PUP), f32),
            vmem((PUP, PUP), f32),
            dma((4 + len(NAMES),)),
            vmem((2 * PAD, 2 * PUP), f32),
            vmem((2 * PUP, 2 * cols), f32),
            vmem((cols, cols), f32),
            vmem((cols, cols), f32),
            vmem((planes, 3 * rows, cols), f32),
            vmem((planes, span, cols), f32),
            vmem((2, planes * half, cols), f32),
            vmem((2, planes * half, cols), f32),
            vmem((RING, chunk, PUP), f32),
            vmem((RING - 1, chunk, PUP), f32),
            vmem((chunk, PUP), f32),
            vmem((slabs, chunk, PUP), f32),
            vmem((RING, chunk, PUP), f32),
            vmem((1, 128), f32),
            vmem((depths, 1, 128), f32),
            vmem((RING, 1, 128), f32),
            vmem((1, 128), f32),
            dma((2 * planes,)), dma((2 * planes,)), dma((2 * planes,)), dma((2 * planes,)), dma((2 * planes,)), dma((2 * planes,)),
            dma((RING - 1,)), dma((RING - 1,)), dma((slabs - 1,)), dma((slabs - 1,)),
            dma((RING - 1,)), dma((RING - 1,)), dma((lanes - 1,)), dma((depths,)),
            dma((slabs // 2 * lanes,)), dma((RING - 1,)), dma((RING - 1,)),
        ],
        compiler_params=pltpu.CompilerParams(
            collective_id=0, has_side_effects=True, vmem_limit_bytes=48 * 1024 * 1024
        ),
        name="step",
    )(*[
        pltpu.with_memory_space_constraint(value, pltpu.HBM)
        for value in (objects[0], observed[0], pupil_phase[0], pupil_amplitude[0], *[table[name] for name in NAMES])
    ])
    new_objects, new_phase = pl.pallas_call(
        write_kernel,
        out_shape=(
            jax.ShapeDtypeStruct((planes, rows, cols), f32),
            jax.ShapeDtypeStruct((PUP, PUP), f32),
        ),
        in_specs=[pl.BlockSpec(memory_space=pl.ANY)] * 2,
        out_specs=(pl.BlockSpec(memory_space=pltpu.HBM), pl.BlockSpec(memory_space=pltpu.HBM)),
        scratch_shapes=[dma((2,))],
        name="write",
    )(*[pltpu.with_memory_space_constraint(value, vmem) for value in (new_objects, new_phase)])
    return new_objects[None], new_phase[None]


def solution(mesh):
    return jax.shard_map(
        on_device,
        mesh=mesh,
        in_specs=(
            P("depth", None, "tile", None),
            P("depth", None, "tile", None),
            P("depth", None, None),
            P("depth", None, None),
        ),
        out_specs=(P("depth", None, "tile", None), P("depth", None, None)),
        check_vma=False,
    )
```
